256 devices in a mesh: seq: 64 (over z, y, core), head: 4 (over x).
Axes of the slice: x: 4, y: 4, z: 8, core: 2. Of those that a mesh axis runs over, the one named last changes fastest.
Arguments:
- hidden_in: bfloat16 [16384, 2304], P(('seq', 'head')), may hold values from -6 to 6
- qkv_weight: bfloat16 [2304, 3, 2048], P(None, None, 'head'), may hold values from -0.125 to 0.125
- conv_weight: bfloat16 [3, 4, 2048], P(None, None, 'head'), may hold values from -3 to 3
- decay_log: float32 [16], P('head'), may hold values from -9 to -3
- dt_bias: float32 [2048], P('head'), may hold values from -3 to 3
- decay_down: bfloat16 [2304, 128], replicated, may hold values from -0.125 to 0.125
- decay_up: bfloat16 [128, 2048], P(None, 'head'), may hold values from -0.5 to 0.5
- beta_weight: bfloat16 [2304, 16], P(None, 'head'), may hold values from -0.125 to 0.125
- gate_down: bfloat16 [2304, 128], replicated, may hold values from -0.125 to 0.125
- gate_up: bfloat16 [128, 2048], P(None, 'head'), may hold values from -0.5 to 0.5
- norm_gain: float32 [128], replicated, may hold values from 0.1 to 1.9
- out_weight: bfloat16 [2048, 2304], P('head'), may hold values from -0.125 to 0.125
Outputs:
- layer_out: bfloat16 [16384, 2304], P(('seq', 'head'))
The draws below stay inside these ranges and needn't reach their ends.
All inputs are finite; a program needn't handle non-finite values.
Results may differ from the reference program's by a relative error of at most 0.015.
Values may be sent and summed in bfloat16 or wider, within the bound.
A program may use at most 128 MiB of HBM per device.

```python
import jax
import jax.numpy as jnp
from jax import lax

D = 2304
H = 16
DK = 128
RANK = 128
KERNEL = 4
TOKENS = 16384


def level_of(key, extent, shards, smallest, high):
    loudness, own = 1.0, jax.random.fold_in(key, 6)
    for position, parts in shards:
        heights = jnp.exp(jax.random.uniform(jax.random.fold_in(own, position), (parts,), jnp.float32, smallest / len(shards), high / len(shards)))
        loudness = loudness * jnp.repeat(heights, extent[position] // parts).reshape([-1 if axis == position else 1 for axis in range(len(extent))])
    return loudness


def noise(own_key, extent, scale, limit, cuts=(), dtype=jnp.bfloat16):
    array = jax.random.normal(own_key, extent, jnp.float32) * scale
    if len(cuts) > 0:
        array = level_of(own_key, extent, cuts, -0.22, 0.18) * array
    return jnp.clip(array, min=-limit, max=limit).astype(dtype)


def setup_inputs(seed: int = 0) -> dict:
    key_of = jax.random.split(jax.random.key(seed), 13)
    return {
        "hidden_in": noise(key_of[0], (TOKENS, D), 1.0, 6.0, ((0, 256),)),
        "qkv_weight": noise(key_of[1], (D, 3, H * DK), D ** -0.5, 0.125, ((2, 4),)),
        "conv_weight": noise(key_of[2], (3, KERNEL, H * DK), 0.5, 3.0, ((2, 4),)),
        "decay_log": jnp.clip(-9.0 + 6.0 * jax.random.uniform(key_of[3], (H,), jnp.float32) ** level_of(key_of[3], (H,), ((0, 4),), -0.2, 0.2), -9.0, -3.0),
        "dt_bias": noise(key_of[4], (H * DK,), 1.0, 3.0, ((0, 4),), jnp.float32),
        "decay_down": noise(key_of[5], (D, RANK), D ** -0.5, 0.125),
        "decay_up": noise(key_of[6], (RANK, H * DK), RANK ** -0.5, 0.5, ((1, 4),)),
        "beta_weight": noise(key_of[7], (D, H), D ** -0.5, 0.125, ((1, 4),)),
        "gate_down": noise(key_of[8], (D, RANK), D ** -0.5, 0.125),
        "gate_up": noise(key_of[9], (RANK, H * DK), RANK ** -0.5, 0.5, ((1, 4),)),
        "norm_gain": jnp.clip(1.0 + 0.18 * jax.random.normal(key_of[10], (DK,), jnp.float32), 0.1, 1.9),
        "out_weight": noise(key_of[11], (H * DK, D), (H * DK) ** -0.5, 0.125, ((0, 4),)),
    }


def l2_normalize(values):
    return values * lax.rsqrt(lax.optimization_barrier(jnp.sum(values * values, axis=-1, keepdims=True)) + 1e-06)

def reference(hidden_in, qkv_weight, conv_weight, decay_log, dt_bias, decay_down, decay_up, beta_weight, gate_down, gate_up, norm_gain, out_weight):
    token_count = hidden_in.shape[0]
    full_width = H * DK
    projected = jnp.dot(hidden_in, qkv_weight.reshape(D, 3 * full_width), preferred_element_type=jnp.float32).astype(jnp.bfloat16)
    projected = projected.reshape(token_count, 3, full_width)
    padded = jnp.concatenate([jnp.zeros((KERNEL - 1, 3, full_width), jnp.bfloat16), projected], axis=0).astype(jnp.float32)
    taps = conv_weight.astype(jnp.float32)
    convolved = jnp.zeros((token_count, 3, full_width), jnp.float32)
    for tap_index in range(KERNEL):
        convolved = convolved + padded[tap_index:tap_index + token_count] * taps[:, tap_index][None]
    convolved = jax.nn.silu(convolved).astype(jnp.bfloat16)
    decay_low = jnp.dot(hidden_in, decay_down, preferred_element_type=jnp.float32).astype(jnp.bfloat16)
    raw_decay = jnp.dot(decay_low, decay_up, preferred_element_type=jnp.float32) + dt_bias
    log_decay = -jnp.exp(decay_log)[None, :, None] * jax.nn.softplus(raw_decay).reshape(token_count, H, DK)
    strength = jax.nn.sigmoid(jnp.dot(hidden_in, beta_weight, preferred_element_type=jnp.float32))
    queries = l2_normalize(convolved[:, 0].astype(jnp.float32).reshape(token_count, H, DK)) * DK ** (-0.5)
    keys = l2_normalize(convolved[:, 1].astype(jnp.float32).reshape(token_count, H, DK))
    values = convolved[:, 2].astype(jnp.float32).reshape(token_count, H, DK)
    fading = jnp.exp(log_decay)

    def advance(memory_state, inputs):
        current_query_vector, current_key_vector, value_row, fade_row, strength_row = inputs
        memory_state = memory_state * fade_row[:, :, None]
        retrieved_value = jnp.einsum('ci,ciu->cu', current_key_vector, memory_state, precision=lax.Precision.HIGHEST)
        memory_state = memory_state + strength_row[:, None, None] * current_key_vector[:, :, None] * (value_row - retrieved_value)[:, None, :]
        return (memory_state, jnp.einsum('ci,ciu->cu', current_query_vector, memory_state, precision=lax.Precision.HIGHEST))
    initial = jnp.zeros((H, DK, DK), jnp.float32)
    _, attended = lax.scan(advance, initial, (queries, keys, values, fading, strength))
    gate_low = jnp.dot(hidden_in, gate_down, preferred_element_type=jnp.float32).astype(jnp.bfloat16)
    out_gate = jax.nn.sigmoid(jnp.dot(gate_low, gate_up, preferred_element_type=jnp.float32)).reshape(token_count, H, DK)
    inverse_rms = lax.rsqrt(lax.optimization_barrier(jnp.mean(attended * attended, axis=-1, keepdims=True)) + 1e-05)
    normed = (attended * inverse_rms * norm_gain * out_gate).astype(jnp.bfloat16).reshape(token_count, full_width)
    return jnp.dot(normed, out_weight, preferred_element_type=jnp.float32).astype(jnp.bfloat16)
```

```python
import functools

import jax
import jax.numpy as jnp
import numpy as np
from jax import lax
from jax.experimental import pallas as pl
from jax.experimental.pallas import tpu as pltpu
from jax.sharding import PartitionSpec as P

F32 = jnp.float32
BF16 = jnp.bfloat16
MESH = pl.DeviceIdType.MESH

HALO = 16
EDGE = 8
HALF = 128
LEVELS = (1, 2, 4, 8, 16, 32, 64)
PLANE = 8


def span_matrix():
    r, i = np.arange(HALF)[:, None], np.arange(HALF)[None, :]
    rows = []
    for size in LEVELS:
        middle = (r // (2 * size)) * 2 * size + size - 1
        late = (r % (2 * size)) >= size
        rows.append(np.where(late, (i > middle) & (i <= r), (i > r) & (i <= middle)))
    rows.append(i <= r)
    rows.append(i > r)
    spans = np.concatenate(rows, axis=0)
    return np.concatenate([spans, spans], axis=1).astype(np.float32)


def mm(a, b, dims=((1,), (0,))):
    return lax.dot_general(
        a.astype(BF16), b.astype(BF16), (dims, ((), ())), preferred_element_type=F32
    )


def sigmoid(v):
    return 1.0 / (1.0 + jnp.exp(-v))


def gather_kernel(seq_size, x_ref, out_ref, zero_ref, send_sem, recv_sem, edge_sem, local_sem):
    s = lax.axis_index("seq")
    h = lax.axis_index("head")
    right, left = lax.rem(h + 1, 4), lax.rem(h + 3, 4)
    rows = x_ref.shape[0]
    half = rows // 2
    has_next = s < seq_size - 1
    sends_edge = jnp.logical_and(h == 3, has_next)

    barrier = pltpu.get_barrier_semaphore()
    pl.semaphore_signal(barrier, 1, device_id={"head": right}, device_id_type=MESH)
    pl.semaphore_signal(barrier, 1, device_id={"head": left}, device_id_type=MESH)

    @pl.when(s > 0)
    def _():
        pl.semaphore_signal(
            barrier, 1, device_id={"seq": s - 1, "head": 3}, device_id_type=MESH
        )

    zero_ref[...] = jnp.zeros_like(zero_ref)
    own = pltpu.make_async_copy(
        x_ref, out_ref.at[pl.ds(pl.multiple_of(HALO + h * rows, 16), rows)], local_sem.at[0]
    )
    own.start()
    blank = pltpu.make_async_copy(zero_ref.at[pl.ds(0, EDGE)], out_ref.at[pl.ds(0, EDGE)], local_sem.at[1])
    blank.start()
    blank_edge = pltpu.make_async_copy(
        zero_ref.at[pl.ds(EDGE, EDGE)], out_ref.at[pl.ds(EDGE, EDGE)], local_sem.at[2]
    )

    @pl.when(s == 0)
    def _():
        blank_edge.start()

    @pl.when(sends_edge)
    def _():
        pl.semaphore_wait(barrier, 6)

    @pl.when(jnp.logical_not(sends_edge))
    def _():
        pl.semaphore_wait(barrier, 2)

    def place(owner, part):
        return out_ref.at[pl.ds(pl.multiple_of(HALO + owner * rows + part * half, 16), half)]

    def piece(src, owner, part, target, k):
        return pltpu.make_async_remote_copy(
            src_ref=src,
            dst_ref=place(owner, part),
            send_sem=send_sem.at[k],
            recv_sem=recv_sem.at[k],
            device_id={"head": target},
            device_id_type=MESH,
        )

    mine = [x_ref.at[pl.ds(0, half)], x_ref.at[pl.ds(half, half)]]
    to_right = [piece(mine[0], h, 0, right, 0), piece(mine[1], h, 1, right, 1)]
    to_left = [piece(mine[1], h, 1, left, 2), piece(mine[0], h, 0, left, 3)]
    to_right[0].start()
    to_left[0].start()
    to_right[1].start()
    to_left[1].start()

    def edge(target):
        return pltpu.make_async_remote_copy(
            src_ref=x_ref.at[pl.ds(rows - EDGE, EDGE)],
            dst_ref=out_ref.at[pl.ds(EDGE, EDGE)],
            send_sem=edge_sem.at[target],
            recv_sem=edge_sem.at[4],
            device_id={"seq": s + 1, "head": target},
            device_id_type=MESH,
        )

    @pl.when(sends_edge)
    def _():
        for target in range(4):
            edge(target).start()

    far = lax.rem(h + 2, 4)
    pass_right = piece(place(left, 0), left, 0, right, 4)
    pass_left = piece(place(right, 1), right, 1, left, 5)
    piece(mine[0], left, 0, right, 0).wait_recv()
    pass_right.start()
    piece(mine[1], right, 1, left, 2).wait_recv()
    pass_left.start()
    piece(mine[1], left, 1, right, 1).wait_recv()
    piece(mine[0], right, 0, left, 3).wait_recv()
    piece(mine[0], far, 0, right, 4).wait_recv()
    piece(mine[1], far, 1, left, 5).wait_recv()

    @pl.when(s > 0)
    def _():
        edge(0).wait_recv()

    @pl.when(s == 0)
    def _():
        blank_edge.wait()

    for copy in (*to_right, *to_left, pass_right, pass_left):
        copy.wait_send()

    @pl.when(sends_edge)
    def _():
        for target in range(4):
            edge(target).wait_send()

    own.wait()
    blank.wait()


def gather(seq_size, x):
    rows, width = x.shape
    return pl.pallas_call(
        functools.partial(gather_kernel, seq_size),
        name="gather",
        out_shape=jax.ShapeDtypeStruct((HALO + 4 * rows, width), x.dtype),
        in_specs=[pl.BlockSpec(memory_space=pl.ANY)],
        out_specs=pl.BlockSpec(memory_space=pl.ANY),
        scratch_shapes=[
            pltpu.VMEM((HALO, width), x.dtype),
            pltpu.SemaphoreType.DMA((6,)),
            pltpu.SemaphoreType.DMA((6,)),
            pltpu.SemaphoreType.DMA((5,)),
            pltpu.SemaphoreType.DMA((3,)),
        ],
        compiler_params=pltpu.CompilerParams(collective_id=0, has_side_effects=True),
    )(x)


def block_kernel(
    xg_ref, w_ref, down_ref, gdown_ref, beta_ref, up_ref, gup_ref, conv_ref, dlog_ref, bias_ref,
    span_ref, o_ref, r_ref, gate_ref, z_ref, proj_ref, q_ref, k_ref, v_ref, e_ref,
):
    count = xg_ref.shape[0] - HALO
    width = w_ref.shape[2]
    heads = width // 128
    x = xg_ref[HALO:, :]

    low = jnp.dot(x, down_ref[...], preferred_element_type=F32).astype(BF16)
    raw = jnp.dot(low, up_ref[...], preferred_element_type=F32) + bias_ref[...]
    soft = jnp.maximum(raw, 0.0) + jnp.log1p(jnp.exp(-jnp.abs(raw)))
    rate = jnp.concatenate(
        [jnp.exp(jnp.full((1, 128), dlog_ref[i], F32)) for i in range(heads)], axis=1
    )
    log_decay = -rate * soft
    for c in range(2):
        part = log_decay[c * HALF : (c + 1) * HALF]
        top = part.astype(BF16)
        rest = (part - top.astype(F32)).astype(BF16)
        e_ref[c] = jnp.exp(
            jnp.dot(
                span_ref[...], jnp.concatenate([top, rest], axis=0), preferred_element_type=F32
            )
        )
    gate_low = jnp.dot(x, gdown_ref[...], preferred_element_type=F32).astype(BF16)
    gate_ref[...] = sigmoid(jnp.dot(gate_low, gup_ref[...], preferred_element_type=F32))
    beta = sigmoid(
        lax.dot_general(
            x, beta_ref[...], (((1,), (1,)), ((), ())), preferred_element_type=F32
        )
    )

    for c, target in enumerate((q_ref, k_ref, v_ref)):
        proj_ref[...] = (
            jnp.dot(xg_ref[...], w_ref[c], preferred_element_type=F32).astype(BF16).astype(F32)
        )
        taps = conv_ref[c].astype(F32)
        total = proj_ref[pl.ds(HALO - 3, count), :] * taps[0:1]
        for i in range(1, 4):
            total = total + proj_ref[pl.ds(HALO - 3 + i, count), :] * taps[i : i + 1]
        total = (total * sigmoid(total)).astype(BF16).astype(F32)
        if c == 2:
            target[...] = total
            continue
        for i in range(heads):
            lanes = slice(i * 128, (i + 1) * 128)
            u = total[:, lanes]
            scale = lax.rsqrt(jnp.sum(u * u, axis=1, keepdims=True) + 1e-06)
            if c == 0:
                scale = scale * (128**-0.5)
            target[:, lanes] = u * scale

    t = lax.broadcasted_iota(jnp.int32, (HALF, HALF), 0)
    j = lax.broadcasted_iota(jnp.int32, (HALF, HALF), 1)
    row = lax.broadcasted_iota(jnp.int32, (HALF, 128), 0)
    masks = [
        ((t ^ j) >= size) & ((t ^ j) < 2 * size) & (t > j) for size in LEVELS
    ]
    diagonal = t == j

    pairs = [(i, c) for i in range(heads) for c in range(2)]
    lanes_of = [slice(i * 128, (i + 1) * 128) for i in range(heads)]
    rows_of = [slice(c * HALF, (c + 1) * HALF) for c in range(2)]
    strength = {
        (i, c): jnp.broadcast_to(beta[rows_of[c], i : i + 1], (HALF, 128)) for i, c in pairs
    }
    attend, inverse = {}, {}
    for i, c in pairs:
        kc, qc = k_ref[rows_of[c], lanes_of[i]], q_ref[rows_of[c], lanes_of[i]]
        own = jnp.sum(qc * kc, axis=1, keepdims=True) * strength[i, c]
        attend[i, c] = jnp.where(diagonal, own, 0.0)
        inverse[i, c] = jnp.where(diagonal, 1.0, 0.0)
    for n, size in enumerate(LEVELS):
        for i, c in pairs:
            kc, qc = k_ref[rows_of[c], lanes_of[i]], q_ref[rows_of[c], lanes_of[i]]
            fade = e_ref[c, n * HALF : (n + 1) * HALF, lanes_of[i]]
            late = (row & size) != 0
            kx = (kc * fade * jnp.where(late, 1.0, strength[i, c])).astype(BF16)
            qx = (qc * fade).astype(BF16)
            both = mm(jnp.concatenate([kx, qx], axis=0), kx, ((1,), (1,)))
            mixing = jnp.where(masks[n], both[:HALF], 0.0)
            attend[i, c] = jnp.where(masks[n], both[HALF:], attend[i, c])
            if size == 1:
                inverse[i, c] = inverse[i, c] - mixing
            else:
                own = inverse[i, c].astype(BF16)
                inverse[i, c] = inverse[i, c] - mm(mm(own, mixing), own)

    n = len(LEVELS)
    for i in range(heads):
        lanes = lanes_of[i]
        rise = [e_ref[c, n * HALF : (n + 1) * HALF, lanes] for c in range(2)]
        fall = [e_ref[c, (n + 1) * HALF : (n + 2) * HALF, lanes] for c in range(2)]
        whole = [part[HALF - 1 : HALF] for part in rise]
        k = [k_ref[rows_of[c], lanes] for c in range(2)]
        q = [q_ref[rows_of[c], lanes] for c in range(2)]
        k_rise = [k[c] * rise[c] for c in range(2)]
        q_rise = [q[c] * rise[c] for c in range(2)]
        k_fall = [k[c] * fall[c] * strength[i, c] for c in range(2)]
        cross = mm(jnp.concatenate([k_rise[1], q_rise[1]], axis=0), k_fall[0], ((1,), (1,)))
        first = mm(
            inverse[i, 0], jnp.concatenate([v_ref[rows_of[0], lanes], k_rise[0]], axis=1)
        ).astype(BF16)
        second = jnp.concatenate([v_ref[rows_of[1], lanes], k_rise[1] * whole[0]], axis=1)
        second = mm(inverse[i, 1], second - mm(cross[:HALF], first)).astype(BF16)
        out = [mm(attend[i, 0], first), mm(cross[HALF:], first) + mm(attend[i, 1], second)]
        for c in range(2):
            o_ref[rows_of[c], lanes] = out[c][:, :128]
        r_ref[rows_of[0], lanes] = (q_rise[0] - out[0][:, 128:]).astype(BF16)
        r_ref[rows_of[1], lanes] = (q_rise[1] * whole[0] - out[1][:, 128:]).astype(BF16)
        stop = jnp.concatenate([k_fall[0] * whole[1], k_fall[1]], axis=0).astype(BF16)
        z = mm(jnp.concatenate([first, second], axis=0), stop, ((0,), (0,)))
        move = jnp.where(diagonal, whole[0] * whole[1], 0.0) - z[128:]
        z_ref[i, 0:64] = z[0:64].astype(BF16)
        z_ref[i, 64:192] = move.astype(BF16)
        z_ref[i, 192:256] = z[64:128].astype(BF16)


def block(xg, w, down, gdown, beta, up, gup, conv, dlog, bias, span):
    count = xg.shape[0] - HALO
    width = w.shape[2]
    heads = width // 128
    vmem = pl.BlockSpec(memory_space=pltpu.VMEM)
    smem = pl.BlockSpec(memory_space=pltpu.SMEM)
    return pl.pallas_call(
        block_kernel,
        name="block",
        out_shape=(
            jax.ShapeDtypeStruct((count, width), F32),
            jax.ShapeDtypeStruct((count, width), BF16),
            jax.ShapeDtypeStruct((count, width), F32),
            jax.ShapeDtypeStruct((heads, 256, 128), BF16),
        ),
        in_specs=[vmem] * 8 + [smem] + [vmem] * 2,
        out_specs=(vmem,) * 4,
        scratch_shapes=[
            pltpu.VMEM((HALO + count, width), F32),
            pltpu.VMEM((count, width), F32),
            pltpu.VMEM((count, width), F32),
            pltpu.VMEM((count, width), F32),
            pltpu.VMEM((2, (len(LEVELS) + 2) * HALF, width), F32),
        ],
        compiler_params=pltpu.CompilerParams(vmem_limit_bytes=56 << 20),
    )(xg, w, down, gdown, beta, up, gup, conv, dlog, bias, span)


def finish_kernel(
    depth, z_ref, o_ref, r_ref, gate_ref, gain_ref, w_ref, out_ref,
    zin, pre, total, zall, held, lead, state, normed, part, sums, inbox,
    a_send, a_recv, b_send, b_recv, c_send, c_recv, d_send, d_recv,
):
    s = lax.axis_index("seq")
    h = lax.axis_index("head")
    z = lax.div(s, PLANE)
    p = lax.rem(s, PLANE)
    y, core = lax.div(p, 2), lax.rem(p, 2)
    base = z * PLANE
    right, left = lax.rem(h + 1, 4), lax.rem(h + 3, 4)
    map_at = pl.multiple_of(64 * (1 - core), 64)
    shift_at = pl.multiple_of(128 * core, 128)

    barrier = pltpu.get_barrier_semaphore()
    for d in range(1, PLANE):
        pl.semaphore_signal(
            barrier, 1, device_id={"seq": base + lax.rem(p + d, PLANE)}, device_id_type=MESH
        )
    pl.semaphore_signal(barrier, 1, device_id={"head": right}, device_id_type=MESH)
    pl.semaphore_signal(barrier, 1, device_id={"head": left}, device_id_type=MESH)

    def greet(k, _):
        pl.semaphore_signal(barrier, 1, device_id={"seq": k * PLANE + p}, device_id_type=MESH)
        return 0

    lax.fori_loop(0, z, greet, 0)
    pl.semaphore_wait(barrier, PLANE - 1 + 2 + (depth - 1 - z))

    def to_owner(d):
        q = lax.rem(p + d, PLANE)
        here = pl.ds(pl.multiple_of(64 * lax.rem(q, 2), 64), 192)
        return pltpu.make_async_remote_copy(
            src_ref=z_ref.at[lax.div(q, 2), here],
            dst_ref=zin.at[p],
            send_sem=a_send.at[d],
            recv_sem=a_recv.at[p],
            device_id={"seq": base + q},
            device_id_type=MESH,
        )

    for d in range(1, PLANE):
        to_owner(d).start()
    zin[p] = z_ref[y, pl.ds(pl.multiple_of(64 * core, 64), 192), :]

    def arrived(k):
        @pl.when(p != k)
        def _():
            pltpu.make_async_remote_copy(
                src_ref=zin.at[k],
                dst_ref=zin.at[k],
                send_sem=a_send.at[0],
                recv_sem=a_recv.at[k],
                device_id={"seq": s},
                device_id_type=MESH,
            ).wait_recv()

    eye = lax.broadcasted_iota(jnp.int32, (128, 128), 0) == lax.broadcasted_iota(
        jnp.int32, (128, 128), 1
    )
    pre[0, 0:128] = jnp.where(eye, 1.0, 0.0).astype(BF16)
    pre[0, 128:192] = jnp.zeros((64, 128), BF16)
    arrived(0)
    move = zin[0, pl.ds(map_at, 128), :]
    shift = zin[0, pl.ds(shift_at, 64), :]
    so_far = jnp.concatenate([move, shift], axis=0)
    pre[1] = so_far
    for k in range(1, PLANE):
        arrived(k)
        move = zin[k, pl.ds(map_at, 128), :]
        shift = zin[k, pl.ds(shift_at, 64), :].astype(F32)
        nxt = mm(so_far, move)
        so_far = jnp.concatenate(
            [nxt[:128].astype(BF16), (nxt[128:] + shift).astype(BF16)], axis=0
        )
        if k < PLANE - 1:
            pre[k + 1] = so_far
        else:
            total[...] = so_far

    def to_later(k):
        return pltpu.make_async_remote_copy(
            src_ref=total,
            dst_ref=zall.at[z],
            send_sem=b_send.at[k],
            recv_sem=b_recv.at[z],
            device_id={"seq": k * PLANE + p},
            device_id_type=MESH,
        )

    def send_later(k, _):
        to_later(k).start()
        return 0

    lax.fori_loop(z + 1, depth, send_later, 0)

    held[...] = jnp.zeros_like(held)

    def from_earlier(k, _):
        pltpu.make_async_remote_copy(
            src_ref=total,
            dst_ref=zall.at[k],
            send_sem=b_send.at[k],
            recv_sem=b_recv.at[k],
            device_id={"seq": s},
            device_id_type=MESH,
        ).wait_recv()
        held[...] = (mm(held[...], zall[k, 0:128]) + zall[k, 128:192].astype(F32)).astype(BF16)
        return 0

    lax.fori_loop(0, z, from_earlier, 0)
    carry = held[...]

    mine = pl.ds(pl.multiple_of(64 * core, 64), 64)

    def to_block(d):
        q = lax.rem(p + d, PLANE)
        return pltpu.make_async_remote_copy(
            src_ref=lead.at[d],
            dst_ref=state.at[y, mine],
            send_sem=c_send.at[d],
            recv_sem=c_recv.at[p],
            device_id={"seq": base + q},
            device_id_type=MESH,
        )

    for d in range(1, PLANE):
        q = lax.rem(p + d, PLANE)
        lead[d] = (mm(carry, pre[q, 0:128]) + pre[q, 128:192].astype(F32)).astype(BF16)
        to_block(d).start()
    state[y, mine, :] = (mm(carry, pre[p, 0:128]) + pre[p, 128:192].astype(F32)).astype(BF16)
    for k in range(PLANE):

        @pl.when(p != k)
        def _():
            pltpu.make_async_remote_copy(
                src_ref=lead.at[0],
                dst_ref=state.at[k // 2, pl.ds(64 * (k % 2), 64)],
                send_sem=c_send.at[0],
                recv_sem=c_recv.at[k],
                device_id={"seq": s},
                device_id_type=MESH,
            ).wait_recv()

    heads = z_ref.shape[0]
    for i in range(heads):
        lanes = slice(i * 128, (i + 1) * 128)
        attended = o_ref[:, lanes] + mm(r_ref[:, lanes], state[i], ((1,), (1,)))
        scale = lax.rsqrt(jnp.mean(attended * attended, axis=1, keepdims=True) + 1e-05)
        normed[:, lanes] = (attended * scale * gain_ref[...] * gate_ref[:, lanes]).astype(BF16)

    rows = out_ref.shape[0]
    half = rows // 2
    far = lax.rem(h + 2, 4)

    def partial(owner):
        at = pl.ds(pl.multiple_of(owner * rows, 16), rows)
        return jnp.dot(normed[at, :], w_ref[...], preferred_element_type=F32)

    def piece(k, src, dst, target):
        return pltpu.make_async_remote_copy(
            src_ref=src,
            dst_ref=dst,
            send_sem=d_send.at[k],
            recv_sem=d_recv.at[k],
            device_id={"head": target},
            device_id_type=MESH,
        )

    top, low = pl.ds(0, half), pl.ds(half, half)
    part[0] = partial(far).astype(BF16)
    far_right = piece(0, part.at[0, top], inbox.at[0, top], right)
    far_left = piece(1, part.at[0, low], inbox.at[0, low], left)
    far_right.start()
    far_left.start()
    sums[0] = partial(right)
    part[1, low] = sums[0, low].astype(BF16)
    right_low = piece(2, part.at[1, low], inbox.at[1, low], right)
    right_low.start()
    sums[1] = partial(left)
    part[2, top] = sums[1, top].astype(BF16)
    left_top = piece(3, part.at[2, top], inbox.at[2, top], left)
    left_top.start()
    far_right.wait_recv()
    part[1, top] = (sums[0, top] + inbox[0, top].astype(F32)).astype(BF16)
    right_top = piece(4, part.at[1, top], inbox.at[1, top], right)
    right_top.start()
    far_left.wait_recv()
    part[2, low] = (sums[1, low] + inbox[0, low].astype(F32)).astype(BF16)
    left_low = piece(5, part.at[2, low], inbox.at[2, low], left)
    left_low.start()
    own = partial(h)
    right_low.wait_recv()
    left_top.wait_recv()
    right_top.wait_recv()
    left_low.wait_recv()
    out_ref[...] = (own + inbox[1].astype(F32) + inbox[2].astype(F32)).astype(BF16)

    for copy in (far_right, far_left, right_low, left_top, right_top, left_low):
        copy.wait_send()
    for d in range(1, PLANE):
        to_owner(d).wait_send()
        to_block(d).wait_send()

    def sent(k, _):
        to_later(k).wait_send()
        return 0

    lax.fori_loop(z + 1, depth, sent, 0)


def finish(depth, z, o, r, gate, gain, w):
    vmem = pl.BlockSpec(memory_space=pltpu.VMEM)
    rows, width = o.shape[0] // 4, w.shape[1]
    dma = pltpu.SemaphoreType.DMA
    return pl.pallas_call(
        functools.partial(finish_kernel, depth),
        name="finish",
        out_shape=jax.ShapeDtypeStruct((rows, width), BF16),
        in_specs=[vmem] * 6,
        out_specs=vmem,
        scratch_shapes=[
            pltpu.VMEM((PLANE, 192, 128), BF16),
            pltpu.VMEM((PLANE, 192, 128), BF16),
            pltpu.VMEM((192, 128), BF16),
            pltpu.VMEM((depth, 192, 128), BF16),
            pltpu.VMEM((64, 128), BF16),
            pltpu.VMEM((PLANE, 64, 128), BF16),
            pltpu.VMEM((4, 128, 128), BF16),
            pltpu.VMEM(o.shape, BF16),
            pltpu.VMEM((3, rows, width), BF16),
            pltpu.VMEM((2, rows, width), F32),
            pltpu.VMEM((3, rows, width), BF16),
            dma((PLANE,)), dma((PLANE,)), dma((depth,)), dma((depth,)),
            dma((PLANE,)), dma((PLANE,)), dma((6,)), dma((6,)),
        ],
        compiler_params=pltpu.CompilerParams(
            collective_id=1, has_side_effects=True, vmem_limit_bytes=56 << 20
        ),
    )(z, o, r, gate, gain, w)


def solution(mesh):
    seq_size = mesh.shape["seq"]
    span = span_matrix()

    def shards(
        hidden_in, qkv_weight, conv_weight, decay_log, dt_bias, decay_down, decay_up,
        beta_weight, gate_down, gate_up, norm_gain, out_weight,
    ):
        xg = gather(seq_size, hidden_in)
        o, r, gate, z = block(
            xg,
            jnp.transpose(qkv_weight, (1, 0, 2)),
            decay_down,
            gate_down,
            beta_weight.T,
            decay_up,
            gate_up,
            conv_weight,
            decay_log,
            dt_bias.reshape(1, -1),
            jnp.asarray(span, BF16),
        )
        return finish(
            seq_size // PLANE, z, o, r, gate, norm_gain.reshape(1, -1), out_weight
        )

    rows = P(("seq", "head"), None)
    return jax.shard_map(
        shards,
        mesh=mesh,
        in_specs=(
            rows, P(None, None, "head"), P(None, None, "head"), P("head"), P("head"), P(),
            P(None, "head"), P(None, "head"), P(), P(None, "head"), P(), P("head", None),
        ),
        out_specs=rows,
        check_vma=False,
    )
```

```python
import functools

import jax
import jax.numpy as jnp
import numpy as np
from jax import lax
from jax.experimental import pallas as pl
from jax.experimental.pallas import tpu as pltpu
from jax.sharding import PartitionSpec as P

F32 = jnp.float32
BF16 = jnp.bfloat16
MESH = pl.DeviceIdType.MESH

HALO = 16
EDGE = 8
HALF = 128
LEVELS = (1, 2, 4, 8, 16, 32, 64)
PLANE = 8


def span_matrix():
    r, i = np.arange(HALF)[:, None], np.arange(HALF)[None, :]
    rows = []
    for size in LEVELS:
        middle = (r // (2 * size)) * 2 * size + size - 1
        late = (r % (2 * size)) >= size
        rows.append(np.where(late, (i > middle) & (i <= r), (i > r) & (i <= middle)))
    rows.append(i <= r)
    rows.append(i > r)
    spans = np.concatenate(rows, axis=0)
    return np.concatenate([spans, spans], axis=1).astype(np.float32)


def mm(a, b, dims=((1,), (0,))):
    return lax.dot_general(
        a.astype(BF16), b.astype(BF16), (dims, ((), ())), preferred_element_type=F32
    )


def sigmoid(v):
    return 1.0 / (1.0 + jnp.exp(-v))


def kernel(
    depth, x_hbm, w_hbm, down_hbm, gdown_hbm, beta_hbm, up_ref, gup_ref, conv_ref, dlog_ref,
    bias_ref, span_hbm, gain_ref, ow_hbm, out_ref,
    x_ref, w_ref, dg_ref, beta_ref, span_ref, ow_ref,
    proj_ref, low_ref, strength_ref, q_ref, k_ref, v_ref, e_ref, o_ref, r_ref, gate_ref, z_ref,
    zin, pre, total, zall, held, lead, state, normed, part, sums, inbox,
    l_sem, x_send, x_recv, e_sem,
    a_send, a_recv, b_send, b_recv, c_send, c_recv, d_send, d_recv,
):
    s = lax.axis_index("seq")
    h = lax.axis_index("head")
    z = lax.div(s, PLANE)
    p = lax.rem(s, PLANE)
    y, core = lax.div(p, 2), lax.rem(p, 2)
    base = z * PLANE
    right, left, far = lax.rem(h + 1, 4), lax.rem(h + 3, 4), lax.rem(h + 2, 4)
    owner = core == 0
    sends_edge = jnp.logical_and(h == 3, s < depth * PLANE - 1)
    rows = x_hbm.shape[0]
    half = rows // 2
    count = 4 * rows
    width = w_ref.shape[2]
    heads = width // 128

    barrier = pltpu.get_barrier_semaphore()
    pl.semaphore_signal(barrier, 1, device_id={"head": right}, device_id_type=MESH)
    pl.semaphore_signal(barrier, 1, device_id={"head": left}, device_id_type=MESH)

    @pl.when(s > 0)
    def _():
        pl.semaphore_signal(
            barrier, 1, device_id={"seq": s - 1, "head": 3}, device_id_type=MESH
        )

    for d in range(1, PLANE):
        pl.semaphore_signal(
            barrier, 1, device_id={"seq": base + lax.rem(p + d, PLANE)}, device_id_type=MESH
        )

    def greet(k, _):
        pl.semaphore_signal(barrier, 1, device_id={"seq": k * PLANE + p}, device_id_type=MESH)
        return 0

    lax.fori_loop(0, z, greet, 0)

    loads = [
        pltpu.make_async_copy(src, dst, l_sem.at[k])
        for k, (src, dst) in enumerate(
            [
                (x_hbm, x_ref.at[pl.ds(0, rows)]),
                (w_hbm.at[0], w_ref.at[0]),
                (w_hbm.at[1], w_ref.at[1]),
                (w_hbm.at[2], w_ref.at[2]),
                (down_hbm, dg_ref.at[:, pl.ds(0, 128)]),
                (gdown_hbm, dg_ref.at[:, pl.ds(128, 128)]),
                (beta_hbm, beta_ref),
                (span_hbm, span_ref),
                (ow_hbm, ow_ref),
            ]
        )
    ]
    for load in loads:
        load.start()
    x_ref[count + EDGE :, :] = jnp.zeros((HALO - EDGE, x_ref.shape[1]), BF16)

    @pl.when(s == 0)
    def _():
        x_ref[count : count + EDGE, :] = jnp.zeros((EDGE, x_ref.shape[1]), BF16)

    pl.semaphore_wait(
        barrier, 2 + PLANE - 1 + (depth - 1 - z) + jnp.where(sends_edge, 4, 0)
    )

    def piece(src, slot, half_at, target, k):
        return pltpu.make_async_remote_copy(
            src_ref=src,
            dst_ref=x_ref.at[pl.ds(slot * rows + half_at * half, half)],
            send_sem=x_send.at[k],
            recv_sem=x_recv.at[k],
            device_id={"head": target},
            device_id_type=MESH,
        )

    def rows_at(slot, half_at):
        return x_ref.at[pl.ds(slot * rows + half_at * half, half)]

    mine = [x_hbm.at[pl.ds(0, half)], x_hbm.at[pl.ds(half, half)]]
    moves = [
        piece(mine[0], 1, 0, right, 0),
        piece(mine[1], 2, 1, left, 1),
        piece(mine[1], 1, 1, right, 2),
        piece(mine[0], 2, 0, left, 3),
        piece(rows_at(1, 0), 3, 0, right, 4),
        piece(rows_at(2, 1), 3, 1, left, 5),
    ]
    for move in moves[:4]:
        move.start()

    def edge(target):
        return pltpu.make_async_remote_copy(
            src_ref=x_hbm.at[pl.ds(rows - EDGE, EDGE)],
            dst_ref=x_ref.at[pl.ds(count, EDGE)],
            send_sem=e_sem.at[target],
            recv_sem=e_sem.at[4],
            device_id={"seq": s + 1, "head": target},
            device_id_type=MESH,
        )

    @pl.when(sends_edge)
    def _():
        for target in range(4):
            edge(target).start()

    moves[0].wait_recv()
    moves[4].start()
    moves[1].wait_recv()
    moves[5].start()
    for load in loads[:7]:
        load.wait()
    moves[2].wait_recv()
    moves[3].wait_recv()

    def project(first, slots):
        size = len(slots) * rows
        at = [pl.ds(pl.multiple_of(slot * rows, 16), rows) for slot in slots]
        some = x_ref[first : first + size, :]
        both = jnp.dot(some, dg_ref[...], preferred_element_type=F32).astype(BF16)
        force = sigmoid(
            lax.dot_general(
                some, beta_ref[...], (((1,), (1,)), ((), ())), preferred_element_type=F32
            )
        )
        for n, where in enumerate(at):
            low_ref[where, :] = both[n * rows : (n + 1) * rows]
            strength_ref[where, :] = force[n * rows : (n + 1) * rows]

    def project_qkv(c, first, slots, tail):
        size = len(slots) * rows
        some = x_ref[first : first + size + tail, :]
        got = jnp.dot(some, w_ref[c], preferred_element_type=F32).astype(BF16).astype(F32)
        for n, slot in enumerate(slots):
            at = pl.ds(pl.multiple_of(HALO + slot * rows, 16), rows)
            proj_ref[c, at, :] = got[n * rows : (n + 1) * rows]
        if tail:
            proj_ref[c, HALO - EDGE : HALO, :] = got[size : size + EDGE]

    near = (h, left, right)
    project(0, near)
    for c in range(3):
        project_qkv(c, 0, near, 0)
    moves[4].wait_recv()
    moves[5].wait_recv()

    @pl.when(s > 0)
    def _():
        edge(0).wait_recv()

    project(3 * rows, (far,))
    for c in range(3):
        project_qkv(c, 3 * rows, (far,), HALO)

    raw = jnp.dot(low_ref[:, 0:128], up_ref[...], preferred_element_type=F32) + bias_ref[...]
    soft = jnp.maximum(raw, 0.0) + jnp.log1p(jnp.exp(-jnp.abs(raw)))
    rate = jnp.concatenate(
        [jnp.exp(jnp.full((1, 128), dlog_ref[i], F32)) for i in range(heads)], axis=1
    )
    log_decay = -rate * soft
    loads[7].wait()
    for c in range(2):
        piece_of = log_decay[c * HALF : (c + 1) * HALF]
        top = piece_of.astype(BF16)
        rest = (piece_of - top.astype(F32)).astype(BF16)
        e_ref[c] = jnp.exp(
            jnp.dot(
                span_ref[...], jnp.concatenate([top, rest], axis=0), preferred_element_type=F32
            )
        )
    gate_ref[...] = sigmoid(
        jnp.dot(low_ref[:, 128:256], gup_ref[...], preferred_element_type=F32)
    )
    beta = strength_ref[...]

    for c, target in enumerate((q_ref, k_ref, v_ref)):
        taps = conv_ref[c].astype(F32)
        mixed = proj_ref[c, pl.ds(HALO - 3, count), :] * taps[0:1]
        for i in range(1, 4):
            mixed = mixed + proj_ref[c, pl.ds(HALO - 3 + i, count), :] * taps[i : i + 1]
        mixed = (mixed * sigmoid(mixed)).astype(BF16).astype(F32)
        if c == 2:
            target[...] = mixed
            continue
        for i in range(heads):
            lanes = slice(i * 128, (i + 1) * 128)
            u = mixed[:, lanes]
            scale = lax.rsqrt(jnp.sum(u * u, axis=1, keepdims=True) + 1e-06)
            if c == 0:
                scale = scale * (128**-0.5)
            target[:, lanes] = u * scale

    t = lax.broadcasted_iota(jnp.int32, (HALF, HALF), 0)
    j = lax.broadcasted_iota(jnp.int32, (HALF, HALF), 1)
    row = lax.broadcasted_iota(jnp.int32, (HALF, 128), 0)
    masks = [
        ((t ^ j) >= size) & ((t ^ j) < 2 * size) & (t > j) for size in LEVELS
    ]
    diagonal = t == j

    pairs = [(i, c) for i in range(heads) for c in range(2)]
    lanes_of = [slice(i * 128, (i + 1) * 128) for i in range(heads)]
    rows_of = [slice(c * HALF, (c + 1) * HALF) for c in range(2)]
    strength = {
        (i, c): jnp.broadcast_to(beta[rows_of[c], i : i + 1], (HALF, 128)) for i, c in pairs
    }
    attend, inverse = {}, {}
    for i, c in pairs:
        kc, qc = k_ref[rows_of[c], lanes_of[i]], q_ref[rows_of[c], lanes_of[i]]
        own = jnp.sum(qc * kc, axis=1, keepdims=True) * strength[i, c]
        attend[i, c] = jnp.where(diagonal, own, 0.0)
        inverse[i, c] = jnp.where(diagonal, 1.0, 0.0)
    for n, size in enumerate(LEVELS):
        for i, c in pairs:
            kc, qc = k_ref[rows_of[c], lanes_of[i]], q_ref[rows_of[c], lanes_of[i]]
            fade = e_ref[c, n * HALF : (n + 1) * HALF, lanes_of[i]]
            late = (row & size) != 0
            kx = (kc * fade * jnp.where(late, 1.0, strength[i, c])).astype(BF16)
            qx = (qc * fade).astype(BF16)
            both = mm(jnp.concatenate([kx, qx], axis=0), kx, ((1,), (1,)))
            mixing = jnp.where(masks[n], both[:HALF], 0.0)
            attend[i, c] = jnp.where(masks[n], both[HALF:], attend[i, c])
            if size == 1:
                inverse[i, c] = inverse[i, c] - mixing
            else:
                own = inverse[i, c].astype(BF16)
                inverse[i, c] = inverse[i, c] - mm(mm(own, mixing), own)

    def to_owner(i):
        return pltpu.make_async_remote_copy(
            src_ref=z_ref.at[i],
            dst_ref=zin.at[p],
            send_sem=a_send.at[i],
            recv_sem=a_recv.at[p],
            device_id={"seq": base + 2 * i},
            device_id_type=MESH,
        )

    n = len(LEVELS)
    for i in range(heads):
        lanes = lanes_of[i]
        rise = [e_ref[c, n * HALF : (n + 1) * HALF, lanes] for c in range(2)]
        fall = [e_ref[c, (n + 1) * HALF : (n + 2) * HALF, lanes] for c in range(2)]
        whole = [part[HALF - 1 : HALF] for part in rise]
        k = [k_ref[rows_of[c], lanes] for c in range(2)]
        q = [q_ref[rows_of[c], lanes] for c in range(2)]
        k_rise = [k[c] * rise[c] for c in range(2)]
        q_rise = [q[c] * rise[c] for c in range(2)]
        k_fall = [k[c] * fall[c] * strength[i, c] for c in range(2)]
        cross = mm(jnp.concatenate([k_rise[1], q_rise[1]], axis=0), k_fall[0], ((1,), (1,)))
        first = mm(
            inverse[i, 0], jnp.concatenate([v_ref[rows_of[0], lanes], k_rise[0]], axis=1)
        ).astype(BF16)
        second = jnp.concatenate([v_ref[rows_of[1], lanes], k_rise[1] * whole[0]], axis=1)
        second = mm(inverse[i, 1], second - mm(cross[:HALF], first)).astype(BF16)
        out = [mm(attend[i, 0], first), mm(cross[HALF:], first) + mm(attend[i, 1], second)]
        for c in range(2):
            o_ref[rows_of[c], lanes] = out[c][:, :128]
        r_ref[rows_of[0], lanes] = (q_rise[0] - out[0][:, 128:]).astype(BF16)
        r_ref[rows_of[1], lanes] = (q_rise[1] * whole[0] - out[1][:, 128:]).astype(BF16)
        stop = jnp.concatenate([k_fall[0] * whole[1], k_fall[1]], axis=0).astype(BF16)
        maps = mm(jnp.concatenate([first, second], axis=0), stop, ((0,), (0,)))
        move = jnp.where(diagonal, whole[0] * whole[1], 0.0) - maps[128:]
        z_ref[i, 0:128] = move.astype(BF16)
        z_ref[i, 128:256] = maps[:128].astype(BF16)

        @pl.when(p != 2 * i)
        def _():
            to_owner(i).start()

    def to_later(k):
        return pltpu.make_async_remote_copy(
            src_ref=total,
            dst_ref=zall.at[z],
            send_sem=b_send.at[k],
            recv_sem=b_recv.at[z],
            device_id={"seq": k * PLANE + p},
            device_id_type=MESH,
        )

    def to_block(q):
        return pltpu.make_async_remote_copy(
            src_ref=lead.at[q],
            dst_ref=state.at[y],
            send_sem=c_send.at[q],
            recv_sem=c_recv.at[y],
            device_id={"seq": base + q},
            device_id_type=MESH,
        )

    def send_later(k, _):
        to_later(k).start()
        return 0

    def from_earlier(k, _):
        pltpu.make_async_remote_copy(
            src_ref=total,
            dst_ref=zall.at[k],
            send_sem=b_send.at[k],
            recv_sem=b_recv.at[k],
            device_id={"seq": s},
            device_id_type=MESH,
        ).wait_recv()
        held[...] = (mm(held[...], zall[k, 0:128]) + zall[k, 128:256].astype(F32)).astype(BF16)
        return 0

    @pl.when(owner)
    def _():
        zin[p] = z_ref[y]
        for k in range(PLANE):

            @pl.when(p != k)
            def _():
                pltpu.make_async_remote_copy(
                    src_ref=z_ref.at[0],
                    dst_ref=zin.at[k],
                    send_sem=a_send.at[0],
                    recv_sem=a_recv.at[k],
                    device_id={"seq": s},
                    device_id_type=MESH,
                ).wait_recv()

            if k == 0:
                so_far = zin[0]
            else:
                step = mm(so_far, zin[k, 0:128])
                so_far = jnp.concatenate(
                    [
                        step[:128].astype(BF16),
                        (step[128:] + zin[k, 128:256].astype(F32)).astype(BF16),
                    ],
                    axis=0,
                )
            if k < PLANE - 1:
                pre[k + 1] = so_far
            else:
                total[...] = so_far
        lax.fori_loop(z + 1, depth, send_later, 0)
        held[...] = jnp.zeros_like(held)
        lax.fori_loop(0, z, from_earlier, 0)
        carry = held[...]
        for q in range(PLANE):
            if q == 0:
                lead[0] = carry
            else:
                lead[q] = (mm(carry, pre[q, 0:128]) + pre[q, 128:256].astype(F32)).astype(BF16)

            @pl.when(p != q)
            def _():
                to_block(q).start()

        state[y] = lead[p]

    def states_in(i):
        @pl.when(p != 2 * i)
        def _():
            pltpu.make_async_remote_copy(
                src_ref=lead.at[0],
                dst_ref=state.at[i],
                send_sem=c_send.at[0],
                recv_sem=c_recv.at[i],
                device_id={"seq": s},
                device_id_type=MESH,
            ).wait_recv()

    for i in range(heads):
        states_in(i)
        lanes = lanes_of[i]
        attended = o_ref[:, lanes] + mm(r_ref[:, lanes], state[i], ((1,), (1,)))
        scale = lax.rsqrt(jnp.mean(attended * attended, axis=1, keepdims=True) + 1e-05)
        normed[:, lanes] = (attended * scale * gain_ref[...] * gate_ref[:, lanes]).astype(BF16)
    loads[8].wait()


    def partial(to):
        at = pl.ds(pl.multiple_of(to * rows, 16), rows)
        return jnp.dot(normed[at, :], ow_ref[...], preferred_element_type=F32)

    def pass_on(k, src, dst, target):
        return pltpu.make_async_remote_copy(
            src_ref=src,
            dst_ref=dst,
            send_sem=d_send.at[k],
            recv_sem=d_recv.at[k],
            device_id={"head": target},
            device_id_type=MESH,
        )

    top, low = pl.ds(0, half), pl.ds(half, half)
    part[0] = partial(far).astype(BF16)
    far_right = pass_on(0, part.at[0, top], inbox.at[0, top], right)
    far_left = pass_on(1, part.at[0, low], inbox.at[0, low], left)
    far_right.start()
    far_left.start()
    sums[0] = partial(right)
    part[1, low] = sums[0, low].astype(BF16)
    right_low = pass_on(2, part.at[1, low], inbox.at[1, low], right)
    right_low.start()
    sums[1] = partial(left)
    part[2, top] = sums[1, top].astype(BF16)
    left_top = pass_on(3, part.at[2, top], inbox.at[2, top], left)
    left_top.start()
    far_right.wait_recv()
    part[1, top] = (sums[0, top] + inbox[0, top].astype(F32)).astype(BF16)
    right_top = pass_on(4, part.at[1, top], inbox.at[1, top], right)
    right_top.start()
    far_left.wait_recv()
    part[2, low] = (sums[1, low] + inbox[0, low].astype(F32)).astype(BF16)
    left_low = pass_on(5, part.at[2, low], inbox.at[2, low], left)
    left_low.start()
    own = partial(h)
    right_low.wait_recv()
    left_top.wait_recv()
    right_top.wait_recv()
    left_low.wait_recv()
    out_ref[...] = (own + inbox[1].astype(F32) + inbox[2].astype(F32)).astype(BF16)

    for copy in (far_right, far_left, right_low, left_top, right_top, left_low):
        copy.wait_send()
    for move in moves:
        move.wait_send()

    @pl.when(sends_edge)
    def _():
        for target in range(4):
            edge(target).wait_send()

    for i in range(heads):

        @pl.when(p != 2 * i)
        def _():
            to_owner(i).wait_send()

    def sent(k, _):
        to_later(k).wait_send()
        return 0

    @pl.when(owner)
    def _():
        lax.fori_loop(z + 1, depth, sent, 0)
        for q in range(PLANE):

            @pl.when(p != q)
            def _():
                to_block(q).wait_send()


def layer(depth, x, w, down, gdown, beta, up, gup, conv, dlog, bias, span, gain, ow):
    vmem = pl.BlockSpec(memory_space=pltpu.VMEM)
    smem = pl.BlockSpec(memory_space=pltpu.SMEM)
    hbm = pl.BlockSpec(memory_space=pl.ANY)
    rows, model = x.shape
    count, width = 4 * rows, w.shape[2]
    heads = width // 128
    dma = pltpu.SemaphoreType.DMA
    return pl.pallas_call(
        functools.partial(kernel, depth),
        name="layer",
        out_shape=jax.ShapeDtypeStruct((rows, model), BF16),
        in_specs=[hbm] * 5 + [vmem] * 3 + [smem, vmem, hbm, vmem, hbm],
        out_specs=vmem,
        scratch_shapes=[
            pltpu.VMEM((count + HALO, model), BF16),
            pltpu.VMEM(w.shape, BF16),
            pltpu.VMEM((model, 256), BF16),
            pltpu.VMEM(beta.shape, BF16),
            pltpu.VMEM(span.shape, BF16),
            pltpu.VMEM(ow.shape, BF16),
            pltpu.VMEM((3, HALO + count, width), F32),
            pltpu.VMEM((count, 256), BF16),
            pltpu.VMEM((count, heads), F32),
            pltpu.VMEM((count, width), F32),
            pltpu.VMEM((count, width), F32),
            pltpu.VMEM((count, width), F32),
            pltpu.VMEM((2, (len(LEVELS) + 2) * HALF, width), F32),
            pltpu.VMEM((count, width), F32),
            pltpu.VMEM((count, width), BF16),
            pltpu.VMEM((count, width), F32),
            pltpu.VMEM((heads, 256, 128), BF16),
            pltpu.VMEM((PLANE, 256, 128), BF16),
            pltpu.VMEM((PLANE, 256, 128), BF16),
            pltpu.VMEM((256, 128), BF16),
            pltpu.VMEM((depth, 256, 128), BF16),
            pltpu.VMEM((128, 128), BF16),
            pltpu.VMEM((PLANE, 128, 128), BF16),
            pltpu.VMEM((heads, 128, 128), BF16),
            pltpu.VMEM((count, width), BF16),
            pltpu.VMEM((3, rows, model), BF16),
            pltpu.VMEM((2, rows, model), F32),
            pltpu.VMEM((3, rows, model), BF16),
            dma((9,)), dma((6,)), dma((6,)), dma((5,)),
            dma((heads,)), dma((PLANE,)), dma((depth,)), dma((depth,)),
            dma((PLANE,)), dma((heads,)), dma((6,)), dma((6,)),
        ],
        compiler_params=pltpu.CompilerParams(
            collective_id=0, has_side_effects=True, vmem_limit_bytes=56 << 20
        ),
    )(x, w, down, gdown, beta, up, gup, conv, dlog, bias, span, gain, ow)


def solution(mesh):
    seq_size = mesh.shape["seq"]
    span = span_matrix()

    def shards(
        hidden_in, qkv_weight, conv_weight, decay_log, dt_bias, decay_down, decay_up,
        beta_weight, gate_down, gate_up, norm_gain, out_weight,
    ):
        return layer(
            seq_size // PLANE,
            hidden_in,
            jnp.transpose(qkv_weight, (1, 0, 2)),
            decay_down,
            gate_down,
            beta_weight.T,
            decay_up,
            gate_up,
            conv_weight,
            decay_log,
            dt_bias.reshape(1, -1),
            jnp.asarray(span, BF16),
            norm_gain.reshape(1, -1),
            out_weight,
        )

    rows = P(("seq", "head"), None)
    return jax.shard_map(
        shards,
        mesh=mesh,
        in_specs=(
            rows, P(None, None, "head"), P(None, None, "head"), P("head"), P("head"), P(),
            P(None, "head"), P(None, "head"), P(), P(None, "head"), P(), P("head", None),
        ),
        out_specs=rows,
        check_vma=False,
    )
```

```python
import functools

import jax
import jax.numpy as jnp
import numpy as np
from jax import lax
from jax.experimental import pallas as pl
from jax.experimental.pallas import tpu as pltpu
from jax.sharding import PartitionSpec as P

F32 = jnp.float32
BF16 = jnp.bfloat16
MESH = pl.DeviceIdType.MESH

HALO = 16
EDGE = 8
HALF = 128
LEVELS = (1, 2, 4, 8, 16, 32, 64)
PLANE = 8
GROUP = 4


def span_matrix():
    r, i = np.arange(HALF)[:, None], np.arange(HALF)[None, :]
    rows = []
    for size in LEVELS:
        middle = (r // (2 * size)) * 2 * size + size - 1
        late = (r % (2 * size)) >= size
        rows.append(np.where(late, (i > middle) & (i <= r), (i > r) & (i <= middle)))
    rows.append(i <= r)
    rows.append(i > r)
    spans = np.concatenate(rows, axis=0)
    return np.concatenate([spans, spans], axis=1).astype(np.float32)


def mm(a, b, dims=((1,), (0,))):
    return lax.dot_general(
        a.astype(BF16), b.astype(BF16), (dims, ((), ())), preferred_element_type=F32
    )


def sigmoid(v):
    return 1.0 / (1.0 + jnp.exp(-v))


def kernel(
    depth, x_hbm, w_hbm, down_hbm, gdown_hbm, beta_hbm, up_ref, gup_ref, conv_ref, dlog_ref,
    bias_ref, span_hbm, gain_ref, ow_hbm, out_ref,
    x_ref, w_ref, dg_ref, beta_ref, span_ref, ow_ref,
    proj_ref, low_ref, strength_ref, q_ref, k_ref, v_ref, e_ref, o_ref, r_ref, gate_ref, z_ref,
    mix_ref, attend_ref, zin, pre, total, zall, chain, link, held, lead, state, normed, part, sums, inbox,
    l_sem, x_send, x_recv, e_sem, f_sem,
    a_send, a_recv, b_send, b_recv, c_send, c_recv, d_send, d_recv,
):
    s = lax.axis_index("seq")
    h = lax.axis_index("head")
    z = lax.div(s, PLANE)
    p = lax.rem(s, PLANE)
    y, core = lax.div(p, 2), lax.rem(p, 2)
    base = z * PLANE
    right, left, far = lax.rem(h + 1, 4), lax.rem(h + 3, 4), lax.rem(h + 2, 4)
    owner = core == 0
    group, rank = lax.div(z, GROUP), lax.rem(z, GROUP)
    feeds = jnp.logical_and(group == 0, jnp.logical_or(rank == 0, rank == GROUP - 1))
    has_next = s < depth * PLANE - 1
    edge_from = jnp.where(h == 1, 3, h)
    rows = x_hbm.shape[0]
    half = rows // 2
    count = 4 * rows
    width = w_ref.shape[2]
    heads = width // 128

    barrier = pltpu.get_barrier_semaphore()
    pl.semaphore_signal(barrier, 1, device_id={"head": right}, device_id_type=MESH)
    pl.semaphore_signal(barrier, 1, device_id={"head": left}, device_id_type=MESH)

    @pl.when(s > 0)
    def _():
        pl.semaphore_signal(
            barrier, 1, device_id={"seq": s - 1, "head": edge_from}, device_id_type=MESH
        )

    for d in range(1, PLANE):
        q = lax.rem(p + d, PLANE)

        @pl.when(jnp.logical_or(owner, lax.rem(q, 2) == 0))
        def _():
            pl.semaphore_signal(barrier, 1, device_id={"seq": base + q}, device_id_type=MESH)

    @pl.when(owner)
    def _():
        for d in range(1, GROUP):
            other = group * GROUP + lax.rem(rank + d, GROUP)
            pl.semaphore_signal(
                barrier, 1, device_id={"seq": other * PLANE + p}, device_id_type=MESH
            )

        @pl.when(group == 1)
        def _():
            feeder = jnp.where(rank < 2, GROUP - 1, 0)
            pl.semaphore_signal(
                barrier, 1, device_id={"seq": feeder * PLANE + p}, device_id_type=MESH
            )

    greeted = (
        2
        + jnp.where(owner, PLANE - 1 + GROUP - 1, PLANE // 2)
        + jnp.where(jnp.logical_and(owner, feeds), 2, 0)
        + jnp.where(has_next, jnp.where(h == 3, 2, jnp.where(h == 1, 0, 1)), 0)
    )

    loads = [
        pltpu.make_async_copy(src, dst, l_sem.at[k])
        for k, (src, dst) in enumerate(
            [
                (x_hbm, x_ref.at[pl.ds(0, rows)]),
                (w_hbm.at[0], w_ref.at[0]),
                (w_hbm.at[1], w_ref.at[1]),
                (w_hbm.at[2], w_ref.at[2]),
                (down_hbm, dg_ref.at[:, pl.ds(0, 128)]),
                (gdown_hbm, dg_ref.at[:, pl.ds(128, 128)]),
                (beta_hbm, beta_ref),
                (span_hbm, span_ref),
                (ow_hbm, ow_ref),
            ]
        )
    ]
    for load in loads:
        load.start()
    x_ref[count + EDGE :, :] = jnp.zeros((HALO - EDGE, x_ref.shape[1]), BF16)

    @pl.when(s == 0)
    def _():
        x_ref[count : count + EDGE, :] = jnp.zeros((EDGE, x_ref.shape[1]), BF16)

    pl.semaphore_wait(barrier, greeted)

    def piece(src, slot, half_at, target, k):
        return pltpu.make_async_remote_copy(
            src_ref=src,
            dst_ref=x_ref.at[pl.ds(slot * rows + half_at * half, half)],
            send_sem=x_send.at[k],
            recv_sem=x_recv.at[k],
            device_id={"head": target},
            device_id_type=MESH,
        )

    def rows_at(slot, half_at):
        return x_ref.at[pl.ds(slot * rows + half_at * half, half)]

    mine = [x_hbm.at[pl.ds(0, half)], x_hbm.at[pl.ds(half, half)]]
    moves = [
        piece(mine[0], 1, 0, right, 0),
        piece(mine[1], 2, 1, left, 1),
        piece(mine[1], 1, 1, right, 2),
        piece(mine[0], 2, 0, left, 3),
        piece(rows_at(1, 0), 3, 0, right, 4),
        piece(rows_at(2, 1), 3, 1, left, 5),
    ]
    for move in moves[:4]:
        move.start()

    def edge(k, src, target):
        return pltpu.make_async_remote_copy(
            src_ref=src,
            dst_ref=x_ref.at[pl.ds(count, EDGE)],
            send_sem=e_sem.at[k],
            recv_sem=e_sem.at[2],
            device_id={"seq": s + 1, "head": target},
            device_id_type=MESH,
        )

    last = pl.ds(rows - EDGE, EDGE)
    edges = {
        3: [edge(0, x_hbm.at[last], 3), edge(1, x_hbm.at[last], 1)],
        0: [edge(0, x_ref.at[pl.ds(2 * rows - EDGE, EDGE)], 0)],
        2: [edge(0, x_ref.at[pl.ds(3 * rows - EDGE, EDGE)], 2)],
    }

    def each_edge(head, act):
        @pl.when(jnp.logical_and(h == head, has_next))
        def _():
            for copy in edges[head]:
                act(copy)

    each_edge(3, lambda copy: copy.start())
    moves[0].wait_recv()
    moves[4].start()
    moves[1].wait_recv()
    moves[5].start()
    each_edge(2, lambda copy: copy.start())
    for load in loads[:7]:
        load.wait()
    moves[2].wait_recv()
    each_edge(0, lambda copy: copy.start())
    moves[3].wait_recv()

    def project(first, slots):
        size = len(slots) * rows
        at = [pl.ds(pl.multiple_of(slot * rows, 16), rows) for slot in slots]
        some = x_ref[first : first + size, :]
        both = jnp.dot(some, dg_ref[...], preferred_element_type=F32).astype(BF16)
        force = sigmoid(
            lax.dot_general(
                some, beta_ref[...], (((1,), (1,)), ((), ())), preferred_element_type=F32
            )
        )
        for n, where in enumerate(at):
            low_ref[where, :] = both[n * rows : (n + 1) * rows]
            strength_ref[where, :] = force[n * rows : (n + 1) * rows]

    def project_qkv(c, first, slots, tail):
        size = len(slots) * rows
        some = x_ref[first : first + size + tail, :]
        got = jnp.dot(some, w_ref[c], preferred_element_type=F32).astype(BF16).astype(F32)
        for n, slot in enumerate(slots):
            at = pl.ds(pl.multiple_of(HALO + slot * rows, 16), rows)
            proj_ref[c, at, :] = got[n * rows : (n + 1) * rows]
        if tail:
            proj_ref[c, HALO - EDGE : HALO, :] = got[size : size + EDGE]

    near = (h, left, right)
    project(0, near)
    for c in range(3):
        project_qkv(c, 0, near, 0)
    moves[4].wait_recv()
    moves[5].wait_recv()

    @pl.when(s > 0)
    def _():
        edges[0][0].wait_recv()

    project(3 * rows, (far,))
    for c in range(3):
        project_qkv(c, 3 * rows, (far,), HALO)

    raw = jnp.dot(low_ref[:, 0:128], up_ref[...], preferred_element_type=F32) + bias_ref[...]
    soft = jnp.maximum(raw, 0.0) + jnp.log1p(jnp.exp(-jnp.abs(raw)))
    rate = jnp.concatenate(
        [jnp.exp(jnp.full((1, 128), dlog_ref[i], F32)) for i in range(heads)], axis=1
    )
    log_decay = -rate * soft
    loads[7].wait()
    for c in range(2):
        piece_of = log_decay[c * HALF : (c + 1) * HALF]
        top = piece_of.astype(BF16)
        rest = (piece_of - top.astype(F32)).astype(BF16)
        e_ref[c] = jnp.exp(
            jnp.dot(
                span_ref[...], jnp.concatenate([top, rest], axis=0), preferred_element_type=F32
            )
        )
    gate_ref[...] = sigmoid(
        jnp.dot(low_ref[:, 128:256], gup_ref[...], preferred_element_type=F32)
    )
    beta = strength_ref[...]

    for c, target in enumerate((q_ref, k_ref, v_ref)):
        taps = conv_ref[c].astype(F32)
        mixed = proj_ref[c, pl.ds(HALO - 3, count), :] * taps[0:1]
        for i in range(1, 4):
            mixed = mixed + proj_ref[c, pl.ds(HALO - 3 + i, count), :] * taps[i : i + 1]
        mixed = (mixed * sigmoid(mixed)).astype(BF16).astype(F32)
        if c == 2:
            target[...] = mixed
            continue
        for i in range(heads):
            lanes = slice(i * 128, (i + 1) * 128)
            u = mixed[:, lanes]
            scale = lax.rsqrt(jnp.sum(u * u, axis=1, keepdims=True) + 1e-06)
            if c == 0:
                scale = scale * (128**-0.5)
            target[:, lanes] = u * scale

    t = lax.broadcasted_iota(jnp.int32, (HALF, HALF), 0)
    j = lax.broadcasted_iota(jnp.int32, (HALF, HALF), 1)
    row = lax.broadcasted_iota(jnp.int32, (HALF, 128), 0)
    masks = [
        ((t ^ j) >= size) & ((t ^ j) < 2 * size) & (t > j) for size in LEVELS
    ]
    diagonal = t == j

    lanes_of = [slice(i * 128, (i + 1) * 128) for i in range(heads)]
    rows_of = [slice(c * HALF, (c + 1) * HALF) for c in range(2)]

    def to_owner(i):
        return pltpu.make_async_remote_copy(
            src_ref=z_ref.at[i],
            dst_ref=zin.at[p],
            send_sem=a_send.at[i],
            recv_sem=a_recv.at[p],
            device_id={"seq": base + 2 * i},
            device_id_type=MESH,
        )

    for pair in range(0, heads, 2):
        some = range(pair, pair + 2)
        units = [(i, c) for i in some for c in range(2)]
        strength, inverse = {}, {}
        for u, (i, c) in enumerate(units):
            kc, qc = k_ref[rows_of[c], lanes_of[i]], q_ref[rows_of[c], lanes_of[i]]
            strength[i, c] = jnp.broadcast_to(beta[rows_of[c], i : i + 1], (HALF, 128))
            own = jnp.sum(qc * kc, axis=1, keepdims=True) * strength[i, c]
            attend = jnp.where(diagonal, own, 0.0)
            for n, size in enumerate(LEVELS):
                fade = e_ref[c, n * HALF : (n + 1) * HALF, lanes_of[i]]
                late = (row & size) != 0
                kx = (kc * fade * jnp.where(late, 1.0, strength[i, c])).astype(BF16)
                qx = (qc * fade).astype(BF16)
                both = mm(jnp.concatenate([kx, qx], axis=0), kx, ((1,), (1,)))
                mix_ref[u, n] = jnp.where(masks[n], both[:HALF], 0.0).astype(BF16)
                attend = jnp.where(masks[n], both[HALF:], attend)
            attend_ref[u] = attend.astype(BF16)
        for u, unit in enumerate(units):
            inverse[unit] = jnp.where(diagonal, 1.0, 0.0) - mix_ref[u, 0].astype(F32)
        for n in range(1, len(LEVELS)):
            own = {unit: inverse[unit].astype(BF16) for unit in units}
            left_part = {
                unit: mm(own[unit], mix_ref[u, n]).astype(BF16) for u, unit in enumerate(units)
            }
            for unit in units:
                inverse[unit] = inverse[unit] - mm(left_part[unit], own[unit])
        inverse = {unit: inverse[unit].astype(BF16) for unit in units}

        n = len(LEVELS)
        rise = {u: e_ref[u[1], n * HALF : (n + 1) * HALF, lanes_of[u[0]]] for u in units}
        fall = {u: e_ref[u[1], (n + 1) * HALF : (n + 2) * HALF, lanes_of[u[0]]] for u in units}
        whole = {u: rise[u][HALF - 1 : HALF] for u in units}
        k_rise = {u: k_ref[rows_of[u[1]], lanes_of[u[0]]] * rise[u] for u in units}
        q_rise = {u: q_ref[rows_of[u[1]], lanes_of[u[0]]] * rise[u] for u in units}
        k_fall = {
            u: k_ref[rows_of[u[1]], lanes_of[u[0]]] * fall[u] * strength[u] for u in units
        }
        cross, first, second = {}, {}, {}
        for i in some:
            cross[i] = mm(
                jnp.concatenate([k_rise[i, 1], q_rise[i, 1]], axis=0), k_fall[i, 0], ((1,), (1,))
            ).astype(BF16)
        for i in some:
            first[i] = mm(
                inverse[i, 0],
                jnp.concatenate([v_ref[rows_of[0], lanes_of[i]], k_rise[i, 0]], axis=1),
            ).astype(BF16)
        late_part = {i: mm(cross[i], first[i]) for i in some}
        for i in some:
            start = jnp.concatenate(
                [v_ref[rows_of[1], lanes_of[i]], k_rise[i, 1] * whole[i, 0]], axis=1
            )
            second[i] = mm(inverse[i, 1], start - late_part[i][:HALF]).astype(BF16)
        for i in some:
            stop = jnp.concatenate(
                [k_fall[i, 0] * whole[i, 1], k_fall[i, 1]], axis=0
            ).astype(BF16)
            maps = mm(jnp.concatenate([first[i], second[i]], axis=0), stop, ((0,), (0,)))
            move = jnp.where(diagonal, whole[i, 0] * whole[i, 1], 0.0) - maps[128:]
            z_ref[i, 0:128] = move.astype(BF16)
            z_ref[i, 128:256] = maps[:128].astype(BF16)

            @pl.when(p != 2 * i)
            def _():
                to_owner(i).start()

        for i in some:
            lanes = lanes_of[i]
            u = 2 * (i - pair)
            out = [
                mm(attend_ref[u], first[i]),
                late_part[i][HALF:] + mm(attend_ref[u + 1], second[i]),
            ]
            for c in range(2):
                o_ref[rows_of[c], lanes] = out[c][:, :128]
            r_ref[rows_of[0], lanes] = (q_rise[i, 0] - out[0][:, 128:]).astype(BF16)
            r_ref[rows_of[1], lanes] = (
                q_rise[i, 1] * whole[i, 0] - out[1][:, 128:]
            ).astype(BF16)

    def to_group(k):
        return pltpu.make_async_remote_copy(
            src_ref=total,
            dst_ref=zall.at[rank],
            send_sem=b_send.at[k],
            recv_sem=b_recv.at[rank],
            device_id={"seq": (group * GROUP + k) * PLANE + p},
            device_id_type=MESH,
        )

    def to_next(k):
        target = jnp.where(rank == 0, 2 * GROUP - 1 - k, GROUP + k)
        return pltpu.make_async_remote_copy(
            src_ref=chain.at[GROUP],
            dst_ref=held,
            send_sem=f_sem.at[k],
            recv_sem=f_sem.at[2],
            device_id={"seq": target * PLANE + p},
            device_id_type=MESH,
        )

    def to_block(q):
        return pltpu.make_async_remote_copy(
            src_ref=lead.at[q],
            dst_ref=state.at[y],
            send_sem=c_send.at[q],
            recv_sem=c_recv.at[y],
            device_id={"seq": base + q},
            device_id_type=MESH,
        )

    def arrived(ref, sem, k, here):
        @pl.when(here != k)
        def _():
            pltpu.make_async_remote_copy(
                src_ref=ref.at[k],
                dst_ref=ref.at[k],
                send_sem=sem.at[k],
                recv_sem=sem.at[k],
                device_id={"seq": s},
                device_id_type=MESH,
            ).wait_recv()

    def after(so_far, ref, k):
        step = mm(so_far, ref[k, 0:128])
        return jnp.concatenate(
            [step[:128].astype(BF16), (step[128:] + ref[k, 128:256].astype(F32)).astype(BF16)],
            axis=0,
        )

    def moved(entry, at):
        return (mm(entry, pre[at, 0:128]) + pre[at, 128:256].astype(F32)).astype(BF16)

    @pl.when(owner)
    def _():
        zin[p] = z_ref[y]
        for k in range(PLANE):
            arrived(zin, a_recv, k, p)
        half_plane = PLANE // 2
        one, two = zin[0], zin[half_plane]
        for k in range(1, half_plane):
            pre[k], pre[half_plane + k] = one, two
            one, two = after(one, zin, k), after(two, zin, half_plane + k)
        pre[half_plane] = one
        step = mm(one, two[:128])
        whole_map = jnp.concatenate(
            [step[:128].astype(BF16), (step[128:] + two[128:].astype(F32)).astype(BF16)], axis=0
        )
        total[...] = whole_map
        for k in range(GROUP):

            @pl.when(rank != k)
            def _():
                to_group(k).start()

        zall[rank] = whole_map
        for k in range(GROUP):
            arrived(zall, b_recv, k, rank)

        @pl.when(group == 0)
        def _():
            chain[0] = jnp.zeros((128, 128), BF16)
            so_far = zall[0, 128:256]
            chain[1] = so_far
            for k in range(1, GROUP):
                so_far = (
                    mm(so_far, zall[k, 0:128]) + zall[k, 128:256].astype(F32)
                ).astype(BF16)
                chain[k + 1] = so_far

            @pl.when(feeds)
            def _():
                for k in range(2):
                    to_next(k).start()

            held[...] = chain[rank]

        @pl.when(group == 1)
        def _():
            link[0, 0:128] = jnp.where(diagonal, 1.0, 0.0).astype(BF16)
            link[0, 128:256] = jnp.zeros((128, 128), BF16)
            so_far = zall[0]
            link[1] = so_far
            for k in range(1, GROUP - 1):
                so_far = after(so_far, zall, k)
                link[k + 1] = so_far
            to_next(0).wait_recv()
            held[...] = (
                mm(held[...], link[rank, 0:128]) + link[rank, 128:256].astype(F32)
            ).astype(BF16)

        entry = held[...]
        for q in (half_plane, 0, 1, 2, 3, 5, 6, 7):
            if q == half_plane:
                middle = moved(entry, q)
                lead[q] = middle
            elif q == 0:
                lead[q] = entry
            else:
                lead[q] = moved(entry if q < half_plane else middle, q)

            @pl.when(p != q)
            def _():
                to_block(q).start()

        state[y] = lead[p]

    def states_in(i):
        @pl.when(p != 2 * i)
        def _():
            pltpu.make_async_remote_copy(
                src_ref=lead.at[0],
                dst_ref=state.at[i],
                send_sem=c_send.at[0],
                recv_sem=c_recv.at[i],
                device_id={"seq": s},
                device_id_type=MESH,
            ).wait_recv()

    for i in range(heads):
        states_in(i)
        lanes = lanes_of[i]
        attended = o_ref[:, lanes] + mm(r_ref[:, lanes], state[i], ((1,), (1,)))
        scale = lax.rsqrt(jnp.mean(attended * attended, axis=1, keepdims=True) + 1e-05)
        normed[:, lanes] = (attended * scale * gain_ref[...] * gate_ref[:, lanes]).astype(BF16)
    loads[8].wait()


    def partial(to):
        at = pl.ds(pl.multiple_of(to * rows, 16), rows)
        return jnp.dot(normed[at, :], ow_ref[...], preferred_element_type=F32)

    def pass_on(k, src, dst, target):
        return pltpu.make_async_remote_copy(
            src_ref=src,
            dst_ref=dst,
            send_sem=d_send.at[k],
            recv_sem=d_recv.at[k],
            device_id={"head": target},
            device_id_type=MESH,
        )

    top, low = pl.ds(0, half), pl.ds(half, half)
    part[0] = partial(far).astype(BF16)
    far_right = pass_on(0, part.at[0, top], inbox.at[0, top], right)
    far_left = pass_on(1, part.at[0, low], inbox.at[0, low], left)
    far_right.start()
    far_left.start()
    sums[0] = partial(right)
    part[1, low] = sums[0, low].astype(BF16)
    right_low = pass_on(2, part.at[1, low], inbox.at[1, low], right)
    right_low.start()
    sums[1] = partial(left)
    part[2, top] = sums[1, top].astype(BF16)
    left_top = pass_on(3, part.at[2, top], inbox.at[2, top], left)
    left_top.start()
    far_right.wait_recv()
    part[1, top] = (sums[0, top] + inbox[0, top].astype(F32)).astype(BF16)
    right_top = pass_on(4, part.at[1, top], inbox.at[1, top], right)
    right_top.start()
    far_left.wait_recv()
    part[2, low] = (sums[1, low] + inbox[0, low].astype(F32)).astype(BF16)
    left_low = pass_on(5, part.at[2, low], inbox.at[2, low], left)
    left_low.start()
    own = partial(h)
    right_low.wait_recv()
    left_top.wait_recv()
    right_top.wait_recv()
    left_low.wait_recv()
    out_ref[...] = (own + inbox[1].astype(F32) + inbox[2].astype(F32)).astype(BF16)

    for copy in (far_right, far_left, right_low, left_top, right_top, left_low):
        copy.wait_send()
    for move in moves:
        move.wait_send()

    for head in (0, 2, 3):
        each_edge(head, lambda copy: copy.wait_send())

    for i in range(heads):

        @pl.when(p != 2 * i)
        def _():
            to_owner(i).wait_send()

    @pl.when(owner)
    def _():
        for k in range(GROUP):

            @pl.when(rank != k)
            def _():
                to_group(k).wait_send()

        @pl.when(feeds)
        def _():
            for k in range(2):
                to_next(k).wait_send()

        for q in range(PLANE):

            @pl.when(p != q)
            def _():
                to_block(q).wait_send()


def layer(depth, x, w, down, gdown, beta, up, gup, conv, dlog, bias, span, gain, ow):
    vmem = pl.BlockSpec(memory_space=pltpu.VMEM)
    smem = pl.BlockSpec(memory_space=pltpu.SMEM)
    hbm = pl.BlockSpec(memory_space=pl.ANY)
    rows, model = x.shape
    count, width = 4 * rows, w.shape[2]
    heads = width // 128
    dma = pltpu.SemaphoreType.DMA
    return pl.pallas_call(
        functools.partial(kernel, depth),
        name="layer",
        out_shape=jax.ShapeDtypeStruct((rows, model), BF16),
        in_specs=[hbm] * 5 + [vmem] * 3 + [smem, vmem, hbm, vmem, hbm],
        out_specs=vmem,
        scratch_shapes=[
            pltpu.VMEM((count + HALO, model), BF16),
            pltpu.VMEM(w.shape, BF16),
            pltpu.VMEM((model, 256), BF16),
            pltpu.VMEM(beta.shape, BF16),
            pltpu.VMEM(span.shape, BF16),
            pltpu.VMEM(ow.shape, BF16),
            pltpu.VMEM((3, HALO + count, width), F32),
            pltpu.VMEM((count, 256), BF16),
            pltpu.VMEM((count, heads), F32),
            pltpu.VMEM((count, width), F32),
            pltpu.VMEM((count, width), F32),
            pltpu.VMEM((count, width), F32),
            pltpu.VMEM((2, (len(LEVELS) + 2) * HALF, width), F32),
            pltpu.VMEM((count, width), F32),
            pltpu.VMEM((count, width), BF16),
            pltpu.VMEM((count, width), F32),
            pltpu.VMEM((heads, 256, 128), BF16),
            pltpu.VMEM((4, len(LEVELS), HALF, HALF), BF16),
            pltpu.VMEM((4, HALF, HALF), BF16),
            pltpu.VMEM((PLANE, 256, 128), BF16),
            pltpu.VMEM((PLANE, 256, 128), BF16),
            pltpu.VMEM((256, 128), BF16),
            pltpu.VMEM((GROUP, 256, 128), BF16),
            pltpu.VMEM((GROUP + 1, 128, 128), BF16),
            pltpu.VMEM((GROUP, 256, 128), BF16),
            pltpu.VMEM((128, 128), BF16),
            pltpu.VMEM((PLANE, 128, 128), BF16),
            pltpu.VMEM((heads, 128, 128), BF16),
            pltpu.VMEM((count, width), BF16),
            pltpu.VMEM((3, rows, model), BF16),
            pltpu.VMEM((2, rows, model), F32),
            pltpu.VMEM((3, rows, model), BF16),
            dma((9,)), dma((6,)), dma((6,)), dma((3,)), dma((3,)),
            dma((heads,)), dma((PLANE,)), dma((GROUP,)), dma((GROUP,)),
            dma((PLANE,)), dma((heads,)), dma((6,)), dma((6,)),
        ],
        compiler_params=pltpu.CompilerParams(
            collective_id=0, has_side_effects=True, vmem_limit_bytes=56 << 20
        ),
    )(x, w, down, gdown, beta, up, gup, conv, dlog, bias, span, gain, ow)


def solution(mesh):
    seq_size = mesh.shape["seq"]
    span = span_matrix()

    def shards(
        hidden_in, qkv_weight, conv_weight, decay_log, dt_bias, decay_down, decay_up,
        beta_weight, gate_down, gate_up, norm_gain, out_weight,
    ):
        return layer(
            seq_size // PLANE,
            hidden_in,
            jnp.transpose(qkv_weight, (1, 0, 2)),
            decay_down,
            gate_down,
            beta_weight.T,
            decay_up,
            gate_up,
            conv_weight,
            decay_log,
            dt_bias.reshape(1, -1),
            jnp.asarray(span, BF16),
            norm_gain.reshape(1, -1),
            out_weight,
        )

    rows = P(("seq", "head"), None)
    return jax.shard_map(
        shards,
        mesh=mesh,
        in_specs=(
            rows, P(None, None, "head"), P(None, None, "head"), P("head"), P("head"), P(),
            P(None, "head"), P(None, "head"), P(), P(None, "head"), P(), P("head", None),
        ),
        out_specs=rows,
        check_vma=False,
    )
```

```python
import functools

import jax
import jax.numpy as jnp
import numpy as np
from jax import lax
from jax.experimental import pallas as pl
from jax.experimental.pallas import tpu as pltpu
from jax.sharding import PartitionSpec as P

F32 = jnp.float32
BF16 = jnp.bfloat16
MESH = pl.DeviceIdType.MESH

HALO = 16
EDGE = 8
HALF = 128
LEVELS = (1, 2, 4, 8, 16, 32, 64)
PLANE = 8
GROUP = 4


def span_matrix():
    r, i = np.arange(HALF)[:, None], np.arange(HALF)[None, :]
    rows = []
    for size in LEVELS:
        middle = (r // (2 * size)) * 2 * size + size - 1
        late = (r % (2 * size)) >= size
        rows.append(np.where(late, (i > middle) & (i <= r), (i > r) & (i <= middle)))
    rows.append(i <= r)
    rows.append(i > r)
    spans = np.concatenate(rows, axis=0)
    return np.concatenate([spans, spans], axis=1).astype(np.float32)


def mm(a, b, dims=((1,), (0,))):
    return lax.dot_general(
        a.astype(BF16), b.astype(BF16), (dims, ((), ())), preferred_element_type=F32
    )


def sigmoid(v):
    return 1.0 / (1.0 + jnp.exp(-v))


def kernel(
    depth, x_hbm, w_hbm, down_hbm, gdown_hbm, beta_hbm, up_ref, gup_ref, conv_ref, dlog_ref,
    bias_ref, span_hbm, gain_ref, ow_hbm, out_ref,
    x_ref, w_ref, dg_ref, beta_ref, span_ref, ow_ref,
    proj_ref, fade_ref, strength_ref, q_ref, k_ref, v_ref, e_ref, o_ref, r_ref, gate_ref, z_ref,
    mix_ref, attend_ref, zin, pre, total, zall, chain, link, held, entry, lead, state, normed, part, sums, inbox,
    l_sem, x_send, x_recv, e_sem, f_sem, g_send, g_recv,
    a_send, a_recv, b_send, b_recv, c_send, c_recv, d_send, d_recv,
):
    s = lax.axis_index("seq")
    h = lax.axis_index("head")
    z = lax.div(s, PLANE)
    p = lax.rem(s, PLANE)
    y, core = lax.div(p, 2), lax.rem(p, 2)
    base = z * PLANE
    right, left, far = lax.rem(h + 1, 4), lax.rem(h + 3, 4), lax.rem(h + 2, 4)
    owner = core == 0
    group, rank = lax.div(z, GROUP), lax.rem(z, GROUP)
    feeds = jnp.logical_and(group == 0, jnp.logical_or(rank == 0, rank == GROUP - 1))
    has_next = s < depth * PLANE - 1
    edge_from = jnp.where(h == 1, 3, h)
    rows = x_hbm.shape[0]
    half = rows // 2
    count = 4 * rows
    width = w_ref.shape[2]
    heads = width // 128

    barrier = pltpu.get_barrier_semaphore()
    pl.semaphore_signal(barrier, 1, device_id={"head": right}, device_id_type=MESH)
    pl.semaphore_signal(barrier, 1, device_id={"head": left}, device_id_type=MESH)

    @pl.when(s > 0)
    def _():
        pl.semaphore_signal(
            barrier, 1, device_id={"seq": s - 1, "head": edge_from}, device_id_type=MESH
        )

    for d in range(1, PLANE):
        q = lax.rem(p + d, PLANE)

        @pl.when(jnp.logical_or(owner, lax.rem(q, 2) == 0))
        def _():
            pl.semaphore_signal(barrier, 1, device_id={"seq": base + q}, device_id_type=MESH)

    @pl.when(owner)
    def _():
        for d in range(1, GROUP):
            other = group * GROUP + lax.rem(rank + d, GROUP)
            pl.semaphore_signal(
                barrier, 1, device_id={"seq": other * PLANE + p}, device_id_type=MESH
            )

        @pl.when(group == 1)
        def _():
            feeder = jnp.where(rank < 2, GROUP - 1, 0)
            pl.semaphore_signal(
                barrier, 1, device_id={"seq": feeder * PLANE + p}, device_id_type=MESH
            )

    greeted = (
        2
        + jnp.where(owner, PLANE - 1 + GROUP - 1, PLANE // 2)
        + jnp.where(jnp.logical_and(owner, feeds), 2, 0)
        + jnp.where(has_next, jnp.where(h == 3, 2, jnp.where(h == 1, 0, 1)), 0)
    )

    loads = [
        pltpu.make_async_copy(src, dst, l_sem.at[k])
        for k, (src, dst) in enumerate(
            [
                (x_hbm, x_ref.at[pl.ds(0, rows)]),
                (w_hbm.at[0], w_ref.at[0]),
                (w_hbm.at[1], w_ref.at[1]),
                (w_hbm.at[2], w_ref.at[2]),
                (down_hbm, dg_ref.at[:, pl.ds(0, 128)]),
                (gdown_hbm, dg_ref.at[:, pl.ds(128, 128)]),
                (beta_hbm, beta_ref),
                (span_hbm, span_ref),
                (ow_hbm, ow_ref),
            ]
        )
    ]
    for load in loads:
        load.start()
    x_ref[count + EDGE :, :] = jnp.zeros((HALO - EDGE, x_ref.shape[1]), BF16)

    @pl.when(s == 0)
    def _():
        x_ref[count : count + EDGE, :] = jnp.zeros((EDGE, x_ref.shape[1]), BF16)

    pl.semaphore_wait(barrier, greeted)

    def piece(src, slot, half_at, target, k):
        return pltpu.make_async_remote_copy(
            src_ref=src,
            dst_ref=x_ref.at[pl.ds(slot * rows + half_at * half, half)],
            send_sem=x_send.at[k],
            recv_sem=x_recv.at[k],
            device_id={"head": target},
            device_id_type=MESH,
        )

    def rows_at(slot, half_at):
        return x_ref.at[pl.ds(slot * rows + half_at * half, half)]

    mine = [x_hbm.at[pl.ds(0, half)], x_hbm.at[pl.ds(half, half)]]
    moves = [
        piece(mine[0], 1, 0, right, 0),
        piece(mine[1], 2, 1, left, 1),
        piece(mine[1], 1, 1, right, 2),
        piece(mine[0], 2, 0, left, 3),
        piece(rows_at(1, 0), 3, 0, right, 4),
        piece(rows_at(2, 1), 3, 1, left, 5),
    ]
    for move in moves[:4]:
        move.start()

    def edge(k, src, target):
        return pltpu.make_async_remote_copy(
            src_ref=src,
            dst_ref=x_ref.at[pl.ds(count, EDGE)],
            send_sem=e_sem.at[k],
            recv_sem=e_sem.at[2],
            device_id={"seq": s + 1, "head": target},
            device_id_type=MESH,
        )

    last = pl.ds(rows - EDGE, EDGE)
    edges = {
        3: [edge(0, x_hbm.at[last], 3), edge(1, x_hbm.at[last], 1)],
        0: [edge(0, x_ref.at[pl.ds(2 * rows - EDGE, EDGE)], 0)],
        2: [edge(0, x_ref.at[pl.ds(3 * rows - EDGE, EDGE)], 2)],
    }

    def each_edge(head, act):
        @pl.when(jnp.logical_and(h == head, has_next))
        def _():
            for copy in edges[head]:
                act(copy)

    each_edge(3, lambda copy: copy.start())
    moves[0].wait_recv()
    moves[2].wait_send()
    moves[4].start()
    moves[1].wait_recv()
    moves[3].wait_send()
    moves[5].start()
    each_edge(2, lambda copy: copy.start())
    for load in loads[:7]:
        load.wait()
    moves[2].wait_recv()
    each_edge(0, lambda copy: copy.start())
    moves[3].wait_recv()

    rate = jnp.concatenate(
        [jnp.exp(jnp.full((1, 128), dlog_ref[i], F32)) for i in range(heads)], axis=1
    )

    def project(first, slots):
        size = len(slots) * rows
        at = [pl.ds(pl.multiple_of(slot * rows, 16), rows) for slot in slots]
        some = x_ref[first : first + size, :]
        both = jnp.dot(some, dg_ref[...], preferred_element_type=F32).astype(BF16)
        force = sigmoid(
            lax.dot_general(
                some, beta_ref[...], (((1,), (1,)), ((), ())), preferred_element_type=F32
            )
        )
        raw = jnp.dot(both[:, 0:128], up_ref[...], preferred_element_type=F32) + bias_ref[...]
        soft = jnp.maximum(raw, 0.0) + jnp.log1p(jnp.exp(-jnp.abs(raw)))
        log_decay = -rate * soft
        gate = sigmoid(jnp.dot(both[:, 128:256], gup_ref[...], preferred_element_type=F32))
        for n, where in enumerate(at):
            own = slice(n * rows, (n + 1) * rows)
            fade_ref[where, :] = log_decay[own]
            gate_ref[where, :] = gate[own]
            strength_ref[where, :] = force[own]

    def project_qkv(c, first, slots, tail):
        size = len(slots) * rows
        some = x_ref[first : first + size + tail, :]
        got = jnp.dot(some, w_ref[c], preferred_element_type=F32).astype(BF16).astype(F32)
        for n, slot in enumerate(slots):
            at = pl.ds(pl.multiple_of(HALO + slot * rows, 16), rows)
            proj_ref[c, at, :] = got[n * rows : (n + 1) * rows]
        if tail:
            proj_ref[c, HALO - EDGE : HALO, :] = got[size : size + EDGE]

    near = (h, left, right)
    project(0, near)
    for c in range(3):
        project_qkv(c, 0, near, 0)
    moves[4].wait_recv()
    moves[5].wait_recv()

    @pl.when(s > 0)
    def _():
        edges[0][0].wait_recv()

    project(3 * rows, (far,))
    for c in range(3):
        project_qkv(c, 3 * rows, (far,), HALO)

    loads[7].wait()
    for c in range(2):
        piece_of = fade_ref[c * HALF : (c + 1) * HALF, :]
        top = piece_of.astype(BF16)
        rest = (piece_of - top.astype(F32)).astype(BF16)
        e_ref[c] = jnp.exp(
            jnp.dot(
                span_ref[...], jnp.concatenate([top, rest], axis=0), preferred_element_type=F32
            )
        )
    beta = strength_ref[...]

    for c, target in enumerate((q_ref, k_ref, v_ref)):
        taps = conv_ref[c].astype(F32)
        mixed = proj_ref[c, pl.ds(HALO - 3, count), :] * taps[0:1]
        for i in range(1, 4):
            mixed = mixed + proj_ref[c, pl.ds(HALO - 3 + i, count), :] * taps[i : i + 1]
        mixed = (mixed * sigmoid(mixed)).astype(BF16).astype(F32)
        if c == 2:
            target[...] = mixed
            continue
        for i in range(heads):
            lanes = slice(i * 128, (i + 1) * 128)
            u = mixed[:, lanes]
            scale = lax.rsqrt(jnp.sum(u * u, axis=1, keepdims=True) + 1e-06)
            if c == 0:
                scale = scale * (128**-0.5)
            target[:, lanes] = u * scale

    t = lax.broadcasted_iota(jnp.int32, (HALF, HALF), 0)
    j = lax.broadcasted_iota(jnp.int32, (HALF, HALF), 1)
    row = lax.broadcasted_iota(jnp.int32, (HALF, 128), 0)
    masks = [
        ((t ^ j) >= size) & ((t ^ j) < 2 * size) & (t > j) for size in LEVELS
    ]
    diagonal = t == j

    lanes_of = [slice(i * 128, (i + 1) * 128) for i in range(heads)]
    rows_of = [slice(c * HALF, (c + 1) * HALF) for c in range(2)]

    def to_owner(i):
        return pltpu.make_async_remote_copy(
            src_ref=z_ref.at[i],
            dst_ref=zin.at[p],
            send_sem=a_send.at[i],
            recv_sem=a_recv.at[p],
            device_id={"seq": base + 2 * i},
            device_id_type=MESH,
        )

    for pair in range(0, heads, 2):
        some = range(pair, pair + 2)
        units = [(i, c) for i in some for c in range(2)]
        strength, inverse = {}, {}
        for u, (i, c) in enumerate(units):
            kc, qc = k_ref[rows_of[c], lanes_of[i]], q_ref[rows_of[c], lanes_of[i]]
            strength[i, c] = jnp.broadcast_to(beta[rows_of[c], i : i + 1], (HALF, 128))
            own = jnp.sum(qc * kc, axis=1, keepdims=True) * strength[i, c]
            attend = jnp.where(diagonal, own, 0.0)
            for n, size in enumerate(LEVELS):
                fade = e_ref[c, n * HALF : (n + 1) * HALF, lanes_of[i]]
                late = (row & size) != 0
                kx = (kc * fade * jnp.where(late, 1.0, strength[i, c])).astype(BF16)
                qx = (qc * fade).astype(BF16)
                both = mm(jnp.concatenate([kx, qx], axis=0), kx, ((1,), (1,)))
                mix_ref[u, n] = jnp.where(masks[n], both[:HALF], 0.0).astype(BF16)
                attend = jnp.where(masks[n], both[HALF:], attend)
            attend_ref[u] = attend.astype(BF16)
        for u, unit in enumerate(units):
            inverse[unit] = jnp.where(diagonal, 1.0, 0.0) - mix_ref[u, 0].astype(F32)
        for n in range(1, len(LEVELS)):
            own = {unit: inverse[unit].astype(BF16) for unit in units}
            left_part = {
                unit: mm(own[unit], mix_ref[u, n]).astype(BF16) for u, unit in enumerate(units)
            }
            for unit in units:
                inverse[unit] = inverse[unit] - mm(left_part[unit], own[unit])
        inverse = {unit: inverse[unit].astype(BF16) for unit in units}

        n = len(LEVELS)
        rise = {u: e_ref[u[1], n * HALF : (n + 1) * HALF, lanes_of[u[0]]] for u in units}
        fall = {u: e_ref[u[1], (n + 1) * HALF : (n + 2) * HALF, lanes_of[u[0]]] for u in units}
        whole = {u: rise[u][HALF - 1 : HALF] for u in units}
        k_rise = {u: k_ref[rows_of[u[1]], lanes_of[u[0]]] * rise[u] for u in units}
        q_rise = {u: q_ref[rows_of[u[1]], lanes_of[u[0]]] * rise[u] for u in units}
        k_fall = {
            u: k_ref[rows_of[u[1]], lanes_of[u[0]]] * fall[u] * strength[u] for u in units
        }
        cross, first, second = {}, {}, {}
        for i in some:
            cross[i] = mm(
                jnp.concatenate([k_rise[i, 1], q_rise[i, 1]], axis=0), k_fall[i, 0], ((1,), (1,))
            ).astype(BF16)
        for i in some:
            first[i] = mm(
                inverse[i, 0],
                jnp.concatenate([v_ref[rows_of[0], lanes_of[i]], k_rise[i, 0]], axis=1),
            ).astype(BF16)
        late_part = {i: mm(cross[i], first[i]) for i in some}
        for i in some:
            start = jnp.concatenate(
                [v_ref[rows_of[1], lanes_of[i]], k_rise[i, 1] * whole[i, 0]], axis=1
            )
            second[i] = mm(inverse[i, 1], start - late_part[i][:HALF]).astype(BF16)
        for i in some:
            stop = jnp.concatenate(
                [k_fall[i, 0] * whole[i, 1], k_fall[i, 1]], axis=0
            ).astype(BF16)
            maps = mm(jnp.concatenate([first[i], second[i]], axis=0), stop, ((0,), (0,)))
            move = jnp.where(diagonal, whole[i, 0] * whole[i, 1], 0.0) - maps[128:]
            z_ref[i, 0:128] = move.astype(BF16)
            z_ref[i, 128:256] = maps[:128].astype(BF16)

            @pl.when(p != 2 * i)
            def _():
                to_owner(i).start()

        for i in some:
            lanes = lanes_of[i]
            u = 2 * (i - pair)
            out = [
                mm(attend_ref[u], first[i]),
                late_part[i][HALF:] + mm(attend_ref[u + 1], second[i]),
            ]
            for c in range(2):
                o_ref[rows_of[c], lanes] = out[c][:, :128]
            r_ref[rows_of[0], lanes] = (q_rise[i, 0] - out[0][:, 128:]).astype(BF16)
            r_ref[rows_of[1], lanes] = (
                q_rise[i, 1] * whole[i, 0] - out[1][:, 128:]
            ).astype(BF16)

    def to_group(k, at):
        return pltpu.make_async_remote_copy(
            src_ref=total.at[at],
            dst_ref=zall.at[rank, at],
            send_sem=b_send.at[k],
            recv_sem=b_recv.at[rank],
            device_id={"seq": (group * GROUP + k) * PLANE + p},
            device_id_type=MESH,
        )

    def from_group(k, at):
        return pltpu.make_async_remote_copy(
            src_ref=total.at[at],
            dst_ref=zall.at[k, at],
            send_sem=b_send.at[k],
            recv_sem=b_recv.at[k],
            device_id={"seq": s},
            device_id_type=MESH,
        )

    def to_next(k):
        target = jnp.where(rank == 0, 2 * GROUP - 1 - k, GROUP + k)
        return pltpu.make_async_remote_copy(
            src_ref=chain,
            dst_ref=held,
            send_sem=f_sem.at[k],
            recv_sem=f_sem.at[2],
            device_id={"seq": target * PLANE + p},
            device_id_type=MESH,
        )

    def prefix_to(q):
        return pltpu.make_async_remote_copy(
            src_ref=pre.at[q],
            dst_ref=lead.at[y],
            send_sem=g_send.at[q],
            recv_sem=g_recv.at[y],
            device_id={"seq": base + q},
            device_id_type=MESH,
        )

    def entry_to(q):
        return pltpu.make_async_remote_copy(
            src_ref=entry,
            dst_ref=state.at[y],
            send_sem=c_send.at[q],
            recv_sem=c_recv.at[y],
            device_id={"seq": base + q},
            device_id_type=MESH,
        )

    def landed(ref, sem, k):
        pltpu.make_async_remote_copy(
            src_ref=ref.at[k],
            dst_ref=ref.at[k],
            send_sem=sem.at[k],
            recv_sem=sem.at[k],
            device_id={"seq": s},
            device_id_type=MESH,
        ).wait_recv()

    everything, shift_only = pl.ds(0, 256), pl.ds(128, 128)
    half_plane = PLANE // 2

    def join(one, two):
        step = mm(one, two[:128])
        return jnp.concatenate(
            [step[:128].astype(BF16), (step[128:] + two[128:].astype(F32)).astype(BF16)], axis=0
        )

    def moved(state_in, both):
        return (mm(state_in, both[0:128]) + both[128:256].astype(F32)).astype(BF16)

    def group_copies(act):
        for k in range(GROUP):
            @pl.when(jnp.logical_and(jnp.logical_and(group == 0, rank == 0), k > 0))
            def _():
                act(to_group(k, shift_only))

            wanted = k > rank
            if k == 0:
                wanted = jnp.logical_and(group == 0, rank > 0)
            else:
                wanted = jnp.logical_and(
                    wanted, jnp.logical_or(group == 1, rank > 0)
                )

            @pl.when(wanted)
            def _():
                act(to_group(k, everything))

    @pl.when(owner)
    def _():
        zin[p] = z_ref[y]
        for k in range(PLANE):

            @pl.when(p != k)
            def _():
                landed(zin, a_recv, k)

        one, two = zin[0], zin[half_plane]
        later = {}
        for k in range(1, half_plane):
            pre[k], later[half_plane + k] = one, two
            one, two = join(one, zin[k]), join(two, zin[half_plane + k])
        pre[half_plane] = one
        whole_map = join(one, two)
        total[...] = whole_map
        group_copies(lambda copy: copy.start())
        zall[rank] = whole_map
        for k in range(half_plane + 1, PLANE):
            pre[k] = join(one, later[k])
        for q in range(1, PLANE):

            @pl.when(p != q)
            def _():
                prefix_to(q).start()

        @pl.when(p > 0)
        def _():
            lead[y] = pre[p]

        @pl.when(group == 0)
        def _():
            chain[...] = jnp.zeros_like(chain)
            entry[...] = jnp.zeros_like(entry)
            for k in range(GROUP):
                needed = jnp.logical_or(feeds, k < rank)
                if k == 0:

                    @pl.when(rank > 0)
                    def _():
                        from_group(0, shift_only).wait_recv()

                else:

                    @pl.when(jnp.logical_and(needed, rank != k))
                    def _():
                        from_group(k, everything).wait_recv()

                @pl.when(rank == k)
                def _():
                    entry[...] = chain[...]

                @pl.when(needed)
                def _():
                    if k == 0:
                        chain[...] = zall[0, 128:256]
                    else:
                        chain[...] = moved(chain[...], zall[k])

            @pl.when(feeds)
            def _():
                for k in range(2):
                    to_next(k).start()

        @pl.when(group == 1)
        def _():
            for k in range(GROUP - 1):

                @pl.when(k < rank)
                def _():
                    from_group(k, everything).wait_recv()
                    if k == 0:
                        link[...] = zall[0]
                    else:
                        link[...] = join(link[...], zall[k])

            to_next(0).wait_recv()

            @pl.when(rank == 0)
            def _():
                entry[...] = held[...]

            @pl.when(rank > 0)
            def _():
                entry[...] = moved(held[...], link[...])

        for q in range(PLANE):

            @pl.when(p != q)
            def _():
                entry_to(q).start()

        state[y] = entry[...]

    @pl.when(p > 0)
    def _():
        for i in range(heads):

            @pl.when(p != 2 * i)
            def _():
                landed(lead, g_recv, i)

        for i in range(heads):
            lanes = lanes_of[i]
            both = mm(r_ref[:, lanes], lead[i], ((1,), (1,)))
            o_ref[:, lanes] = o_ref[:, lanes] + both[:, 128:]
            r_ref[:, lanes] = both[:, :128].astype(BF16)

    def states_in(i):
        @pl.when(p != 2 * i)
        def _():
            landed(state, c_recv, i)

    for i in range(heads):
        states_in(i)
        lanes = lanes_of[i]
        attended = o_ref[:, lanes] + mm(r_ref[:, lanes], state[i], ((1,), (1,)))
        scale = lax.rsqrt(jnp.mean(attended * attended, axis=1, keepdims=True) + 1e-05)
        normed[:, lanes] = (attended * scale * gain_ref[...] * gate_ref[:, lanes]).astype(BF16)
    loads[8].wait()


    def partial(to):
        at = pl.ds(pl.multiple_of(to * rows, 16), rows)
        return jnp.dot(normed[at, :], ow_ref[...], preferred_element_type=F32)

    def pass_on(k, src, dst, target):
        return pltpu.make_async_remote_copy(
            src_ref=src,
            dst_ref=dst,
            send_sem=d_send.at[k],
            recv_sem=d_recv.at[k],
            device_id={"head": target},
            device_id_type=MESH,
        )

    top, low = pl.ds(0, half), pl.ds(half, half)
    part[0] = partial(far).astype(BF16)
    far_right = pass_on(0, part.at[0, top], inbox.at[0, top], right)
    far_left = pass_on(1, part.at[0, low], inbox.at[0, low], left)
    far_right.start()
    far_left.start()
    sums[0] = partial(right)
    part[1, low] = sums[0, low].astype(BF16)
    right_low = pass_on(2, part.at[1, low], inbox.at[1, low], right)
    right_low.start()
    sums[1] = partial(left)
    part[2, top] = sums[1, top].astype(BF16)
    left_top = pass_on(3, part.at[2, top], inbox.at[2, top], left)
    left_top.start()
    far_right.wait_recv()
    part[1, top] = (sums[0, top] + inbox[0, top].astype(F32)).astype(BF16)
    right_top = pass_on(4, part.at[1, top], inbox.at[1, top], right)
    right_top.start()
    far_left.wait_recv()
    part[2, low] = (sums[1, low] + inbox[0, low].astype(F32)).astype(BF16)
    left_low = pass_on(5, part.at[2, low], inbox.at[2, low], left)
    left_low.start()
    own = partial(h)
    right_low.wait_recv()
    left_top.wait_recv()
    right_top.wait_recv()
    left_low.wait_recv()
    out_ref[...] = (own + inbox[1].astype(F32) + inbox[2].astype(F32)).astype(BF16)

    for copy in (far_right, far_left, right_low, left_top, right_top, left_low):
        copy.wait_send()
    for n in (0, 1, 4, 5):
        moves[n].wait_send()

    for head in (0, 2, 3):
        each_edge(head, lambda copy: copy.wait_send())

    for i in range(heads):

        @pl.when(p != 2 * i)
        def _():
            to_owner(i).wait_send()

    @pl.when(owner)
    def _():
        group_copies(lambda copy: copy.wait_send())

        @pl.when(feeds)
        def _():
            for k in range(2):
                to_next(k).wait_send()

        for q in range(PLANE):

            @pl.when(p != q)
            def _():
                if q > 0:
                    prefix_to(q).wait_send()
                entry_to(q).wait_send()


def layer(depth, x, w, down, gdown, beta, up, gup, conv, dlog, bias, span, gain, ow):
    vmem = pl.BlockSpec(memory_space=pltpu.VMEM)
    smem = pl.BlockSpec(memory_space=pltpu.SMEM)
    hbm = pl.BlockSpec(memory_space=pl.ANY)
    rows, model = x.shape
    count, width = 4 * rows, w.shape[2]
    heads = width // 128
    dma = pltpu.SemaphoreType.DMA
    return pl.pallas_call(
        functools.partial(kernel, depth),
        name="layer",
        out_shape=jax.ShapeDtypeStruct((rows, model), BF16),
        in_specs=[hbm] * 5 + [vmem] * 3 + [smem, vmem, hbm, vmem, hbm],
        out_specs=vmem,
        scratch_shapes=[
            pltpu.VMEM((count + HALO, model), BF16),
            pltpu.VMEM(w.shape, BF16),
            pltpu.VMEM((model, 256), BF16),
            pltpu.VMEM(beta.shape, BF16),
            pltpu.VMEM(span.shape, BF16),
            pltpu.VMEM(ow.shape, BF16),
            pltpu.VMEM((3, HALO + count, width), F32),
            pltpu.VMEM((count, width), F32),
            pltpu.VMEM((count, heads), F32),
            pltpu.VMEM((count, width), F32),
            pltpu.VMEM((count, width), F32),
            pltpu.VMEM((count, width), F32),
            pltpu.VMEM((2, (len(LEVELS) + 2) * HALF, width), F32),
            pltpu.VMEM((count, width), F32),
            pltpu.VMEM((count, width), BF16),
            pltpu.VMEM((count, width), F32),
            pltpu.VMEM((heads, 256, 128), BF16),
            pltpu.VMEM((4, len(LEVELS), HALF, HALF), BF16),
            pltpu.VMEM((4, HALF, HALF), BF16),
            pltpu.VMEM((PLANE, 256, 128), BF16),
            pltpu.VMEM((PLANE, 256, 128), BF16),
            pltpu.VMEM((256, 128), BF16),
            pltpu.VMEM((GROUP, 256, 128), BF16),
            pltpu.VMEM((128, 128), BF16),
            pltpu.VMEM((256, 128), BF16),
            pltpu.VMEM((128, 128), BF16),
            pltpu.VMEM((128, 128), BF16),
            pltpu.VMEM((heads, 256, 128), BF16),
            pltpu.VMEM((heads, 128, 128), BF16),
            pltpu.VMEM((count, width), BF16),
            pltpu.VMEM((3, rows, model), BF16),
            pltpu.VMEM((2, rows, model), F32),
            pltpu.VMEM((3, rows, model), BF16),
            dma((9,)), dma((6,)), dma((6,)), dma((3,)), dma((3,)), dma((PLANE,)), dma((heads,)),
            dma((heads,)), dma((PLANE,)), dma((GROUP,)), dma((GROUP,)),
            dma((PLANE,)), dma((heads,)), dma((6,)), dma((6,)),
        ],
        compiler_params=pltpu.CompilerParams(
            collective_id=0, has_side_effects=True, vmem_limit_bytes=56 << 20
        ),
    )(x, w, down, gdown, beta, up, gup, conv, dlog, bias, span, gain, ow)


def solution(mesh):
    seq_size = mesh.shape["seq"]
    span = span_matrix()

    def shards(
        hidden_in, qkv_weight, conv_weight, decay_log, dt_bias, decay_down, decay_up,
        beta_weight, gate_down, gate_up, norm_gain, out_weight,
    ):
        return layer(
            seq_size // PLANE,
            hidden_in,
            jnp.transpose(qkv_weight, (1, 0, 2)),
            decay_down,
            gate_down,
            beta_weight.T,
            decay_up,
            gate_up,
            conv_weight,
            decay_log,
            dt_bias.reshape(1, -1),
            jnp.asarray(span, BF16),
            norm_gain.reshape(1, -1),
            out_weight,
        )

    rows = P(("seq", "head"), None)
    return jax.shard_map(
        shards,
        mesh=mesh,
        in_specs=(
            rows, P(None, None, "head"), P(None, None, "head"), P("head"), P("head"), P(),
            P(None, "head"), P(None, "head"), P(), P(None, "head"), P(), P("head", None),
        ),
        out_specs=rows,
        check_vma=False,
    )
```

```python
import functools

import jax
import jax.numpy as jnp
import numpy as np
from jax import lax
from jax.experimental import pallas as pl
from jax.experimental.pallas import tpu as pltpu
from jax.sharding import PartitionSpec as P

F32 = jnp.float32
BF16 = jnp.bfloat16
MESH = pl.DeviceIdType.MESH

HALO = 16
EDGE = 8
HALF = 128
LEVELS = (1, 2, 4, 8, 16, 32, 64)
PLANE = 8
GROUP = 4
FAR_FIRST = (4, 5, 2, 3, 6, 7, 1)
ENTRIES = (7, 4, 2, 3, 6, 1)


def span_matrix():
    r, i = np.arange(HALF)[:, None], np.arange(HALF)[None, :]
    rows = []
    for size in LEVELS:
        middle = (r // (2 * size)) * 2 * size + size - 1
        late = (r % (2 * size)) >= size
        rows.append(np.where(late, (i > middle) & (i <= r), (i > r) & (i <= middle)))
    rows.append(i <= r)
    rows.append(i > r)
    spans = np.concatenate(rows, axis=0)
    return np.concatenate([spans, spans], axis=1).astype(np.float32)


def mm(a, b, dims=((1,), (0,))):
    return lax.dot_general(
        a.astype(BF16), b.astype(BF16), (dims, ((), ())), preferred_element_type=F32
    )


def sigmoid(v):
    return 1.0 / (1.0 + jnp.exp(-v))


def kernel(
    depth, x_hbm, w_hbm, down_hbm, gdown_hbm, beta_hbm, up_hbm, gup_hbm, conv_hbm, dlog_hbm,
    bias_hbm, span_hbm, gain_hbm, ow_hbm, out_ref,
    x_ref, w_ref, dg_ref, beta_ref, up_ref, gup_ref, conv_ref, dlog_ref, bias_ref, span_ref,
    gain_ref, ow_ref,
    proj_ref, fade_ref, strength_ref, q_ref, k_ref, v_ref, e_ref, o_ref, r_ref, gate_ref, z_ref,
    mix_ref, attend_ref, zin, pre, total, zall, chain, link, held, entry, lead, state, normed, part, sums, inbox,
    l_sem, x_send, x_recv, e_sem, f_sem, g_send, g_recv,
    a_send, a_recv, b_send, b_recv, c_send, c_recv, d_send, d_recv,
):
    s = lax.axis_index("seq")
    h = lax.axis_index("head")
    z = lax.div(s, PLANE)
    p = lax.rem(s, PLANE)
    y, core = lax.div(p, 2), lax.rem(p, 2)
    base = z * PLANE
    right, left, far = lax.rem(h + 1, 4), lax.rem(h + 3, 4), lax.rem(h + 2, 4)
    owner = core == 0
    group, rank = lax.div(z, GROUP), lax.rem(z, GROUP)
    feeds = jnp.logical_and(group == 0, jnp.logical_or(rank == 0, rank == GROUP - 1))
    has_next = s < depth * PLANE - 1
    edge_from = jnp.where(h == 1, 2, h)
    rows = x_hbm.shape[0]
    half = rows // 2
    count = 4 * rows
    width = w_ref.shape[2]
    heads = width // 128

    barrier = pltpu.get_barrier_semaphore()
    pl.semaphore_signal(barrier, 1, device_id={"head": right}, device_id_type=MESH)
    pl.semaphore_signal(barrier, 1, device_id={"head": left}, device_id_type=MESH)

    @pl.when(s > 0)
    def _():
        pl.semaphore_signal(
            barrier, 1, device_id={"seq": s - 1, "head": edge_from}, device_id_type=MESH
        )

    for d in range(1, PLANE):
        q = lax.rem(p + d, PLANE)

        @pl.when(jnp.logical_or(owner, lax.rem(q, 2) == 0))
        def _():
            pl.semaphore_signal(barrier, 1, device_id={"seq": base + q}, device_id_type=MESH)

    @pl.when(core == 1)
    def _():
        pl.semaphore_signal(
            barrier, 1, device_id={"seq": base + lax.rem(p + 2, PLANE)}, device_id_type=MESH
        )

    @pl.when(owner)
    def _():
        for d in range(1, GROUP):
            other = group * GROUP + lax.rem(rank + d, GROUP)
            pl.semaphore_signal(
                barrier, 1, device_id={"seq": other * PLANE + p}, device_id_type=MESH
            )

        @pl.when(group == 1)
        def _():
            feeder = jnp.where(rank < 2, GROUP - 1, 0)
            pl.semaphore_signal(
                barrier, 1, device_id={"seq": feeder * PLANE + p}, device_id_type=MESH
            )

    greeted = (
        2
        + jnp.where(owner, PLANE - 1 + GROUP - 1, PLANE // 2 + 1)
        + jnp.where(jnp.logical_and(owner, feeds), 2, 0)
        + jnp.where(has_next, jnp.where(h == 2, 2, jnp.where(h == 1, 0, 1)), 0)
    )

    loads = [
        pltpu.make_async_copy(src, dst, l_sem.at[k])
        for k, (src, dst) in enumerate(
            [
                (x_hbm, x_ref.at[pl.ds(0, rows)]),
                (w_hbm.at[0], w_ref.at[0]),
                (w_hbm.at[1], w_ref.at[1]),
                (w_hbm.at[2], w_ref.at[2]),
                (down_hbm, dg_ref.at[:, pl.ds(0, 128)]),
                (gdown_hbm, dg_ref.at[:, pl.ds(128, 128)]),
                (beta_hbm, beta_ref),
                (up_hbm, up_ref),
                (gup_hbm, gup_ref),
                (conv_hbm, conv_ref),
                (dlog_hbm, dlog_ref),
                (bias_hbm, bias_ref),
                (gain_hbm, gain_ref),
                (span_hbm, span_ref),
                (ow_hbm, ow_ref),
            ]
        )
    ]
    for load in loads:
        load.start()
    x_ref[count + EDGE :, :] = jnp.zeros((HALO - EDGE, x_ref.shape[1]), BF16)

    @pl.when(s == 0)
    def _():
        x_ref[count : count + EDGE, :] = jnp.zeros((EDGE, x_ref.shape[1]), BF16)

    pl.semaphore_wait(barrier, greeted)

    def piece(src, slot, half_at, target, k):
        return pltpu.make_async_remote_copy(
            src_ref=src,
            dst_ref=x_ref.at[pl.ds(slot * rows + half_at * half, half)],
            send_sem=x_send.at[k],
            recv_sem=x_recv.at[k],
            device_id={"head": target},
            device_id_type=MESH,
        )

    def rows_at(slot, half_at):
        return x_ref.at[pl.ds(slot * rows + half_at * half, half)]

    loads[0].wait()
    mine = [rows_at(0, 0), rows_at(0, 1)]
    moves = [
        piece(mine[0], 1, 0, right, 0),
        piece(mine[1], 2, 1, left, 1),
        piece(mine[1], 1, 1, right, 2),
        piece(mine[0], 2, 0, left, 3),
        piece(rows_at(1, 0), 3, 0, right, 4),
        piece(rows_at(2, 1), 3, 1, left, 5),
    ]
    for move in moves[:4]:
        move.start()

    def edge(k, src, target):
        return pltpu.make_async_remote_copy(
            src_ref=src,
            dst_ref=x_ref.at[pl.ds(count, EDGE)],
            send_sem=e_sem.at[k],
            recv_sem=e_sem.at[2],
            device_id={"seq": s + 1, "head": target},
            device_id_type=MESH,
        )

    last = pl.ds(rows - EDGE, EDGE)
    edges = {
        3: [edge(0, x_ref.at[last], 3)],
        0: [edge(0, x_ref.at[pl.ds(2 * rows - EDGE, EDGE)], 0)],
        2: [
            edge(0, x_ref.at[pl.ds(3 * rows - EDGE, EDGE)], 2),
            edge(1, x_ref.at[pl.ds(3 * rows - EDGE, EDGE)], 1),
        ],
    }

    def each_edge(head, act):
        @pl.when(jnp.logical_and(h == head, has_next))
        def _():
            for copy in edges[head]:
                act(copy)

    each_edge(3, lambda copy: copy.start())
    moves[0].wait_recv()
    moves[2].wait_send()
    moves[4].start()
    moves[1].wait_recv()
    moves[3].wait_send()
    moves[5].start()
    each_edge(2, lambda copy: copy.start())
    for load in loads[1:14]:
        load.wait()
    moves[2].wait_recv()
    each_edge(0, lambda copy: copy.start())
    moves[3].wait_recv()

    rate = jnp.concatenate(
        [jnp.exp(jnp.full((1, 128), dlog_ref[i], F32)) for i in range(heads)], axis=1
    )

    def project(first, slots):
        size = len(slots) * rows
        at = [pl.ds(pl.multiple_of(slot * rows, 16), rows) for slot in slots]
        some = x_ref[first : first + size, :]
        both = jnp.dot(some, dg_ref[...], preferred_element_type=F32).astype(BF16)
        force = sigmoid(
            lax.dot_general(
                some, beta_ref[...], (((1,), (1,)), ((), ())), preferred_element_type=F32
            )
        )
        raw = jnp.dot(both[:, 0:128], up_ref[...], preferred_element_type=F32) + bias_ref[...]
        soft = jnp.maximum(raw, 0.0) + jnp.log1p(jnp.exp(-jnp.abs(raw)))
        log_decay = -rate * soft
        gate = sigmoid(jnp.dot(both[:, 128:256], gup_ref[...], preferred_element_type=F32))
        for n, where in enumerate(at):
            own = slice(n * rows, (n + 1) * rows)
            fade_ref[where, :] = log_decay[own]
            gate_ref[where, :] = gate[own]
            strength_ref[where, :] = force[own]

    def project_qkv(c, first, slots, tail):
        size = len(slots) * rows
        some = x_ref[first : first + size + tail, :]
        got = jnp.dot(some, w_ref[c], preferred_element_type=F32).astype(BF16).astype(F32)
        for n, slot in enumerate(slots):
            at = pl.ds(pl.multiple_of(HALO + slot * rows, 16), rows)
            proj_ref[c, at, :] = got[n * rows : (n + 1) * rows]
        if tail:
            proj_ref[c, HALO - EDGE : HALO, :] = got[size : size + EDGE]

    near = (h, left, right)
    project(0, near)
    for c in range(3):
        project_qkv(c, 0, near, 0)
    moves[4].wait_recv()
    moves[5].wait_recv()

    @pl.when(s > 0)
    def _():
        edges[0][0].wait_recv()

    def decays(c):
        piece_of = fade_ref[c * HALF : (c + 1) * HALF, :]
        top = piece_of.astype(BF16)
        rest = (piece_of - top.astype(F32)).astype(BF16)
        e_ref[c] = jnp.exp(
            jnp.dot(
                span_ref[...], jnp.concatenate([top, rest], axis=0), preferred_element_type=F32
            )
        )

    def convolve(c):
        target = (q_ref, k_ref, v_ref)[c]
        taps = conv_ref[c].astype(F32)
        mixed = proj_ref[c, pl.ds(HALO - 3, count), :] * taps[0:1]
        for i in range(1, 4):
            mixed = mixed + proj_ref[c, pl.ds(HALO - 3 + i, count), :] * taps[i : i + 1]
        mixed = (mixed * sigmoid(mixed)).astype(BF16).astype(F32)
        if c == 2:
            target[...] = mixed
            return
        for i in range(heads):
            lanes = slice(i * 128, (i + 1) * 128)
            u = mixed[:, lanes]
            scale = lax.rsqrt(jnp.sum(u * u, axis=1, keepdims=True) + 1e-06)
            if c == 0:
                scale = scale * (128**-0.5)
            target[:, lanes] = u * scale

    project(3 * rows, (far,))
    project_qkv(1, 3 * rows, (far,), HALO)
    decays(0)
    project_qkv(0, 3 * rows, (far,), HALO)
    convolve(1)
    decays(1)
    project_qkv(2, 3 * rows, (far,), HALO)
    convolve(0)
    convolve(2)
    beta = strength_ref[...]

    t = lax.broadcasted_iota(jnp.int32, (HALF, HALF), 0)
    j = lax.broadcasted_iota(jnp.int32, (HALF, HALF), 1)
    row = lax.broadcasted_iota(jnp.int32, (HALF, 128), 0)
    masks = [
        ((t ^ j) >= size) & ((t ^ j) < 2 * size) & (t > j) for size in LEVELS
    ]
    diagonal = t == j

    lanes_of = [slice(i * 128, (i + 1) * 128) for i in range(heads)]
    rows_of = [slice(c * HALF, (c + 1) * HALF) for c in range(2)]

    def to_owner(i):
        return pltpu.make_async_remote_copy(
            src_ref=z_ref.at[i],
            dst_ref=zin.at[p],
            send_sem=a_send.at[i],
            recv_sem=a_recv.at[p],
            device_id={"seq": base + 2 * i},
            device_id_type=MESH,
        )

    strength, inverse = {}, {}

    def unit_of(i, c):
        return 2 * i + c

    def mix(i, c, n, attend):
        kc, qc = k_ref[rows_of[c], lanes_of[i]], q_ref[rows_of[c], lanes_of[i]]
        if n == 0:
            strength[i, c] = jnp.broadcast_to(beta[rows_of[c], i : i + 1], (HALF, 128))
            own = jnp.sum(qc * kc, axis=1, keepdims=True) * strength[i, c]
            attend = jnp.where(diagonal, own, 0.0)
        size = LEVELS[n]
        fade = e_ref[c, n * HALF : (n + 1) * HALF, lanes_of[i]]
        late = (row & size) != 0
        kx = (kc * fade * jnp.where(late, 1.0, strength[i, c])).astype(BF16)
        qx = (qc * fade).astype(BF16)
        both = mm(jnp.concatenate([kx, qx], axis=0), kx, ((1,), (1,)))
        mix_ref[unit_of(i, c), n] = jnp.where(masks[n], both[:HALF], 0.0).astype(BF16)
        attend = jnp.where(masks[n], both[HALF:], attend)
        if n == len(LEVELS) - 1:
            attend_ref[unit_of(i, c)] = attend.astype(BF16)
        return attend

    def mixes(some):
        for i in some:
            for c in range(2):
                attend = None
                for n in range(len(LEVELS)):
                    attend = mix(i, c, n, attend)
                    yield

    def doublings(some):
        units = [(i, c) for i in some for c in range(2)]
        for unit in units:
            inverse[unit] = jnp.where(diagonal, 1.0, 0.0) - mix_ref[unit_of(*unit), 0].astype(F32)
        for n in range(1, len(LEVELS)):
            own = {unit: inverse[unit].astype(BF16) for unit in units}
            left_part = {}
            for unit in units:
                left_part[unit] = mm(own[unit], mix_ref[unit_of(*unit), n]).astype(BF16)
            yield
            for unit in units:
                inverse[unit] = inverse[unit] - mm(left_part[unit], own[unit])
            yield
        for unit in units:
            inverse[unit] = inverse[unit].astype(BF16)

    parts = {}

    def maps_of(some):
        n = len(LEVELS)
        units = [(i, c) for i in some for c in range(2)]
        rise = {u: e_ref[u[1], n * HALF : (n + 1) * HALF, lanes_of[u[0]]] for u in units}
        fall = {u: e_ref[u[1], (n + 1) * HALF : (n + 2) * HALF, lanes_of[u[0]]] for u in units}
        whole = {u: rise[u][HALF - 1 : HALF] for u in units}
        k_rise = {u: k_ref[rows_of[u[1]], lanes_of[u[0]]] * rise[u] for u in units}
        q_rise = {u: q_ref[rows_of[u[1]], lanes_of[u[0]]] * rise[u] for u in units}
        k_fall = {
            u: k_ref[rows_of[u[1]], lanes_of[u[0]]] * fall[u] * strength[u] for u in units
        }
        cross, first, second = {}, {}, {}
        for i in some:
            cross[i] = mm(
                jnp.concatenate([k_rise[i, 1], q_rise[i, 1]], axis=0), k_fall[i, 0], ((1,), (1,))
            ).astype(BF16)
        for i in some:
            first[i] = mm(
                inverse[i, 0],
                jnp.concatenate([v_ref[rows_of[0], lanes_of[i]], k_rise[i, 0]], axis=1),
            ).astype(BF16)
        yield
        late_part = {i: mm(cross[i], first[i]) for i in some}
        yield
        for i in some:
            start = jnp.concatenate(
                [v_ref[rows_of[1], lanes_of[i]], k_rise[i, 1] * whole[i, 0]], axis=1
            )
            second[i] = mm(inverse[i, 1], start - late_part[i][:HALF]).astype(BF16)
        yield
        for i in some:
            stop = jnp.concatenate(
                [k_fall[i, 0] * whole[i, 1], k_fall[i, 1]], axis=0
            ).astype(BF16)
            maps = mm(jnp.concatenate([first[i], second[i]], axis=0), stop, ((0,), (0,)))
            move = jnp.where(diagonal, whole[i, 0] * whole[i, 1], 0.0) - maps[128:]
            z_ref[i, 0:128] = move.astype(BF16)
            z_ref[i, 128:256] = maps[:128].astype(BF16)
            parts[i] = (q_rise, whole, first, second, late_part)

    def outputs_of(some):
        for i in some:
            q_rise, whole, first, second, late_part = parts[i]
            lanes = lanes_of[i]
            out = [
                mm(attend_ref[unit_of(i, 0)], first[i]),
                late_part[i][HALF:] + mm(attend_ref[unit_of(i, 1)], second[i]),
            ]
            for c in range(2):
                o_ref[rows_of[c], lanes] = out[c][:, :128]
            r_ref[rows_of[0], lanes] = (q_rise[i, 0] - out[0][:, 128:]).astype(BF16)
            r_ref[rows_of[1], lanes] = (
                q_rise[i, 1] * whole[i, 0] - out[1][:, 128:]
            ).astype(BF16)
            yield

    def send_maps(some):
        for i in some:

            @pl.when(p != 2 * i)
            def _():
                to_owner(i).start()

    def together(main, other, share):
        for _ in main:
            for _ in range(share):
                next(other, None)

    def finish(*works):
        for work in works:
            for _ in work:
                pass

    early, late_heads = range(0, heads, 2), range(1, heads, 2)
    finish(mixes(early))
    other = mixes(late_heads)
    together(doublings(early), other, 3)
    finish(other)
    other = doublings(late_heads)
    together(maps_of(early), other, 1)
    send_maps(early)
    outputs = outputs_of(early)
    together(other, outputs, 1)
    finish(outputs, maps_of(late_heads))
    send_maps(late_heads)
    finish(outputs_of(late_heads))

    def to_group(k, at):
        return pltpu.make_async_remote_copy(
            src_ref=total.at[at],
            dst_ref=zall.at[rank, at],
            send_sem=b_send.at[k],
            recv_sem=b_recv.at[rank],
            device_id={"seq": (group * GROUP + k) * PLANE + p},
            device_id_type=MESH,
        )

    def from_group(k, at):
        return pltpu.make_async_remote_copy(
            src_ref=total.at[at],
            dst_ref=zall.at[k, at],
            send_sem=b_send.at[k],
            recv_sem=b_recv.at[k],
            device_id={"seq": s},
            device_id_type=MESH,
        )

    def to_next(k):
        target = jnp.where(rank == 0, 2 * GROUP - 1 - k, GROUP + k)
        return pltpu.make_async_remote_copy(
            src_ref=chain,
            dst_ref=held,
            send_sem=f_sem.at[k],
            recv_sem=f_sem.at[2],
            device_id={"seq": target * PLANE + p},
            device_id_type=MESH,
        )

    def prefix_to(q):
        return pltpu.make_async_remote_copy(
            src_ref=pre.at[q],
            dst_ref=lead.at[y],
            send_sem=g_send.at[q],
            recv_sem=g_recv.at[y],
            device_id={"seq": base + q},
            device_id_type=MESH,
        )

    def entry_to(q):
        return pltpu.make_async_remote_copy(
            src_ref=entry,
            dst_ref=state.at[y],
            send_sem=c_send.at[q],
            recv_sem=c_recv.at[y],
            device_id={"seq": base + q},
            device_id_type=MESH,
        )

    def landed(ref, sem, k):
        pltpu.make_async_remote_copy(
            src_ref=ref.at[k],
            dst_ref=ref.at[k],
            send_sem=sem.at[k],
            recv_sem=sem.at[k],
            device_id={"seq": s},
            device_id_type=MESH,
        ).wait_recv()

    everything, shift_only = pl.ds(0, 256), pl.ds(128, 128)
    half_plane = PLANE // 2

    def join(one, two):
        step = mm(one, two[:128])
        return jnp.concatenate(
            [step[:128].astype(BF16), (step[128:] + two[128:].astype(F32)).astype(BF16)], axis=0
        )

    def moved(state_in, both):
        return (mm(state_in, both[0:128]) + both[128:256].astype(F32)).astype(BF16)

    def group_copies(act):
        for k in range(GROUP):
            @pl.when(jnp.logical_and(jnp.logical_and(group == 0, rank == 0), k > 0))
            def _():
                act(to_group(k, shift_only))

            wanted = k > rank
            if k == 0:
                wanted = jnp.logical_and(group == 0, rank > 0)
            else:
                wanted = jnp.logical_and(
                    wanted, jnp.logical_or(group == 1, rank > 0)
                )

            @pl.when(wanted)
            def _():
                act(to_group(k, everything))

    @pl.when(owner)
    def _():
        zin[p] = z_ref[y]
        for k in range(PLANE):

            @pl.when(p != k)
            def _():
                landed(zin, a_recv, k)

        one, two = zin[0], zin[half_plane]
        later = {}
        for k in range(1, half_plane):
            pre[k], later[half_plane + k] = one, two
            one, two = join(one, zin[k]), join(two, zin[half_plane + k])
        pre[half_plane] = one
        whole_map = join(one, two)
        total[...] = whole_map
        group_copies(lambda copy: copy.start())
        zall[rank] = whole_map
        for k in range(half_plane + 1, PLANE):
            pre[k] = join(one, later[k])
        for d in FAR_FIRST:
            q = lax.rem(p + d, PLANE)

            @pl.when(q > 0)
            def _():
                prefix_to(q).start()

        @pl.when(p > 0)
        def _():
            lead[y] = pre[p]

        @pl.when(group == 0)
        def _():
            chain[...] = jnp.zeros_like(chain)
            entry[...] = jnp.zeros_like(entry)
            for k in range(GROUP):
                needed = jnp.logical_or(feeds, k < rank)
                if k == 0:

                    @pl.when(rank > 0)
                    def _():
                        from_group(0, shift_only).wait_recv()

                else:

                    @pl.when(jnp.logical_and(needed, rank != k))
                    def _():
                        from_group(k, everything).wait_recv()

                @pl.when(rank == k)
                def _():
                    entry[...] = chain[...]

                @pl.when(needed)
                def _():
                    if k == 0:
                        chain[...] = zall[0, 128:256]
                    else:
                        chain[...] = moved(chain[...], zall[k])

            @pl.when(feeds)
            def _():
                for k in range(2):
                    to_next(k).start()

        @pl.when(group == 1)
        def _():
            for k in range(GROUP - 1):

                @pl.when(k < rank)
                def _():
                    from_group(k, everything).wait_recv()
                    if k == 0:
                        link[...] = zall[0]
                    else:
                        link[...] = join(link[...], zall[k])

            to_next(0).wait_recv()

            @pl.when(rank == 0)
            def _():
                entry[...] = held[...]

            @pl.when(rank > 0)
            def _():
                entry[...] = moved(held[...], link[...])

        @pl.when(z > 0)
        def _():
            for d in ENTRIES:
                entry_to(lax.rem(p + d, PLANE)).start()

            state[y] = entry[...]

    @pl.when(z == 0)
    def _():
        state[...] = jnp.zeros_like(state)

    @pl.when(p > 0)
    def _():
        for i in range(heads):

            @pl.when(p != 2 * i)
            def _():
                landed(lead, g_recv, i)

        for i in range(heads):
            lanes = lanes_of[i]
            both = mm(r_ref[:, lanes], lead[i], ((1,), (1,)))
            o_ref[:, lanes] = o_ref[:, lanes] + both[:, 128:]
            r_ref[:, lanes] = both[:, :128].astype(BF16)

    after_own = lax.rem(y + 1, heads)
    passes_on = jnp.logical_and(core == 1, z > 0)
    passed = pltpu.make_async_remote_copy(
        src_ref=state.at[after_own],
        dst_ref=state.at[after_own],
        send_sem=c_send.at[0],
        recv_sem=c_recv.at[after_own],
        device_id={"seq": base + lax.rem(p + PLANE - 2, PLANE)},
        device_id_type=MESH,
    )
    for d in (1, 0, 3, 2):
        i = lax.rem(y + d, heads)

        @pl.when(jnp.logical_and(p != 2 * i, z > 0))
        def _():
            landed(state, c_recv, i)

        if d == 1:

            @pl.when(passes_on)
            def _():
                passed.start()

        lanes = pl.ds(pl.multiple_of(i * 128, 128), 128)
        attended = o_ref[:, lanes] + mm(r_ref[:, lanes], state[i], ((1,), (1,)))
        scale = lax.rsqrt(jnp.mean(attended * attended, axis=1, keepdims=True) + 1e-05)
        normed[:, lanes] = (attended * scale * gain_ref[...] * gate_ref[:, lanes]).astype(BF16)
    loads[14].wait()


    def partial(to):
        at = pl.ds(pl.multiple_of(to * rows, 16), rows)
        return jnp.dot(normed[at, :], ow_ref[...], preferred_element_type=F32)

    def pass_on(k, src, dst, target):
        return pltpu.make_async_remote_copy(
            src_ref=src,
            dst_ref=dst,
            send_sem=d_send.at[k],
            recv_sem=d_recv.at[k],
            device_id={"head": target},
            device_id_type=MESH,
        )

    top, low = pl.ds(0, half), pl.ds(half, half)
    part[0] = partial(far).astype(BF16)
    far_right = pass_on(0, part.at[0, top], inbox.at[0, top], right)
    far_left = pass_on(1, part.at[0, low], inbox.at[0, low], left)
    far_right.start()
    far_left.start()
    sums[0] = partial(right)
    part[1, low] = sums[0, low].astype(BF16)
    right_low = pass_on(2, part.at[1, low], inbox.at[1, low], right)
    right_low.start()
    sums[1] = partial(left)
    part[2, top] = sums[1, top].astype(BF16)
    left_top = pass_on(3, part.at[2, top], inbox.at[2, top], left)
    left_top.start()
    far_right.wait_recv()
    part[1, top] = (sums[0, top] + inbox[0, top].astype(F32)).astype(BF16)
    right_top = pass_on(4, part.at[1, top], inbox.at[1, top], right)
    right_top.start()
    far_left.wait_recv()
    part[2, low] = (sums[1, low] + inbox[0, low].astype(F32)).astype(BF16)
    left_low = pass_on(5, part.at[2, low], inbox.at[2, low], left)
    left_low.start()
    own = partial(h)
    right_low.wait_recv()
    left_top.wait_recv()
    right_top.wait_recv()
    left_low.wait_recv()
    out_ref[...] = (own + inbox[1].astype(F32) + inbox[2].astype(F32)).astype(BF16)

    for copy in (far_right, far_left, right_low, left_top, right_top, left_low):
        copy.wait_send()
    for n in (0, 1, 4, 5):
        moves[n].wait_send()

    for head in (0, 2, 3):
        each_edge(head, lambda copy: copy.wait_send())

    for i in range(heads):

        @pl.when(p != 2 * i)
        def _():
            to_owner(i).wait_send()

    @pl.when(owner)
    def _():
        group_copies(lambda copy: copy.wait_send())

        @pl.when(feeds)
        def _():
            for k in range(2):
                to_next(k).wait_send()

        for d in FAR_FIRST:
            q = lax.rem(p + d, PLANE)

            @pl.when(q > 0)
            def _():
                prefix_to(q).wait_send()

        @pl.when(z > 0)
        def _():
            for d in ENTRIES:
                entry_to(lax.rem(p + d, PLANE)).wait_send()

    @pl.when(passes_on)
    def _():
        passed.wait_send()


def layer(depth, x, w, down, gdown, beta, up, gup, conv, dlog, bias, span, gain, ow):
    vmem = pl.BlockSpec(memory_space=pltpu.VMEM)
    hbm = pl.BlockSpec(memory_space=pl.ANY)
    rows, model = x.shape
    count, width = 4 * rows, w.shape[2]
    heads = width // 128
    dma = pltpu.SemaphoreType.DMA
    return pl.pallas_call(
        functools.partial(kernel, depth),
        name="layer",
        out_shape=pltpu.VMEM((rows, model), BF16),
        in_specs=[hbm] * 13,
        out_specs=vmem,
        scratch_shapes=[
            pltpu.VMEM((count + HALO, model), BF16),
            pltpu.VMEM(w.shape, BF16),
            pltpu.VMEM((model, 256), BF16),
            pltpu.VMEM(beta.shape, BF16),
            pltpu.VMEM(up.shape, BF16),
            pltpu.VMEM(gup.shape, BF16),
            pltpu.VMEM(conv.shape, BF16),
            pltpu.SMEM(dlog.shape, F32),
            pltpu.VMEM(bias.shape, F32),
            pltpu.VMEM(span.shape, BF16),
            pltpu.VMEM(gain.shape, F32),
            pltpu.VMEM(ow.shape, BF16),
            pltpu.VMEM((3, HALO + count, width), F32),
            pltpu.VMEM((count, width), F32),
            pltpu.VMEM((count, heads), F32),
            pltpu.VMEM((count, width), F32),
            pltpu.VMEM((count, width), F32),
            pltpu.VMEM((count, width), F32),
            pltpu.VMEM((2, (len(LEVELS) + 2) * HALF, width), F32),
            pltpu.VMEM((count, width), F32),
            pltpu.VMEM((count, width), BF16),
            pltpu.VMEM((count, width), F32),
            pltpu.VMEM((heads, 256, 128), BF16),
            pltpu.VMEM((2 * heads, len(LEVELS), HALF, HALF), BF16),
            pltpu.VMEM((2 * heads, HALF, HALF), BF16),
            pltpu.VMEM((PLANE, 256, 128), BF16),
            pltpu.VMEM((PLANE, 256, 128), BF16),
            pltpu.VMEM((256, 128), BF16),
            pltpu.VMEM((GROUP, 256, 128), BF16),
            pltpu.VMEM((128, 128), BF16),
            pltpu.VMEM((256, 128), BF16),
            pltpu.VMEM((128, 128), BF16),
            pltpu.VMEM((128, 128), BF16),
            pltpu.VMEM((heads, 256, 128), BF16),
            pltpu.VMEM((heads, 128, 128), BF16),
            pltpu.VMEM((count, width), BF16),
            pltpu.VMEM((3, rows, model), BF16),
            pltpu.VMEM((2, rows, model), F32),
            pltpu.VMEM((3, rows, model), BF16),
            dma((15,)), dma((6,)), dma((6,)), dma((3,)), dma((3,)), dma((PLANE,)), dma((heads,)),
            dma((heads,)), dma((PLANE,)), dma((GROUP,)), dma((GROUP,)),
            dma((PLANE,)), dma((heads,)), dma((6,)), dma((6,)),
        ],
        compiler_params=pltpu.CompilerParams(
            collective_id=0, has_side_effects=True, vmem_limit_bytes=56 << 20
        ),
    )(x, w, down, gdown, beta, up, gup, conv, dlog, bias, span, gain, ow)


def solution(mesh):
    seq_size = mesh.shape["seq"]
    span = span_matrix()

    def shards(
        hidden_in, qkv_weight, conv_weight, decay_log, dt_bias, decay_down, decay_up,
        beta_weight, gate_down, gate_up, norm_gain, out_weight,
    ):
        return layer(
            seq_size // PLANE,
            hidden_in,
            jnp.transpose(qkv_weight, (1, 0, 2)),
            decay_down,
            gate_down,
            beta_weight.T,
            decay_up,
            gate_up,
            conv_weight,
            decay_log,
            dt_bias.reshape(1, -1),
            jnp.asarray(span, BF16),
            norm_gain.reshape(1, -1),
            out_weight,
        )

    rows = P(("seq", "head"), None)
    return jax.shard_map(
        shards,
        mesh=mesh,
        in_specs=(
            rows, P(None, None, "head"), P(None, None, "head"), P("head"), P("head"), P(),
            P(None, "head"), P(None, "head"), P(), P(None, "head"), P(), P("head", None),
        ),
        out_specs=rows,
        check_vma=False,
    )
```

```python
import functools

import jax
import jax.numpy as jnp
import numpy as np
from jax import lax
from jax.experimental import pallas as pl
from jax.experimental.pallas import tpu as pltpu
from jax.sharding import PartitionSpec as P

F32 = jnp.float32
BF16 = jnp.bfloat16
MESH = pl.DeviceIdType.MESH

HALO = 16
EDGE = 8
HALF = 128
LEVELS = (1, 2, 4, 8, 16, 32, 64)
PLANE = 8
GROUP = 4
FAR_FIRST = (4, 5, 2, 3, 6, 7, 1)
ENTRIES = (7, 4, 2, 3, 6, 1)


def span_matrix():
    r, i = np.arange(HALF)[:, None], np.arange(HALF)[None, :]
    rows = []
    for size in LEVELS:
        middle = (r // (2 * size)) * 2 * size + size - 1
        late = (r % (2 * size)) >= size
        rows.append(np.where(late, (i > middle) & (i <= r), (i > r) & (i <= middle)))
    rows.append(i <= r)
    rows.append(i > r)
    spans = np.concatenate(rows, axis=0)
    return np.concatenate([spans, spans], axis=1).astype(np.float32)


def mm(a, b, dims=((1,), (0,))):
    return lax.dot_general(
        a.astype(BF16), b.astype(BF16), (dims, ((), ())), preferred_element_type=F32
    )


def sigmoid(v):
    return 1.0 / (1.0 + jnp.exp(-v))


def kernel(
    depth, x_hbm, w_hbm, down_hbm, gdown_hbm, beta_hbm, up_hbm, gup_hbm, conv_hbm, dlog_hbm,
    bias_hbm, span_hbm, gain_hbm, ow_hbm, out_ref,
    x_ref, w_ref, dg_ref, beta_ref, up_ref, gup_ref, conv_ref, dlog_ref, bias_ref, span_ref,
    gain_ref, ow_ref,
    proj_ref, fade_ref, strength_ref, q_ref, k_ref, v_ref, e_ref, o_ref, r_ref, gate_ref, z_ref,
    mix_ref, attend_ref, zin, pre, total, zall, chain, link, held, entry, lead, state, normed, part, sums, inbox,
    l_sem, x_send, x_recv, e_sem, f_sem, g_send, g_recv,
    a_send, a_recv, b_send, b_recv, c_send, c_recv, d_send, d_recv,
):
    s = lax.axis_index("seq")
    h = lax.axis_index("head")
    z = lax.div(s, PLANE)
    p = lax.rem(s, PLANE)
    y, core = lax.div(p, 2), lax.rem(p, 2)
    base = z * PLANE
    right, left, far = lax.rem(h + 1, 4), lax.rem(h + 3, 4), lax.rem(h + 2, 4)
    owner = core == 0
    group, rank = lax.div(z, GROUP), lax.rem(z, GROUP)
    feeds = jnp.logical_and(group == 0, jnp.logical_or(rank == 0, rank == GROUP - 1))
    has_next = s < depth * PLANE - 1
    edge_from = jnp.where(h == 1, 2, h)
    rows = x_hbm.shape[0]
    half = rows // 2
    count = 4 * rows
    width = w_ref.shape[2]
    heads = width // 128

    barrier = pltpu.get_barrier_semaphore()
    pl.semaphore_signal(barrier, 1, device_id={"head": right}, device_id_type=MESH)
    pl.semaphore_signal(barrier, 1, device_id={"head": left}, device_id_type=MESH)

    @pl.when(s > 0)
    def _():
        pl.semaphore_signal(
            barrier, 1, device_id={"seq": s - 1, "head": edge_from}, device_id_type=MESH
        )

    for d in range(1, PLANE):
        q = lax.rem(p + d, PLANE)

        @pl.when(jnp.logical_or(owner, lax.rem(q, 2) == 0))
        def _():
            pl.semaphore_signal(barrier, 1, device_id={"seq": base + q}, device_id_type=MESH)

    @pl.when(core == 1)
    def _():
        pl.semaphore_signal(
            barrier, 1, device_id={"seq": base + lax.rem(p + 2, PLANE)}, device_id_type=MESH
        )

    @pl.when(owner)
    def _():
        for d in range(1, GROUP):
            other = group * GROUP + lax.rem(rank + d, GROUP)
            pl.semaphore_signal(
                barrier, 1, device_id={"seq": other * PLANE + p}, device_id_type=MESH
            )

        @pl.when(group == 1)
        def _():
            feeder = jnp.where(rank < 2, GROUP - 1, 0)
            pl.semaphore_signal(
                barrier, 1, device_id={"seq": feeder * PLANE + p}, device_id_type=MESH
            )

    greeted = (
        2
        + jnp.where(owner, PLANE - 1 + GROUP - 1, PLANE // 2 + 1)
        + jnp.where(jnp.logical_and(owner, feeds), 2, 0)
        + jnp.where(has_next, jnp.where(h == 2, 2, jnp.where(h == 1, 0, 1)), 0)
    )

    loads = [
        pltpu.make_async_copy(src, dst, l_sem.at[k])
        for k, (src, dst) in enumerate(
            [
                (x_hbm, x_ref.at[pl.ds(0, rows)]),
                (w_hbm.at[0], w_ref.at[0]),
                (w_hbm.at[1], w_ref.at[1]),
                (w_hbm.at[2], w_ref.at[2]),
                (down_hbm, dg_ref.at[:, pl.ds(0, 128)]),
                (gdown_hbm, dg_ref.at[:, pl.ds(128, 128)]),
                (beta_hbm, beta_ref),
                (up_hbm, up_ref),
                (gup_hbm, gup_ref),
                (conv_hbm, conv_ref),
                (dlog_hbm, dlog_ref),
                (bias_hbm, bias_ref),
                (gain_hbm, gain_ref),
                (span_hbm, span_ref),
                (ow_hbm, ow_ref),
            ]
        )
    ]
    for load in loads:
        load.start()
    x_ref[count + EDGE :, :] = jnp.zeros((HALO - EDGE, x_ref.shape[1]), BF16)

    @pl.when(s == 0)
    def _():
        x_ref[count : count + EDGE, :] = jnp.zeros((EDGE, x_ref.shape[1]), BF16)

    pl.semaphore_wait(barrier, greeted)

    def piece(src, slot, half_at, target, k):
        return pltpu.make_async_remote_copy(
            src_ref=src,
            dst_ref=x_ref.at[pl.ds(slot * rows + half_at * half, half)],
            send_sem=x_send.at[k],
            recv_sem=x_recv.at[k],
            device_id={"head": target},
            device_id_type=MESH,
        )

    def rows_at(slot, half_at):
        return x_ref.at[pl.ds(slot * rows + half_at * half, half)]

    loads[0].wait()
    mine = [rows_at(0, 0), rows_at(0, 1)]
    moves = [
        piece(mine[0], 1, 0, right, 0),
        piece(mine[1], 2, 1, left, 1),
        piece(mine[1], 1, 1, right, 2),
        piece(mine[0], 2, 0, left, 3),
        piece(rows_at(1, 0), 3, 0, right, 4),
        piece(rows_at(2, 1), 3, 1, left, 5),
    ]
    for move in moves[:4]:
        move.start()

    def edge(k, src, target):
        return pltpu.make_async_remote_copy(
            src_ref=src,
            dst_ref=x_ref.at[pl.ds(count, EDGE)],
            send_sem=e_sem.at[k],
            recv_sem=e_sem.at[2],
            device_id={"seq": s + 1, "head": target},
            device_id_type=MESH,
        )

    last = pl.ds(rows - EDGE, EDGE)
    edges = {
        3: [edge(0, x_ref.at[last], 3)],
        0: [edge(0, x_ref.at[pl.ds(2 * rows - EDGE, EDGE)], 0)],
        2: [
            edge(0, x_ref.at[pl.ds(3 * rows - EDGE, EDGE)], 2),
            edge(1, x_ref.at[pl.ds(3 * rows - EDGE, EDGE)], 1),
        ],
    }

    def each_edge(head, act):
        @pl.when(jnp.logical_and(h == head, has_next))
        def _():
            for copy in edges[head]:
                act(copy)

    each_edge(3, lambda copy: copy.start())
    for load in loads[1:14]:
        load.wait()

    rate = jnp.concatenate(
        [jnp.exp(jnp.full((1, 128), dlog_ref[i], F32)) for i in range(heads)], axis=1
    )

    def project(first, slots):
        size = len(slots) * rows
        at = [pl.ds(pl.multiple_of(slot * rows, 16), rows) for slot in slots]
        some = x_ref[first : first + size, :]
        both = jnp.dot(some, dg_ref[...], preferred_element_type=F32).astype(BF16)
        force = sigmoid(
            lax.dot_general(
                some, beta_ref[...], (((1,), (1,)), ((), ())), preferred_element_type=F32
            )
        )
        raw = jnp.dot(both[:, 0:128], up_ref[...], preferred_element_type=F32) + bias_ref[...]
        soft = jnp.maximum(raw, 0.0) + jnp.log1p(jnp.exp(-jnp.abs(raw)))
        log_decay = -rate * soft
        gate = sigmoid(jnp.dot(both[:, 128:256], gup_ref[...], preferred_element_type=F32))
        for n, where in enumerate(at):
            own = slice(n * rows, (n + 1) * rows)
            fade_ref[where, :] = log_decay[own]
            gate_ref[where, :] = gate[own]
            strength_ref[where, :] = force[own]

    def project_qkv(c, first, slots, tail):
        size = len(slots) * rows
        some = x_ref[first : first + size + tail, :]
        got = jnp.dot(some, w_ref[c], preferred_element_type=F32).astype(BF16).astype(F32)
        for n, slot in enumerate(slots):
            at = pl.ds(pl.multiple_of(HALO + slot * rows, 16), rows)
            proj_ref[c, at, :] = got[n * rows : (n + 1) * rows]
        if tail:
            proj_ref[c, HALO - EDGE : HALO, :] = got[size : size + EDGE]

    project(0, (h,))
    for c in range(3):
        project_qkv(c, 0, (h,), 0)

    moves[0].wait_recv()
    moves[2].wait_send()
    moves[4].start()
    moves[1].wait_recv()
    moves[3].wait_send()
    moves[5].start()
    each_edge(2, lambda copy: copy.start())
    moves[2].wait_recv()
    each_edge(0, lambda copy: copy.start())
    moves[3].wait_recv()

    near = (left, right)
    project(rows, near)
    for c in range(3):
        project_qkv(c, rows, near, 0)

    def decays(c):
        piece_of = fade_ref[c * HALF : (c + 1) * HALF, :]
        top = piece_of.astype(BF16)
        rest = (piece_of - top.astype(F32)).astype(BF16)
        e_ref[c] = jnp.exp(
            jnp.dot(
                span_ref[...], jnp.concatenate([top, rest], axis=0), preferred_element_type=F32
            )
        )

    def convolve(c, first, size):
        target = (q_ref, k_ref, v_ref)[c]
        taps = conv_ref[c].astype(F32)
        at = HALO - 3 + first
        mixed = proj_ref[c, pl.ds(at, size), :] * taps[0:1]
        for i in range(1, 4):
            mixed = mixed + proj_ref[c, pl.ds(at + i, size), :] * taps[i : i + 1]
        mixed = (mixed * sigmoid(mixed)).astype(BF16).astype(F32)
        if c == 2:
            target[first : first + size, :] = mixed
            return
        for i in range(heads):
            lanes = slice(i * 128, (i + 1) * 128)
            u = mixed[:, lanes]
            scale = lax.rsqrt(jnp.sum(u * u, axis=1, keepdims=True) + 1e-06)
            if c == 0:
                scale = scale * (128**-0.5)
            target[first : first + size, lanes] = u * scale

    far_square = lax.div(far, 2)
    for c in range(2):

        @pl.when(far_square == 1 - c)
        def _():
            decays(c)
            for n in range(3):
                convolve(n, c * HALF + EDGE, HALF - EDGE)

    moves[4].wait_recv()
    moves[5].wait_recv()

    @pl.when(s > 0)
    def _():
        edges[0][0].wait_recv()

    for c in range(2):

        @pl.when(far_square == c)
        def _():
            project(3 * rows, (far,))
            project_qkv(1, 3 * rows, (far,), HALO)
            decays(c)
            project_qkv(0, 3 * rows, (far,), HALO)
            convolve(1, c * HALF, HALF)
            project_qkv(2, 3 * rows, (far,), HALO)
            convolve(0, c * HALF, HALF)
            convolve(2, c * HALF, HALF)
            for n in range(3):
                convolve(n, (1 - c) * HALF, EDGE)

    beta = strength_ref[...]

    t = lax.broadcasted_iota(jnp.int32, (HALF, HALF), 0)
    j = lax.broadcasted_iota(jnp.int32, (HALF, HALF), 1)
    row = lax.broadcasted_iota(jnp.int32, (HALF, 128), 0)
    masks = [
        ((t ^ j) >= size) & ((t ^ j) < 2 * size) & (t > j) for size in LEVELS
    ]
    diagonal = t == j

    lanes_of = [slice(i * 128, (i + 1) * 128) for i in range(heads)]
    rows_of = [slice(c * HALF, (c + 1) * HALF) for c in range(2)]

    def to_owner(i):
        return pltpu.make_async_remote_copy(
            src_ref=z_ref.at[i],
            dst_ref=zin.at[p],
            send_sem=a_send.at[i],
            recv_sem=a_recv.at[p],
            device_id={"seq": base + 2 * i},
            device_id_type=MESH,
        )

    strength, inverse = {}, {}

    def unit_of(i, c):
        return 2 * i + c

    def mix(i, c, n, attend):
        kc, qc = k_ref[rows_of[c], lanes_of[i]], q_ref[rows_of[c], lanes_of[i]]
        if n == 0:
            strength[i, c] = jnp.broadcast_to(beta[rows_of[c], i : i + 1], (HALF, 128))
            own = jnp.sum(qc * kc, axis=1, keepdims=True) * strength[i, c]
            attend = jnp.where(diagonal, own, 0.0)
        size = LEVELS[n]
        fade = e_ref[c, n * HALF : (n + 1) * HALF, lanes_of[i]]
        late = (row & size) != 0
        kx = (kc * fade * jnp.where(late, 1.0, strength[i, c])).astype(BF16)
        qx = (qc * fade).astype(BF16)
        both = mm(jnp.concatenate([kx, qx], axis=0), kx, ((1,), (1,)))
        mix_ref[unit_of(i, c), n] = jnp.where(masks[n], both[:HALF], 0.0).astype(BF16)
        attend = jnp.where(masks[n], both[HALF:], attend)
        if n == len(LEVELS) - 1:
            attend_ref[unit_of(i, c)] = attend.astype(BF16)
        return attend

    def mixes(some):
        for i in some:
            for c in range(2):
                attend = None
                for n in range(len(LEVELS)):
                    attend = mix(i, c, n, attend)
                    yield

    def doublings(some):
        units = [(i, c) for i in some for c in range(2)]
        for unit in units:
            inverse[unit] = jnp.where(diagonal, 1.0, 0.0) - mix_ref[unit_of(*unit), 0].astype(F32)
        for n in range(1, len(LEVELS)):
            own = {unit: inverse[unit].astype(BF16) for unit in units}
            left_part = {}
            for unit in units:
                left_part[unit] = mm(own[unit], mix_ref[unit_of(*unit), n]).astype(BF16)
            yield
            for unit in units:
                inverse[unit] = inverse[unit] - mm(left_part[unit], own[unit])
            yield
        for unit in units:
            inverse[unit] = inverse[unit].astype(BF16)

    parts = {}

    def maps_of(some):
        n = len(LEVELS)
        units = [(i, c) for i in some for c in range(2)]
        rise = {u: e_ref[u[1], n * HALF : (n + 1) * HALF, lanes_of[u[0]]] for u in units}
        fall = {u: e_ref[u[1], (n + 1) * HALF : (n + 2) * HALF, lanes_of[u[0]]] for u in units}
        whole = {u: rise[u][HALF - 1 : HALF] for u in units}
        k_rise = {u: k_ref[rows_of[u[1]], lanes_of[u[0]]] * rise[u] for u in units}
        q_rise = {u: q_ref[rows_of[u[1]], lanes_of[u[0]]] * rise[u] for u in units}
        k_fall = {
            u: k_ref[rows_of[u[1]], lanes_of[u[0]]] * fall[u] * strength[u] for u in units
        }
        cross, first, second = {}, {}, {}
        for i in some:
            cross[i] = mm(
                jnp.concatenate([k_rise[i, 1], q_rise[i, 1]], axis=0), k_fall[i, 0], ((1,), (1,))
            ).astype(BF16)
        for i in some:
            first[i] = mm(
                inverse[i, 0],
                jnp.concatenate([v_ref[rows_of[0], lanes_of[i]], k_rise[i, 0]], axis=1),
            ).astype(BF16)
        yield
        late_part = {i: mm(cross[i], first[i]) for i in some}
        yield
        for i in some:
            start = jnp.concatenate(
                [v_ref[rows_of[1], lanes_of[i]], k_rise[i, 1] * whole[i, 0]], axis=1
            )
            second[i] = mm(inverse[i, 1], start - late_part[i][:HALF]).astype(BF16)
        yield
        for i in some:
            stop = jnp.concatenate(
                [k_fall[i, 0] * whole[i, 1], k_fall[i, 1]], axis=0
            ).astype(BF16)
            maps = mm(jnp.concatenate([first[i], second[i]], axis=0), stop, ((0,), (0,)))
            move = jnp.where(diagonal, whole[i, 0] * whole[i, 1], 0.0) - maps[128:]
            z_ref[i, 0:128] = move.astype(BF16)
            z_ref[i, 128:256] = maps[:128].astype(BF16)
            parts[i] = (q_rise, whole, first, second, late_part)

    def outputs_of(some):
        for i in some:
            q_rise, whole, first, second, late_part = parts[i]
            lanes = lanes_of[i]
            out = [
                mm(attend_ref[unit_of(i, 0)], first[i]),
                late_part[i][HALF:] + mm(attend_ref[unit_of(i, 1)], second[i]),
            ]
            for c in range(2):
                o_ref[rows_of[c], lanes] = out[c][:, :128]
            r_ref[rows_of[0], lanes] = (q_rise[i, 0] - out[0][:, 128:]).astype(BF16)
            r_ref[rows_of[1], lanes] = (
                q_rise[i, 1] * whole[i, 0] - out[1][:, 128:]
            ).astype(BF16)
            yield

    def send_maps(some):
        for i in some:

            @pl.when(p != 2 * i)
            def _():
                to_owner(i).start()

    def together(main, other, share):
        for _ in main:
            for _ in range(share):
                next(other, None)

    def finish(*works):
        for work in works:
            for _ in work:
                pass

    early, late_heads = range(0, heads, 2), range(1, heads, 2)
    finish(mixes(early))
    other = mixes(late_heads)
    together(doublings(early), other, 3)
    finish(other)
    other = doublings(late_heads)
    together(maps_of(early), other, 1)
    send_maps(early)
    outputs = outputs_of(early)
    together(other, outputs, 1)
    finish(outputs, maps_of(late_heads))
    send_maps(late_heads)
    finish(outputs_of(late_heads))

    def to_group(k, at):
        return pltpu.make_async_remote_copy(
            src_ref=total.at[at],
            dst_ref=zall.at[rank, at],
            send_sem=b_send.at[k],
            recv_sem=b_recv.at[rank],
            device_id={"seq": (group * GROUP + k) * PLANE + p},
            device_id_type=MESH,
        )

    def from_group(k, at):
        return pltpu.make_async_remote_copy(
            src_ref=total.at[at],
            dst_ref=zall.at[k, at],
            send_sem=b_send.at[k],
            recv_sem=b_recv.at[k],
            device_id={"seq": s},
            device_id_type=MESH,
        )

    def to_next(k):
        target = jnp.where(rank == 0, 2 * GROUP - 1 - k, GROUP + k)
        return pltpu.make_async_remote_copy(
            src_ref=chain,
            dst_ref=held,
            send_sem=f_sem.at[k],
            recv_sem=f_sem.at[2],
            device_id={"seq": target * PLANE + p},
            device_id_type=MESH,
        )

    def prefix_to(q):
        return pltpu.make_async_remote_copy(
            src_ref=pre.at[q],
            dst_ref=lead.at[y],
            send_sem=g_send.at[q],
            recv_sem=g_recv.at[y],
            device_id={"seq": base + q},
            device_id_type=MESH,
        )

    def entry_to(q):
        return pltpu.make_async_remote_copy(
            src_ref=entry,
            dst_ref=state.at[y],
            send_sem=c_send.at[q],
            recv_sem=c_recv.at[y],
            device_id={"seq": base + q},
            device_id_type=MESH,
        )

    def landed(ref, sem, k):
        pltpu.make_async_remote_copy(
            src_ref=ref.at[k],
            dst_ref=ref.at[k],
            send_sem=sem.at[k],
            recv_sem=sem.at[k],
            device_id={"seq": s},
            device_id_type=MESH,
        ).wait_recv()

    everything, shift_only = pl.ds(0, 256), pl.ds(128, 128)
    half_plane = PLANE // 2

    def join(one, two):
        step = mm(one, two[:128])
        return jnp.concatenate(
            [step[:128].astype(BF16), (step[128:] + two[128:].astype(F32)).astype(BF16)], axis=0
        )

    def moved(state_in, both):
        return (mm(state_in, both[0:128]) + both[128:256].astype(F32)).astype(BF16)

    def group_copies(act):
        for k in range(GROUP):
            @pl.when(jnp.logical_and(jnp.logical_and(group == 0, rank == 0), k > 0))
            def _():
                act(to_group(k, shift_only))

            wanted = k > rank
            if k == 0:
                wanted = jnp.logical_and(group == 0, rank > 0)
            else:
                wanted = jnp.logical_and(
                    wanted, jnp.logical_or(group == 1, rank > 0)
                )

            @pl.when(wanted)
            def _():
                act(to_group(k, everything))

    @pl.when(owner)
    def _():
        zin[p] = z_ref[y]
        for k in range(PLANE):

            @pl.when(p != k)
            def _():
                landed(zin, a_recv, k)

        one, two = zin[0], zin[half_plane]
        later = {}
        for k in range(1, half_plane):
            pre[k], later[half_plane + k] = one, two
            one, two = join(one, zin[k]), join(two, zin[half_plane + k])
        pre[half_plane] = one
        whole_map = join(one, two)
        total[...] = whole_map
        group_copies(lambda copy: copy.start())
        zall[rank] = whole_map
        for k in range(half_plane + 1, PLANE):
            pre[k] = join(one, later[k])
        for d in FAR_FIRST:
            q = lax.rem(p + d, PLANE)

            @pl.when(q > 0)
            def _():
                prefix_to(q).start()

        @pl.when(p > 0)
        def _():
            lead[y] = pre[p]

        @pl.when(group == 0)
        def _():
            chain[...] = jnp.zeros_like(chain)
            entry[...] = jnp.zeros_like(entry)
            for k in range(GROUP):
                needed = jnp.logical_or(feeds, k < rank)
                if k == 0:

                    @pl.when(rank > 0)
                    def _():
                        from_group(0, shift_only).wait_recv()

                else:

                    @pl.when(jnp.logical_and(needed, rank != k))
                    def _():
                        from_group(k, everything).wait_recv()

                @pl.when(rank == k)
                def _():
                    entry[...] = chain[...]

                @pl.when(needed)
                def _():
                    if k == 0:
                        chain[...] = zall[0, 128:256]
                    else:
                        chain[...] = moved(chain[...], zall[k])

            @pl.when(feeds)
            def _():
                for k in range(2):
                    to_next(k).start()

        @pl.when(group == 1)
        def _():
            for k in range(GROUP - 1):

                @pl.when(k < rank)
                def _():
                    from_group(k, everything).wait_recv()
                    if k == 0:
                        link[...] = zall[0]
                    else:
                        link[...] = join(link[...], zall[k])

            to_next(0).wait_recv()

            @pl.when(rank == 0)
            def _():
                entry[...] = held[...]

            @pl.when(rank > 0)
            def _():
                entry[...] = moved(held[...], link[...])

        @pl.when(z > 0)
        def _():
            for d in ENTRIES:
                entry_to(lax.rem(p + d, PLANE)).start()

            state[y] = entry[...]

    @pl.when(z == 0)
    def _():
        state[...] = jnp.zeros_like(state)

    @pl.when(p > 0)
    def _():
        for i in range(heads):

            @pl.when(p != 2 * i)
            def _():
                landed(lead, g_recv, i)

        for i in range(heads):
            lanes = lanes_of[i]
            both = mm(r_ref[:, lanes], lead[i], ((1,), (1,)))
            o_ref[:, lanes] = o_ref[:, lanes] + both[:, 128:]
            r_ref[:, lanes] = both[:, :128].astype(BF16)

    after_own = lax.rem(y + 1, heads)
    passes_on = jnp.logical_and(core == 1, z > 0)
    passed = pltpu.make_async_remote_copy(
        src_ref=state.at[after_own],
        dst_ref=state.at[after_own],
        send_sem=c_send.at[0],
        recv_sem=c_recv.at[after_own],
        device_id={"seq": base + lax.rem(p + PLANE - 2, PLANE)},
        device_id_type=MESH,
    )
    for d in (1, 0, 3, 2):
        i = lax.rem(y + d, heads)

        @pl.when(jnp.logical_and(p != 2 * i, z > 0))
        def _():
            landed(state, c_recv, i)

        if d == 1:

            @pl.when(passes_on)
            def _():
                passed.start()

        lanes = pl.ds(pl.multiple_of(i * 128, 128), 128)
        attended = o_ref[:, lanes] + mm(r_ref[:, lanes], state[i], ((1,), (1,)))
        scale = lax.rsqrt(jnp.mean(attended * attended, axis=1, keepdims=True) + 1e-05)
        normed[:, lanes] = (attended * scale * gain_ref[...] * gate_ref[:, lanes]).astype(BF16)
    loads[14].wait()


    def partial(to):
        at = pl.ds(pl.multiple_of(to * rows, 16), rows)
        return jnp.dot(normed[at, :], ow_ref[...], preferred_element_type=F32)

    def pass_on(k, src, dst, target):
        return pltpu.make_async_remote_copy(
            src_ref=src,
            dst_ref=dst,
            send_sem=d_send.at[k],
            recv_sem=d_recv.at[k],
            device_id={"head": target},
            device_id_type=MESH,
        )

    top, low = pl.ds(0, half), pl.ds(half, half)
    part[0] = partial(far).astype(BF16)
    far_right = pass_on(0, part.at[0, top], inbox.at[0, top], right)
    far_left = pass_on(1, part.at[0, low], inbox.at[0, low], left)
    far_right.start()
    far_left.start()
    sums[0] = partial(right)
    part[1, low] = sums[0, low].astype(BF16)
    right_low = pass_on(2, part.at[1, low], inbox.at[1, low], right)
    right_low.start()
    sums[1] = partial(left)
    part[2, top] = sums[1, top].astype(BF16)
    left_top = pass_on(3, part.at[2, top], inbox.at[2, top], left)
    left_top.start()
    far_right.wait_recv()
    part[1, top] = (sums[0, top] + inbox[0, top].astype(F32)).astype(BF16)
    right_top = pass_on(4, part.at[1, top], inbox.at[1, top], right)
    right_top.start()
    far_left.wait_recv()
    part[2, low] = (sums[1, low] + inbox[0, low].astype(F32)).astype(BF16)
    left_low = pass_on(5, part.at[2, low], inbox.at[2, low], left)
    left_low.start()
    own = partial(h)
    right_low.wait_recv()
    left_top.wait_recv()
    right_top.wait_recv()
    left_low.wait_recv()
    out_ref[...] = (own + inbox[1].astype(F32) + inbox[2].astype(F32)).astype(BF16)

    for copy in (far_right, far_left, right_low, left_top, right_top, left_low):
        copy.wait_send()
    for n in (0, 1, 4, 5):
        moves[n].wait_send()

    for head in (0, 2, 3):
        each_edge(head, lambda copy: copy.wait_send())

    for i in range(heads):

        @pl.when(p != 2 * i)
        def _():
            to_owner(i).wait_send()

    @pl.when(owner)
    def _():
        group_copies(lambda copy: copy.wait_send())

        @pl.when(feeds)
        def _():
            for k in range(2):
                to_next(k).wait_send()

        for d in FAR_FIRST:
            q = lax.rem(p + d, PLANE)

            @pl.when(q > 0)
            def _():
                prefix_to(q).wait_send()

        @pl.when(z > 0)
        def _():
            for d in ENTRIES:
                entry_to(lax.rem(p + d, PLANE)).wait_send()

    @pl.when(passes_on)
    def _():
        passed.wait_send()


def layer(depth, x, w, down, gdown, beta, up, gup, conv, dlog, bias, span, gain, ow):
    vmem = pl.BlockSpec(memory_space=pltpu.VMEM)
    hbm = pl.BlockSpec(memory_space=pl.ANY)
    rows, model = x.shape
    count, width = 4 * rows, w.shape[2]
    heads = width // 128
    dma = pltpu.SemaphoreType.DMA
    return pl.pallas_call(
        functools.partial(kernel, depth),
        name="layer",
        out_shape=pltpu.VMEM((rows, model), BF16),
        in_specs=[hbm] * 13,
        out_specs=vmem,
        scratch_shapes=[
            pltpu.VMEM((count + HALO, model), BF16),
            pltpu.VMEM(w.shape, BF16),
            pltpu.VMEM((model, 256), BF16),
            pltpu.VMEM(beta.shape, BF16),
            pltpu.VMEM(up.shape, BF16),
            pltpu.VMEM(gup.shape, BF16),
            pltpu.VMEM(conv.shape, BF16),
            pltpu.SMEM(dlog.shape, F32),
            pltpu.VMEM(bias.shape, F32),
            pltpu.VMEM(span.shape, BF16),
            pltpu.VMEM(gain.shape, F32),
            pltpu.VMEM(ow.shape, BF16),
            pltpu.VMEM((3, HALO + count, width), F32),
            pltpu.VMEM((count, width), F32),
            pltpu.VMEM((count, heads), F32),
            pltpu.VMEM((count, width), F32),
            pltpu.VMEM((count, width), F32),
            pltpu.VMEM((count, width), F32),
            pltpu.VMEM((2, (len(LEVELS) + 2) * HALF, width), F32),
            pltpu.VMEM((count, width), F32),
            pltpu.VMEM((count, width), BF16),
            pltpu.VMEM((count, width), F32),
            pltpu.VMEM((heads, 256, 128), BF16),
            pltpu.VMEM((2 * heads, len(LEVELS), HALF, HALF), BF16),
            pltpu.VMEM((2 * heads, HALF, HALF), BF16),
            pltpu.VMEM((PLANE, 256, 128), BF16),
            pltpu.VMEM((PLANE, 256, 128), BF16),
            pltpu.VMEM((256, 128), BF16),
            pltpu.VMEM((GROUP, 256, 128), BF16),
            pltpu.VMEM((128, 128), BF16),
            pltpu.VMEM((256, 128), BF16),
            pltpu.VMEM((128, 128), BF16),
            pltpu.VMEM((128, 128), BF16),
            pltpu.VMEM((heads, 256, 128), BF16),
            pltpu.VMEM((heads, 128, 128), BF16),
            pltpu.VMEM((count, width), BF16),
            pltpu.VMEM((3, rows, model), BF16),
            pltpu.VMEM((2, rows, model), F32),
            pltpu.VMEM((3, rows, model), BF16),
            dma((15,)), dma((6,)), dma((6,)), dma((3,)), dma((3,)), dma((PLANE,)), dma((heads,)),
            dma((heads,)), dma((PLANE,)), dma((GROUP,)), dma((GROUP,)),
            dma((PLANE,)), dma((heads,)), dma((6,)), dma((6,)),
        ],
        compiler_params=pltpu.CompilerParams(
            collective_id=0, has_side_effects=True, vmem_limit_bytes=56 << 20
        ),
    )(x, w, down, gdown, beta, up, gup, conv, dlog, bias, span, gain, ow)


def solution(mesh):
    seq_size = mesh.shape["seq"]
    span = span_matrix()

    def shards(
        hidden_in, qkv_weight, conv_weight, decay_log, dt_bias, decay_down, decay_up,
        beta_weight, gate_down, gate_up, norm_gain, out_weight,
    ):
        return layer(
            seq_size // PLANE,
            hidden_in,
            jnp.transpose(qkv_weight, (1, 0, 2)),
            decay_down,
            gate_down,
            beta_weight.T,
            decay_up,
            gate_up,
            conv_weight,
            decay_log,
            dt_bias.reshape(1, -1),
            jnp.asarray(span, BF16),
            norm_gain.reshape(1, -1),
            out_weight,
        )

    rows = P(("seq", "head"), None)
    return jax.shard_map(
        shards,
        mesh=mesh,
        in_specs=(
            rows, P(None, None, "head"), P(None, None, "head"), P("head"), P("head"), P(),
            P(None, "head"), P(None, "head"), P(), P(None, "head"), P(), P("head", None),
        ),
        out_specs=rows,
        check_vma=False,
    )
```

```python
import functools

import jax
import jax.numpy as jnp
import numpy as np
from jax import lax
from jax.experimental import pallas as pl
from jax.experimental.pallas import tpu as pltpu
from jax.sharding import PartitionSpec as P

F32 = jnp.float32
BF16 = jnp.bfloat16
MESH = pl.DeviceIdType.MESH

HALO = 16
EDGE = 8
HALF = 128
LEVELS = (1, 2, 4, 8, 16, 32, 64)
PLANE = 8
GROUP = 4
FAR_FIRST = (4, 5, 2, 3, 6, 7, 1)
ENTRIES = (7, 4, 2, 3, 6, 1)


def span_matrix():
    r, i = np.arange(HALF)[:, None], np.arange(HALF)[None, :]
    rows = []
    for size in LEVELS:
        middle = (r // (2 * size)) * 2 * size + size - 1
        late = (r % (2 * size)) >= size
        rows.append(np.where(late, (i > middle) & (i <= r), (i > r) & (i <= middle)))
    rows.append(i <= r)
    rows.append(i > r)
    spans = np.concatenate(rows, axis=0)
    return np.concatenate([spans, spans], axis=1).astype(np.float32)


def mm(a, b, dims=((1,), (0,))):
    return lax.dot_general(
        a.astype(BF16), b.astype(BF16), (dims, ((), ())), preferred_element_type=F32
    )


def sigmoid(v):
    return 1.0 / (1.0 + jnp.exp(-v))


def kernel(
    depth, x_hbm, w_hbm, down_hbm, gdown_hbm, beta_hbm, up_hbm, gup_hbm, conv_hbm, dlog_hbm,
    bias_hbm, span_hbm, gain_hbm, ow_hbm, out_ref,
    x_ref, w_ref, dg_ref, beta_ref, up_ref, gup_ref, conv_ref, dlog_ref, bias_ref, span_ref,
    gain_ref, ow_ref,
    proj_ref, fade_ref, strength_ref, q_ref, k_ref, v_ref, e_ref, o_ref, r_ref, gate_ref, z_ref,
    mix_ref, faded_ref, attend_ref, zin, pre, total, zall, chain, link, held, entry, lead, state, normed, part, sums, inbox,
    l_sem, x_send, x_recv, e_sem, f_sem, g_send, g_recv,
    a_send, a_recv, b_send, b_recv, c_send, c_recv, d_send, d_recv,
):
    s = lax.axis_index("seq")
    h = lax.axis_index("head")
    z = lax.div(s, PLANE)
    p = lax.rem(s, PLANE)
    y, core = lax.div(p, 2), lax.rem(p, 2)
    base = z * PLANE
    right, left, far = lax.rem(h + 1, 4), lax.rem(h + 3, 4), lax.rem(h + 2, 4)
    owner = core == 0
    group, rank = lax.div(z, GROUP), lax.rem(z, GROUP)
    feeds = jnp.logical_and(group == 0, jnp.logical_or(rank == 0, rank == GROUP - 1))
    has_next = s < depth * PLANE - 1
    edge_from = jnp.where(h == 1, 2, h)
    rows = x_hbm.shape[0]
    half = rows // 2
    count = 4 * rows
    width = w_ref.shape[2]
    heads = width // 128

    barrier = pltpu.get_barrier_semaphore()
    pl.semaphore_signal(barrier, 1, device_id={"head": right}, device_id_type=MESH)
    pl.semaphore_signal(barrier, 1, device_id={"head": left}, device_id_type=MESH)

    @pl.when(s > 0)
    def _():
        pl.semaphore_signal(
            barrier, 1, device_id={"seq": s - 1, "head": edge_from}, device_id_type=MESH
        )

    for d in range(1, PLANE):
        q = lax.rem(p + d, PLANE)

        @pl.when(jnp.logical_or(owner, lax.rem(q, 2) == 0))
        def _():
            pl.semaphore_signal(barrier, 1, device_id={"seq": base + q}, device_id_type=MESH)

    @pl.when(core == 1)
    def _():
        pl.semaphore_signal(
            barrier, 1, device_id={"seq": base + lax.rem(p + 2, PLANE)}, device_id_type=MESH
        )

    @pl.when(owner)
    def _():
        for d in range(1, GROUP):
            other = group * GROUP + lax.rem(rank + d, GROUP)
            pl.semaphore_signal(
                barrier, 1, device_id={"seq": other * PLANE + p}, device_id_type=MESH
            )

        @pl.when(group == 1)
        def _():
            feeder = jnp.where(rank < GROUP - 1, GROUP - 1, 0)
            pl.semaphore_signal(
                barrier, 1, device_id={"seq": feeder * PLANE + p}, device_id_type=MESH
            )

    greeted = (
        2
        + jnp.where(owner, PLANE - 1 + GROUP - 1, PLANE // 2 + 1)
        + jnp.where(jnp.logical_and(owner, feeds), jnp.where(rank == 0, 1, GROUP - 1), 0)
        + jnp.where(has_next, jnp.where(h == 2, 2, jnp.where(h == 1, 0, 1)), 0)
    )

    loads = [
        pltpu.make_async_copy(src, dst, l_sem.at[k])
        for k, (src, dst) in enumerate(
            [
                (x_hbm, x_ref.at[pl.ds(0, rows)]),
                (w_hbm.at[0], w_ref.at[0]),
                (w_hbm.at[1], w_ref.at[1]),
                (w_hbm.at[2], w_ref.at[2]),
                (down_hbm, dg_ref.at[:, pl.ds(0, 128)]),
                (gdown_hbm, dg_ref.at[:, pl.ds(128, 128)]),
                (beta_hbm, beta_ref),
                (up_hbm, up_ref),
                (gup_hbm, gup_ref),
                (conv_hbm, conv_ref),
                (dlog_hbm, dlog_ref),
                (bias_hbm, bias_ref),
                (gain_hbm, gain_ref),
                (span_hbm, span_ref),
                (ow_hbm, ow_ref),
            ]
        )
    ]
    for load in loads:
        load.start()
    x_ref[count + EDGE :, :] = jnp.zeros((HALO - EDGE, x_ref.shape[1]), BF16)

    @pl.when(s == 0)
    def _():
        x_ref[count : count + EDGE, :] = jnp.zeros((EDGE, x_ref.shape[1]), BF16)

    pl.semaphore_wait(barrier, greeted)

    def piece(src, slot, half_at, target, k):
        return pltpu.make_async_remote_copy(
            src_ref=src,
            dst_ref=x_ref.at[pl.ds(slot * rows + half_at * half, half)],
            send_sem=x_send.at[k],
            recv_sem=x_recv.at[k],
            device_id={"head": target},
            device_id_type=MESH,
        )

    def rows_at(slot, half_at):
        return x_ref.at[pl.ds(slot * rows + half_at * half, half)]

    loads[0].wait()
    mine = [rows_at(0, 0), rows_at(0, 1)]
    moves = [
        piece(mine[0], 1, 0, right, 0),
        piece(mine[1], 2, 1, left, 1),
        piece(mine[1], 1, 1, right, 2),
        piece(mine[0], 2, 0, left, 3),
        piece(rows_at(1, 0), 3, 0, right, 4),
        piece(rows_at(2, 1), 3, 1, left, 5),
    ]
    for move in moves[:4]:
        move.start()

    def edge(k, src, target):
        return pltpu.make_async_remote_copy(
            src_ref=src,
            dst_ref=x_ref.at[pl.ds(count, EDGE)],
            send_sem=e_sem.at[k],
            recv_sem=e_sem.at[2],
            device_id={"seq": s + 1, "head": target},
            device_id_type=MESH,
        )

    last = pl.ds(rows - EDGE, EDGE)
    edges = {
        3: [edge(0, x_ref.at[last], 3)],
        0: [edge(0, x_ref.at[pl.ds(2 * rows - EDGE, EDGE)], 0)],
        2: [
            edge(0, x_ref.at[pl.ds(3 * rows - EDGE, EDGE)], 2),
            edge(1, x_ref.at[pl.ds(3 * rows - EDGE, EDGE)], 1),
        ],
    }

    def each_edge(head, act):
        @pl.when(jnp.logical_and(h == head, has_next))
        def _():
            for copy in edges[head]:
                act(copy)

    each_edge(3, lambda copy: copy.start())
    for load in loads[1:14]:
        load.wait()

    rate = jnp.concatenate(
        [jnp.exp(jnp.full((1, 128), dlog_ref[i], F32)) for i in range(heads)], axis=1
    )

    def project(first, slots):
        size = len(slots) * rows
        at = [pl.ds(pl.multiple_of(slot * rows, 16), rows) for slot in slots]
        some = x_ref[first : first + size, :]
        both = jnp.dot(some, dg_ref[...], preferred_element_type=F32).astype(BF16)
        force = sigmoid(
            lax.dot_general(
                some, beta_ref[...], (((1,), (1,)), ((), ())), preferred_element_type=F32
            )
        )
        raw = jnp.dot(both[:, 0:128], up_ref[...], preferred_element_type=F32) + bias_ref[...]
        soft = jnp.maximum(raw, 0.0) + jnp.log1p(jnp.exp(-jnp.abs(raw)))
        log_decay = -rate * soft
        gate = sigmoid(jnp.dot(both[:, 128:256], gup_ref[...], preferred_element_type=F32))
        for n, where in enumerate(at):
            own = slice(n * rows, (n + 1) * rows)
            fade_ref[where, :] = log_decay[own]
            gate_ref[where, :] = gate[own]
            strength_ref[where, :] = force[own]

    def project_qkv(c, first, slots, tail):
        size = len(slots) * rows
        some = x_ref[first : first + size + tail, :]
        got = jnp.dot(some, w_ref[c], preferred_element_type=F32).astype(BF16).astype(F32)
        for n, slot in enumerate(slots):
            at = pl.ds(pl.multiple_of(HALO + slot * rows, 16), rows)
            proj_ref[c, at, :] = got[n * rows : (n + 1) * rows]
        if tail:
            proj_ref[c, HALO - EDGE : HALO, :] = got[size : size + EDGE]

    def decays(c):
        piece_of = fade_ref[pl.ds(pl.multiple_of(c * HALF, HALF), HALF), :]
        top = piece_of.astype(BF16)
        rest = (piece_of - top.astype(F32)).astype(BF16)
        e_ref[c] = jnp.exp(
            jnp.dot(
                span_ref[...], jnp.concatenate([top, rest], axis=0), preferred_element_type=F32
            )
        )

    project(0, (h,))
    for c in range(3):
        project_qkv(c, 0, (h,), 0)

    moves[0].wait_recv()
    moves[2].wait_send()
    moves[4].start()
    moves[1].wait_recv()
    moves[3].wait_send()
    moves[5].start()
    each_edge(2, lambda copy: copy.start())
    moves[2].wait_recv()
    each_edge(0, lambda copy: copy.start())
    moves[3].wait_recv()

    near = (left, right)
    project(rows, near)
    for c in range(3):
        project_qkv(c, rows, near, 0)
    far_square = lax.div(far, 2)
    decays(1 - far_square)
    moves[4].wait_recv()
    moves[5].wait_recv()

    @pl.when(s > 0)
    def _():
        edges[0][0].wait_recv()

    def convolve(c):
        target = (q_ref, k_ref, v_ref)[c]
        taps = conv_ref[c].astype(F32)
        mixed = proj_ref[c, pl.ds(HALO - 3, count), :] * taps[0:1]
        for i in range(1, 4):
            mixed = mixed + proj_ref[c, pl.ds(HALO - 3 + i, count), :] * taps[i : i + 1]
        mixed = (mixed * sigmoid(mixed)).astype(BF16).astype(F32)
        if c == 2:
            target[...] = mixed
            return
        for i in range(heads):
            lanes = slice(i * 128, (i + 1) * 128)
            u = mixed[:, lanes]
            scale = lax.rsqrt(jnp.sum(u * u, axis=1, keepdims=True) + 1e-06)
            if c == 0:
                scale = scale * (128**-0.5)
            target[:, lanes] = u * scale

    project(3 * rows, (far,))
    project_qkv(1, 3 * rows, (far,), HALO)
    decays(far_square)
    project_qkv(0, 3 * rows, (far,), HALO)
    convolve(1)
    project_qkv(2, 3 * rows, (far,), HALO)
    convolve(0)
    convolve(2)
    beta = strength_ref[...]

    t = lax.broadcasted_iota(jnp.int32, (HALF, HALF), 0)
    j = lax.broadcasted_iota(jnp.int32, (HALF, HALF), 1)
    row = lax.broadcasted_iota(jnp.int32, (HALF, 128), 0)
    masks = [
        ((t ^ j) >= size) & ((t ^ j) < 2 * size) & (t > j) for size in LEVELS
    ]
    diagonal = t == j

    lanes_of = [slice(i * 128, (i + 1) * 128) for i in range(heads)]
    rows_of = [slice(c * HALF, (c + 1) * HALF) for c in range(2)]

    def to_owner(i):
        return pltpu.make_async_remote_copy(
            src_ref=z_ref.at[i],
            dst_ref=zin.at[p],
            send_sem=a_send.at[i],
            recv_sem=a_recv.at[p],
            device_id={"seq": base + 2 * i},
            device_id_type=MESH,
        )

    strength, inverse = {}, {}

    def unit_of(i, c):
        return 2 * i + c

    def mix(i, c, n):
        kc = k_ref[rows_of[c], lanes_of[i]]
        if n == 0:
            strength[i, c] = jnp.broadcast_to(beta[rows_of[c], i : i + 1], (HALF, 128))
        fade = e_ref[c, n * HALF : (n + 1) * HALF, lanes_of[i]]
        late = (row & LEVELS[n]) != 0
        kx = (kc * fade * jnp.where(late, 1.0, strength[i, c])).astype(BF16)
        faded_ref[unit_of(i, c), n] = kx
        mix_ref[unit_of(i, c), n] = jnp.where(masks[n], mm(kx, kx, ((1,), (1,))), 0.0).astype(BF16)

    def mixes(some):
        for i in some:
            for c in range(2):
                for n in range(len(LEVELS)):
                    mix(i, c, n)
                    yield

    def attends(some):
        for i in some:
            for c in range(2):
                kc, qc = k_ref[rows_of[c], lanes_of[i]], q_ref[rows_of[c], lanes_of[i]]
                own = jnp.sum(qc * kc, axis=1, keepdims=True) * strength[i, c]
                attend = jnp.where(diagonal, own, 0.0)
                for n in range(len(LEVELS)):
                    qx = qc * e_ref[c, n * HALF : (n + 1) * HALF, lanes_of[i]]
                    both = mm(qx, faded_ref[unit_of(i, c), n], ((1,), (1,)))
                    attend = jnp.where(masks[n], both, attend)
                attend_ref[unit_of(i, c)] = attend.astype(BF16)
                yield

    def doublings(some):
        units = [(i, c) for i in some for c in range(2)]
        for unit in units:
            inverse[unit] = jnp.where(diagonal, 1.0, 0.0) - mix_ref[unit_of(*unit), 0].astype(F32)
        for n in range(1, len(LEVELS)):
            own = {unit: inverse[unit].astype(BF16) for unit in units}
            left_part = {}
            for unit in units:
                left_part[unit] = mm(own[unit], mix_ref[unit_of(*unit), n]).astype(BF16)
            yield
            for unit in units:
                inverse[unit] = inverse[unit] - mm(left_part[unit], own[unit])
            yield
        for unit in units:
            inverse[unit] = inverse[unit].astype(BF16)

    parts = {}

    def maps_of(some):
        n = len(LEVELS)
        units = [(i, c) for i in some for c in range(2)]
        rise = {u: e_ref[u[1], n * HALF : (n + 1) * HALF, lanes_of[u[0]]] for u in units}
        fall = {u: e_ref[u[1], (n + 1) * HALF : (n + 2) * HALF, lanes_of[u[0]]] for u in units}
        whole = {u: rise[u][HALF - 1 : HALF] for u in units}
        k_rise = {u: k_ref[rows_of[u[1]], lanes_of[u[0]]] * rise[u] for u in units}
        k_fall = {
            u: k_ref[rows_of[u[1]], lanes_of[u[0]]] * fall[u] * strength[u] for u in units
        }
        cross, first, second = {}, {}, {}
        for i in some:
            cross[i] = mm(k_rise[i, 1], k_fall[i, 0], ((1,), (1,))).astype(BF16)
        for i in some:
            first[i] = mm(
                inverse[i, 0],
                jnp.concatenate([v_ref[rows_of[0], lanes_of[i]], k_rise[i, 0]], axis=1),
            ).astype(BF16)
        yield
        late_part = {i: mm(cross[i], first[i]) for i in some}
        yield
        for i in some:
            start = jnp.concatenate(
                [v_ref[rows_of[1], lanes_of[i]], k_rise[i, 1] * whole[i, 0]], axis=1
            )
            second[i] = mm(inverse[i, 1], start - late_part[i]).astype(BF16)
        yield
        for i in some:
            stop = jnp.concatenate(
                [k_fall[i, 0] * whole[i, 1], k_fall[i, 1]], axis=0
            ).astype(BF16)
            maps = mm(jnp.concatenate([first[i], second[i]], axis=0), stop, ((0,), (0,)))
            move = jnp.where(diagonal, whole[i, 0] * whole[i, 1], 0.0) - maps[128:]
            z_ref[i, 0:128] = move.astype(BF16)
            z_ref[i, 128:256] = maps[:128].astype(BF16)
            parts[i] = (rise, whole, first, second, k_fall)

    def outputs_of(some):
        for i in some:
            rise, whole, first, second, k_fall = parts[i]
            lanes = lanes_of[i]
            q_rise = {
                (i, c): q_ref[rows_of[c], lanes] * rise[i, c] for c in range(2)
            }
            cross = mm(q_rise[i, 1], k_fall[i, 0], ((1,), (1,)))
            out = [
                mm(attend_ref[unit_of(i, 0)], first[i]),
                mm(cross, first[i]) + mm(attend_ref[unit_of(i, 1)], second[i]),
            ]
            for c in range(2):
                o_ref[rows_of[c], lanes] = out[c][:, :128]
            r_ref[rows_of[0], lanes] = (q_rise[i, 0] - out[0][:, 128:]).astype(BF16)
            r_ref[rows_of[1], lanes] = (
                q_rise[i, 1] * whole[i, 0] - out[1][:, 128:]
            ).astype(BF16)
            yield

    def send_maps(some):
        for i in some:

            @pl.when(p != 2 * i)
            def _():
                to_owner(i).start()

    def together(main, other, share):
        for _ in main:
            for _ in range(share):
                next(other, None)

    def finish(*works):
        for work in works:
            for _ in work:
                pass

    early, late_heads = range(0, heads, 2), range(1, heads, 2)
    finish(mixes(early))
    other = mixes(late_heads)
    together(doublings(early), other, 3)
    finish(other)
    other = doublings(late_heads)
    together(maps_of(early), other, 1)
    send_maps(early)
    finish(other, maps_of(late_heads))
    send_maps(late_heads)
    for some in (early, late_heads):
        finish(attends(some), outputs_of(some))

    def to_group(k, at):
        return pltpu.make_async_remote_copy(
            src_ref=total.at[at],
            dst_ref=zall.at[rank, at],
            send_sem=b_send.at[k],
            recv_sem=b_recv.at[rank],
            device_id={"seq": (group * GROUP + k) * PLANE + p},
            device_id_type=MESH,
        )

    def from_group(k, at):
        return pltpu.make_async_remote_copy(
            src_ref=total.at[at],
            dst_ref=zall.at[k, at],
            send_sem=b_send.at[k],
            recv_sem=b_recv.at[k],
            device_id={"seq": s},
            device_id_type=MESH,
        )

    def to_next(k):
        target = jnp.where(rank == 0, 2 * GROUP - 1, 2 * GROUP - 2 - k)
        return pltpu.make_async_remote_copy(
            src_ref=chain,
            dst_ref=held,
            send_sem=f_sem.at[k],
            recv_sem=f_sem.at[3],
            device_id={"seq": target * PLANE + p},
            device_id_type=MESH,
        )

    def feed(act):
        @pl.when(feeds)
        def _():
            act(to_next(0))

        @pl.when(jnp.logical_and(feeds, rank > 0))
        def _():
            for k in range(1, GROUP - 1):
                act(to_next(k))

    def prefix_to(q):
        return pltpu.make_async_remote_copy(
            src_ref=pre.at[q],
            dst_ref=lead.at[y],
            send_sem=g_send.at[q],
            recv_sem=g_recv.at[y],
            device_id={"seq": base + q},
            device_id_type=MESH,
        )

    def entry_to(q):
        return pltpu.make_async_remote_copy(
            src_ref=entry,
            dst_ref=state.at[y],
            send_sem=c_send.at[q],
            recv_sem=c_recv.at[y],
            device_id={"seq": base + q},
            device_id_type=MESH,
        )

    def landed(ref, sem, k):
        pltpu.make_async_remote_copy(
            src_ref=ref.at[k],
            dst_ref=ref.at[k],
            send_sem=sem.at[k],
            recv_sem=sem.at[k],
            device_id={"seq": s},
            device_id_type=MESH,
        ).wait_recv()

    everything, shift_only = pl.ds(0, 256), pl.ds(128, 128)
    half_plane = PLANE // 2

    def join(one, two):
        step = mm(one, two[:128])
        return jnp.concatenate(
            [step[:128].astype(BF16), (step[128:] + two[128:].astype(F32)).astype(BF16)], axis=0
        )

    def moved(state_in, both):
        return (mm(state_in, both[0:128]) + both[128:256].astype(F32)).astype(BF16)

    def group_copies(act):
        for k in range(GROUP):
            @pl.when(jnp.logical_and(jnp.logical_and(group == 0, rank == 0), k > 0))
            def _():
                act(to_group(k, shift_only))

            wanted = k > rank
            if k == 0:
                wanted = jnp.logical_and(group == 0, rank > 0)
            else:
                wanted = jnp.logical_and(
                    wanted, jnp.logical_or(group == 1, rank > 0)
                )

            @pl.when(wanted)
            def _():
                act(to_group(k, everything))

    @pl.when(owner)
    def _():
        zin[p] = z_ref[y]
        for k in range(PLANE):

            @pl.when(p != k)
            def _():
                landed(zin, a_recv, k)

        one, two = zin[0], zin[half_plane]
        later = {}
        for k in range(1, half_plane):
            pre[k], later[half_plane + k] = one, two
            one, two = join(one, zin[k]), join(two, zin[half_plane + k])
        pre[half_plane] = one
        whole_map = join(one, two)
        total[...] = whole_map
        group_copies(lambda copy: copy.start())
        zall[rank] = whole_map
        for k in range(half_plane + 1, PLANE):
            pre[k] = join(one, later[k])
        for d in FAR_FIRST:
            q = lax.rem(p + d, PLANE)

            @pl.when(q > 0)
            def _():
                prefix_to(q).start()

        @pl.when(p > 0)
        def _():
            lead[y] = pre[p]

        @pl.when(group == 0)
        def _():
            chain[...] = jnp.zeros_like(chain)
            entry[...] = jnp.zeros_like(entry)
            for k in range(GROUP):
                needed = jnp.logical_or(feeds, k < rank)
                if k == 0:

                    @pl.when(rank > 0)
                    def _():
                        from_group(0, shift_only).wait_recv()

                else:

                    @pl.when(jnp.logical_and(needed, rank != k))
                    def _():
                        from_group(k, everything).wait_recv()

                @pl.when(rank == k)
                def _():
                    entry[...] = chain[...]

                @pl.when(needed)
                def _():
                    if k == 0:
                        chain[...] = zall[0, 128:256]
                    else:
                        chain[...] = moved(chain[...], zall[k])

            feed(lambda copy: copy.start())

        @pl.when(group == 1)
        def _():
            for k in range(GROUP - 1):

                @pl.when(k < rank)
                def _():
                    from_group(k, everything).wait_recv()
                    if k == 0:
                        link[...] = zall[0]
                    else:
                        link[...] = join(link[...], zall[k])

            to_next(0).wait_recv()

            @pl.when(rank == 0)
            def _():
                entry[...] = held[...]

            @pl.when(rank > 0)
            def _():
                entry[...] = moved(held[...], link[...])

        @pl.when(z > 0)
        def _():
            for d in ENTRIES:
                entry_to(lax.rem(p + d, PLANE)).start()

            state[y] = entry[...]

    @pl.when(z == 0)
    def _():
        state[...] = jnp.zeros_like(state)

    @pl.when(p > 0)
    def _():
        for i in range(heads):

            @pl.when(p != 2 * i)
            def _():
                landed(lead, g_recv, i)

        for i in range(heads):
            lanes = lanes_of[i]
            both = mm(r_ref[:, lanes], lead[i], ((1,), (1,)))
            o_ref[:, lanes] = o_ref[:, lanes] + both[:, 128:]
            r_ref[:, lanes] = both[:, :128].astype(BF16)

    after_own = lax.rem(y + 1, heads)
    passes_on = jnp.logical_and(core == 1, z > 0)
    passed = pltpu.make_async_remote_copy(
        src_ref=state.at[after_own],
        dst_ref=state.at[after_own],
        send_sem=c_send.at[0],
        recv_sem=c_recv.at[after_own],
        device_id={"seq": base + lax.rem(p + PLANE - 2, PLANE)},
        device_id_type=MESH,
    )
    for d in (1, 0, 3, 2):
        i = lax.rem(y + d, heads)

        @pl.when(jnp.logical_and(p != 2 * i, z > 0))
        def _():
            landed(state, c_recv, i)

        if d == 1:

            @pl.when(passes_on)
            def _():
                passed.start()

        lanes = pl.ds(pl.multiple_of(i * 128, 128), 128)
        attended = o_ref[:, lanes] + mm(r_ref[:, lanes], state[i], ((1,), (1,)))
        scale = lax.rsqrt(jnp.mean(attended * attended, axis=1, keepdims=True) + 1e-05)
        normed[:, lanes] = (attended * scale * gain_ref[...] * gate_ref[:, lanes]).astype(BF16)
    loads[14].wait()


    def partial(to):
        at = pl.ds(pl.multiple_of(to * rows, 16), rows)
        return jnp.dot(normed[at, :], ow_ref[...], preferred_element_type=F32)

    def pass_on(k, src, dst, target):
        return pltpu.make_async_remote_copy(
            src_ref=src,
            dst_ref=dst,
            send_sem=d_send.at[k],
            recv_sem=d_recv.at[k],
            device_id={"head": target},
            device_id_type=MESH,
        )

    top, low = pl.ds(0, half), pl.ds(half, half)
    part[0] = partial(far).astype(BF16)
    far_right = pass_on(0, part.at[0, top], inbox.at[0, top], right)
    far_left = pass_on(1, part.at[0, low], inbox.at[0, low], left)
    far_right.start()
    far_left.start()
    sums[0] = partial(right)
    part[1, low] = sums[0, low].astype(BF16)
    right_low = pass_on(2, part.at[1, low], inbox.at[1, low], right)
    right_low.start()
    sums[1] = partial(left)
    part[2, top] = sums[1, top].astype(BF16)
    left_top = pass_on(3, part.at[2, top], inbox.at[2, top], left)
    left_top.start()
    far_right.wait_recv()
    part[1, top] = (sums[0, top] + inbox[0, top].astype(F32)).astype(BF16)
    right_top = pass_on(4, part.at[1, top], inbox.at[1, top], right)
    right_top.start()
    far_left.wait_recv()
    part[2, low] = (sums[1, low] + inbox[0, low].astype(F32)).astype(BF16)
    left_low = pass_on(5, part.at[2, low], inbox.at[2, low], left)
    left_low.start()
    own = partial(h)
    right_low.wait_recv()
    left_top.wait_recv()
    right_top.wait_recv()
    left_low.wait_recv()
    out_ref[...] = (own + inbox[1].astype(F32) + inbox[2].astype(F32)).astype(BF16)

    for copy in (far_right, far_left, right_low, left_top, right_top, left_low):
        copy.wait_send()
    for n in (0, 1, 4, 5):
        moves[n].wait_send()

    for head in (0, 2, 3):
        each_edge(head, lambda copy: copy.wait_send())

    for i in range(heads):

        @pl.when(p != 2 * i)
        def _():
            to_owner(i).wait_send()

    @pl.when(owner)
    def _():
        group_copies(lambda copy: copy.wait_send())

        feed(lambda copy: copy.wait_send())

        for d in FAR_FIRST:
            q = lax.rem(p + d, PLANE)

            @pl.when(q > 0)
            def _():
                prefix_to(q).wait_send()

        @pl.when(z > 0)
        def _():
            for d in ENTRIES:
                entry_to(lax.rem(p + d, PLANE)).wait_send()

    @pl.when(passes_on)
    def _():
        passed.wait_send()


def layer(depth, x, w, down, gdown, beta, up, gup, conv, dlog, bias, span, gain, ow):
    vmem = pl.BlockSpec(memory_space=pltpu.VMEM)
    hbm = pl.BlockSpec(memory_space=pl.ANY)
    rows, model = x.shape
    count, width = 4 * rows, w.shape[2]
    heads = width // 128
    dma = pltpu.SemaphoreType.DMA
    return pl.pallas_call(
        functools.partial(kernel, depth),
        name="layer",
        out_shape=pltpu.VMEM((rows, model), BF16),
        in_specs=[hbm] * 13,
        out_specs=vmem,
        scratch_shapes=[
            pltpu.VMEM((count + HALO, model), BF16),
            pltpu.VMEM(w.shape, BF16),
            pltpu.VMEM((model, 256), BF16),
            pltpu.VMEM(beta.shape, BF16),
            pltpu.VMEM(up.shape, BF16),
            pltpu.VMEM(gup.shape, BF16),
            pltpu.VMEM(conv.shape, BF16),
            pltpu.SMEM(dlog.shape, F32),
            pltpu.VMEM(bias.shape, F32),
            pltpu.VMEM(span.shape, BF16),
            pltpu.VMEM(gain.shape, F32),
            pltpu.VMEM(ow.shape, BF16),
            pltpu.VMEM((3, HALO + count, width), F32),
            pltpu.VMEM((count, width), F32),
            pltpu.VMEM((count, heads), F32),
            pltpu.VMEM((count, width), F32),
            pltpu.VMEM((count, width), F32),
            pltpu.VMEM((count, width), F32),
            pltpu.VMEM((2, (len(LEVELS) + 2) * HALF, width), F32),
            pltpu.VMEM((count, width), F32),
            pltpu.VMEM((count, width), BF16),
            pltpu.VMEM((count, width), F32),
            pltpu.VMEM((heads, 256, 128), BF16),
            pltpu.VMEM((2 * heads, len(LEVELS), HALF, HALF), BF16),
            pltpu.VMEM((2 * heads, len(LEVELS), HALF, 128), BF16),
            pltpu.VMEM((2 * heads, HALF, HALF), BF16),
            pltpu.VMEM((PLANE, 256, 128), BF16),
            pltpu.VMEM((PLANE, 256, 128), BF16),
            pltpu.VMEM((256, 128), BF16),
            pltpu.VMEM((GROUP, 256, 128), BF16),
            pltpu.VMEM((128, 128), BF16),
            pltpu.VMEM((256, 128), BF16),
            pltpu.VMEM((128, 128), BF16),
            pltpu.VMEM((128, 128), BF16),
            pltpu.VMEM((heads, 256, 128), BF16),
            pltpu.VMEM((heads, 128, 128), BF16),
            pltpu.VMEM((count, width), BF16),
            pltpu.VMEM((3, rows, model), BF16),
            pltpu.VMEM((2, rows, model), F32),
            pltpu.VMEM((3, rows, model), BF16),
            dma((15,)), dma((6,)), dma((6,)), dma((3,)), dma((4,)), dma((PLANE,)), dma((heads,)),
            dma((heads,)), dma((PLANE,)), dma((GROUP,)), dma((GROUP,)),
            dma((PLANE,)), dma((heads,)), dma((6,)), dma((6,)),
        ],
        compiler_params=pltpu.CompilerParams(
            collective_id=0, has_side_effects=True, vmem_limit_bytes=56 << 20
        ),
    )(x, w, down, gdown, beta, up, gup, conv, dlog, bias, span, gain, ow)


def solution(mesh):
    seq_size = mesh.shape["seq"]
    span = span_matrix()

    def shards(
        hidden_in, qkv_weight, conv_weight, decay_log, dt_bias, decay_down, decay_up,
        beta_weight, gate_down, gate_up, norm_gain, out_weight,
    ):
        return layer(
            seq_size // PLANE,
            hidden_in,
            jnp.transpose(qkv_weight, (1, 0, 2)),
            decay_down,
            gate_down,
            beta_weight.T,
            decay_up,
            gate_up,
            conv_weight,
            decay_log,
            dt_bias.reshape(1, -1),
            jnp.asarray(span, BF16),
            norm_gain.reshape(1, -1),
            out_weight,
        )

    rows = P(("seq", "head"), None)
    return jax.shard_map(
        shards,
        mesh=mesh,
        in_specs=(
            rows, P(None, None, "head"), P(None, None, "head"), P("head"), P("head"), P(),
            P(None, "head"), P(None, "head"), P(), P(None, "head"), P(), P("head", None),
        ),
        out_specs=rows,
        check_vma=False,
    )
```

```python
import functools

import jax
import jax.numpy as jnp
import numpy as np
from jax import lax
from jax.experimental import pallas as pl
from jax.experimental.pallas import tpu as pltpu
from jax.sharding import PartitionSpec as P

F32 = jnp.float32
BF16 = jnp.bfloat16
MESH = pl.DeviceIdType.MESH

HALO = 16
EDGE = 8
HALF = 128
LEVELS = (1, 2, 4, 8, 16, 32, 64)
PLANE = 8
GROUP = 4
FAR_FIRST = (4, 5, 2, 3, 6, 7, 1)
ENTRIES = (7, 4, 6, 2, 1, 3)


def span_matrix():
    r, i = np.arange(HALF)[:, None], np.arange(HALF)[None, :]
    rows = []
    for size in LEVELS:
        middle = (r // (2 * size)) * 2 * size + size - 1
        late = (r % (2 * size)) >= size
        rows.append(np.where(late, (i > middle) & (i <= r), (i > r) & (i <= middle)))
    rows.append(i <= r)
    rows.append(i > r)
    spans = np.concatenate(rows, axis=0)
    return np.concatenate([spans, spans], axis=1).astype(np.float32)


def mm(a, b, dims=((1,), (0,))):
    return lax.dot_general(
        a.astype(BF16), b.astype(BF16), (dims, ((), ())), preferred_element_type=F32
    )


def sigmoid(v):
    return 1.0 / (1.0 + jnp.exp(-v))


def kernel(
    depth, x_hbm, w_hbm, down_hbm, gdown_hbm, beta_hbm, up_hbm, gup_hbm, conv_hbm, dlog_hbm,
    bias_hbm, span_hbm, gain_hbm, ow_hbm, out_ref,
    x_ref, w_ref, dg_ref, beta_ref, up_ref, gup_ref, conv_ref, dlog_ref, bias_ref, span_ref,
    gain_ref, ow_ref,
    proj_ref, fade_ref, strength_ref, q_ref, k_ref, v_ref, e_ref, o_ref, r_ref, gate_ref, z_ref,
    mix_ref, faded_ref, attend_ref, zin, pre, total, zall, chain, link, held, entry, lead, state, normed, part, sums, inbox,
    l_sem, x_send, x_recv, e_sem, f_sem, g_send, g_recv,
    a_send, a_recv, b_send, b_recv, c_send, c_recv, d_send, d_recv,
):
    s = lax.axis_index("seq")
    h = lax.axis_index("head")
    z = lax.div(s, PLANE)
    p = lax.rem(s, PLANE)
    y, core = lax.div(p, 2), lax.rem(p, 2)
    base = z * PLANE
    right, left, far = lax.rem(h + 1, 4), lax.rem(h + 3, 4), lax.rem(h + 2, 4)
    owner = core == 0
    group, rank = lax.div(z, GROUP), lax.rem(z, GROUP)
    feeds = jnp.logical_and(group == 0, jnp.logical_or(rank == 0, rank == GROUP - 1))
    has_next = s < depth * PLANE - 1
    edge_from = jnp.where(h == 1, 2, h)
    rows = x_hbm.shape[0]
    half = rows // 2
    count = 4 * rows
    width = w_ref.shape[2]
    heads = width // 128

    barrier = pltpu.get_barrier_semaphore()
    pl.semaphore_signal(barrier, 1, device_id={"head": right}, device_id_type=MESH)
    pl.semaphore_signal(barrier, 1, device_id={"head": left}, device_id_type=MESH)

    @pl.when(s > 0)
    def _():
        pl.semaphore_signal(
            barrier, 1, device_id={"seq": s - 1, "head": edge_from}, device_id_type=MESH
        )

    for d in range(1, PLANE):
        q = lax.rem(p + d, PLANE)

        @pl.when(jnp.logical_or(owner, lax.rem(q, 2) == 0))
        def _():
            pl.semaphore_signal(barrier, 1, device_id={"seq": base + q}, device_id_type=MESH)

    @pl.when(core == 1)
    def _():
        pl.semaphore_signal(
            barrier, 1, device_id={"seq": base + lax.rem(p + 2, PLANE)}, device_id_type=MESH
        )

    @pl.when(owner)
    def _():
        for d in range(1, GROUP):
            other = group * GROUP + lax.rem(rank + d, GROUP)
            pl.semaphore_signal(
                barrier, 1, device_id={"seq": other * PLANE + p}, device_id_type=MESH
            )

        @pl.when(group == 1)
        def _():
            feeder = jnp.where(rank < GROUP - 1, GROUP - 1, 0)
            pl.semaphore_signal(
                barrier, 1, device_id={"seq": feeder * PLANE + p}, device_id_type=MESH
            )

    greeted = (
        2
        + jnp.where(owner, PLANE - 1 + GROUP - 1, PLANE // 2 + 1)
        + jnp.where(jnp.logical_and(owner, feeds), jnp.where(rank == 0, 1, GROUP - 1), 0)
        + jnp.where(has_next, jnp.where(h == 2, 2, jnp.where(h == 1, 0, 1)), 0)
    )

    loads = [
        pltpu.make_async_copy(src, dst, l_sem.at[k])
        for k, (src, dst) in enumerate(
            [
                (x_hbm, x_ref.at[pl.ds(0, rows)]),
                (w_hbm.at[0], w_ref.at[0]),
                (w_hbm.at[1], w_ref.at[1]),
                (w_hbm.at[2], w_ref.at[2]),
                (down_hbm, dg_ref.at[:, pl.ds(0, 128)]),
                (gdown_hbm, dg_ref.at[:, pl.ds(128, 128)]),
                (beta_hbm, beta_ref),
                (up_hbm, up_ref),
                (gup_hbm, gup_ref),
                (conv_hbm, conv_ref),
                (dlog_hbm, dlog_ref),
                (bias_hbm, bias_ref),
                (gain_hbm, gain_ref),
                (span_hbm, span_ref),
                (ow_hbm, ow_ref),
            ]
        )
    ]
    for load in loads:
        load.start()
    x_ref[count + EDGE :, :] = jnp.zeros((HALO - EDGE, x_ref.shape[1]), BF16)

    @pl.when(s == 0)
    def _():
        x_ref[count : count + EDGE, :] = jnp.zeros((EDGE, x_ref.shape[1]), BF16)

    pl.semaphore_wait(barrier, greeted)

    def piece(src, slot, half_at, target, k):
        return pltpu.make_async_remote_copy(
            src_ref=src,
            dst_ref=x_ref.at[pl.ds(slot * rows + half_at * half, half)],
            send_sem=x_send.at[k],
            recv_sem=x_recv.at[k],
            device_id={"head": target},
            device_id_type=MESH,
        )

    def rows_at(slot, half_at):
        return x_ref.at[pl.ds(slot * rows + half_at * half, half)]

    loads[0].wait()
    mine = [rows_at(0, 0), rows_at(0, 1)]
    moves = [
        piece(mine[0], 1, 0, right, 0),
        piece(mine[1], 2, 1, left, 1),
        piece(mine[1], 1, 1, right, 2),
        piece(mine[0], 2, 0, left, 3),
        piece(rows_at(1, 0), 3, 0, right, 4),
        piece(rows_at(2, 1), 3, 1, left, 5),
    ]
    for move in moves[:4]:
        move.start()

    def edge(k, src, target):
        return pltpu.make_async_remote_copy(
            src_ref=src,
            dst_ref=x_ref.at[pl.ds(count, EDGE)],
            send_sem=e_sem.at[k],
            recv_sem=e_sem.at[2],
            device_id={"seq": s + 1, "head": target},
            device_id_type=MESH,
        )

    last = pl.ds(rows - EDGE, EDGE)
    edges = {
        3: [edge(0, x_ref.at[last], 3)],
        0: [edge(0, x_ref.at[pl.ds(2 * rows - EDGE, EDGE)], 0)],
        2: [
            edge(0, x_ref.at[pl.ds(3 * rows - EDGE, EDGE)], 2),
            edge(1, x_ref.at[pl.ds(3 * rows - EDGE, EDGE)], 1),
        ],
    }

    def each_edge(head, act):
        @pl.when(jnp.logical_and(h == head, has_next))
        def _():
            for copy in edges[head]:
                act(copy)

    each_edge(3, lambda copy: copy.start())
    for load in loads[1:14]:
        load.wait()

    rate = jnp.concatenate(
        [jnp.exp(jnp.full((1, 128), dlog_ref[i], F32)) for i in range(heads)], axis=1
    )

    def project(first, slots):
        size = len(slots) * rows
        at = [pl.ds(pl.multiple_of(slot * rows, 16), rows) for slot in slots]
        some = x_ref[first : first + size, :]
        both = jnp.dot(some, dg_ref[...], preferred_element_type=F32).astype(BF16)
        force = sigmoid(
            lax.dot_general(
                some, beta_ref[...], (((1,), (1,)), ((), ())), preferred_element_type=F32
            )
        )
        raw = jnp.dot(both[:, 0:128], up_ref[...], preferred_element_type=F32) + bias_ref[...]
        soft = jnp.maximum(raw, 0.0) + jnp.log1p(jnp.exp(-jnp.abs(raw)))
        log_decay = -rate * soft
        gate = sigmoid(jnp.dot(both[:, 128:256], gup_ref[...], preferred_element_type=F32))
        for n, where in enumerate(at):
            own = slice(n * rows, (n + 1) * rows)
            fade_ref[where, :] = log_decay[own]
            gate_ref[where, :] = gate[own]
            strength_ref[where, :] = force[own]

    def project_qkv(c, first, slots, tail):
        size = len(slots) * rows
        some = x_ref[first : first + size + tail, :]
        got = jnp.dot(some, w_ref[c], preferred_element_type=F32).astype(BF16).astype(F32)
        for n, slot in enumerate(slots):
            at = pl.ds(pl.multiple_of(HALO + slot * rows, 16), rows)
            proj_ref[c, at, :] = got[n * rows : (n + 1) * rows]
        if tail:
            proj_ref[c, HALO - EDGE : HALO, :] = got[size : size + EDGE]

    def decays(c):
        piece_of = fade_ref[pl.ds(pl.multiple_of(c * HALF, HALF), HALF), :]
        top = piece_of.astype(BF16)
        rest = (piece_of - top.astype(F32)).astype(BF16)
        e_ref[c] = jnp.exp(
            jnp.dot(
                span_ref[...], jnp.concatenate([top, rest], axis=0), preferred_element_type=F32
            )
        )

    project(0, (h,))
    for c in range(3):
        project_qkv(c, 0, (h,), 0)

    moves[0].wait_recv()
    moves[2].wait_send()
    moves[4].start()
    moves[1].wait_recv()
    moves[3].wait_send()
    moves[5].start()
    each_edge(2, lambda copy: copy.start())
    moves[2].wait_recv()
    each_edge(0, lambda copy: copy.start())
    moves[3].wait_recv()

    near = (left, right)
    project(rows, near)
    for c in range(3):
        project_qkv(c, rows, near, 0)
    far_square = lax.div(far, 2)
    decays(1 - far_square)
    moves[4].wait_recv()
    moves[5].wait_recv()

    @pl.when(s > 0)
    def _():
        edges[0][0].wait_recv()

    def convolve(c):
        target = (q_ref, k_ref, v_ref)[c]
        taps = conv_ref[c].astype(F32)
        mixed = proj_ref[c, pl.ds(HALO - 3, count), :] * taps[0:1]
        for i in range(1, 4):
            mixed = mixed + proj_ref[c, pl.ds(HALO - 3 + i, count), :] * taps[i : i + 1]
        mixed = (mixed * sigmoid(mixed)).astype(BF16).astype(F32)
        if c == 2:
            target[...] = mixed
            return
        for i in range(heads):
            lanes = slice(i * 128, (i + 1) * 128)
            u = mixed[:, lanes]
            scale = lax.rsqrt(jnp.sum(u * u, axis=1, keepdims=True) + 1e-06)
            if c == 0:
                scale = scale * (128**-0.5)
            target[:, lanes] = u * scale

    project(3 * rows, (far,))
    project_qkv(1, 3 * rows, (far,), HALO)
    decays(far_square)
    project_qkv(0, 3 * rows, (far,), HALO)
    convolve(1)
    project_qkv(2, 3 * rows, (far,), HALO)
    convolve(0)
    convolve(2)
    beta = strength_ref[...]

    t = lax.broadcasted_iota(jnp.int32, (HALF, HALF), 0)
    j = lax.broadcasted_iota(jnp.int32, (HALF, HALF), 1)
    row = lax.broadcasted_iota(jnp.int32, (HALF, 128), 0)
    masks = [
        ((t ^ j) >= size) & ((t ^ j) < 2 * size) & (t > j) for size in LEVELS
    ]
    diagonal = t == j

    lanes_of = [slice(i * 128, (i + 1) * 128) for i in range(heads)]
    rows_of = [slice(c * HALF, (c + 1) * HALF) for c in range(2)]

    def to_owner(i):
        return pltpu.make_async_remote_copy(
            src_ref=z_ref.at[i],
            dst_ref=zin.at[p],
            send_sem=a_send.at[i],
            recv_sem=a_recv.at[p],
            device_id={"seq": base + 2 * i},
            device_id_type=MESH,
        )

    strength, written, inverse = {}, {}, {}

    def unit_of(i, c):
        return 2 * i + c

    def mix(i, c, n):
        kc = k_ref[rows_of[c], lanes_of[i]]
        if n == 0:
            strength[i, c] = jnp.broadcast_to(beta[rows_of[c], i : i + 1], (HALF, 128))
            written[i, c] = kc * strength[i, c]
        fade = e_ref[c, n * HALF : (n + 1) * HALF, lanes_of[i]]
        size = LEVELS[n]
        if size < 8:
            chosen = jnp.where((row & size) != 0, kc, written[i, c])
        else:
            chosen = jnp.concatenate(
                [
                    (kc if at & size else written[i, c])[at : at + size]
                    for at in range(0, HALF, size)
                ],
                axis=0,
            )
        kx = (chosen * fade).astype(BF16)
        faded_ref[unit_of(i, c), n] = kx
        mix_ref[unit_of(i, c), n] = jnp.where(masks[n], mm(kx, kx, ((1,), (1,))), 0.0).astype(BF16)

    def mixes(some):
        for i in some:
            for c in range(2):
                for n in range(len(LEVELS)):
                    mix(i, c, n)
                    yield

    def attends(some):
        for i in some:
            for c in range(2):
                kc, qc = k_ref[rows_of[c], lanes_of[i]], q_ref[rows_of[c], lanes_of[i]]
                own = jnp.sum(qc * kc, axis=1, keepdims=True) * strength[i, c]
                attend = jnp.where(diagonal, own, 0.0)
                for n in range(len(LEVELS)):
                    qx = qc * e_ref[c, n * HALF : (n + 1) * HALF, lanes_of[i]]
                    both = mm(qx, faded_ref[unit_of(i, c), n], ((1,), (1,)))
                    attend = jnp.where(masks[n], both, attend)
                attend_ref[unit_of(i, c)] = attend.astype(BF16)
                yield

    def doublings(some):
        units = [(i, c) for i in some for c in range(2)]
        for unit in units:
            inverse[unit] = jnp.where(diagonal, 1.0, 0.0) - mix_ref[unit_of(*unit), 0].astype(F32)
        for n in range(1, len(LEVELS)):
            own = {unit: inverse[unit].astype(BF16) for unit in units}
            left_part = {}
            for unit in units:
                left_part[unit] = mm(own[unit], mix_ref[unit_of(*unit), n]).astype(BF16)
            yield
            for unit in units:
                inverse[unit] = inverse[unit] - mm(left_part[unit], own[unit])
            yield
        for unit in units:
            inverse[unit] = inverse[unit].astype(BF16)

    parts = {}

    def maps_of(some):
        n = len(LEVELS)
        units = [(i, c) for i in some for c in range(2)]
        rise = {u: e_ref[u[1], n * HALF : (n + 1) * HALF, lanes_of[u[0]]] for u in units}
        fall = {u: e_ref[u[1], (n + 1) * HALF : (n + 2) * HALF, lanes_of[u[0]]] for u in units}
        whole = {u: rise[u][HALF - 1 : HALF] for u in units}
        k_rise = {u: k_ref[rows_of[u[1]], lanes_of[u[0]]] * rise[u] for u in units}
        k_fall = {
            u: written[u] * fall[u] for u in units
        }
        cross, first, second = {}, {}, {}
        for i in some:
            cross[i] = mm(k_rise[i, 1], k_fall[i, 0], ((1,), (1,))).astype(BF16)
        for i in some:
            first[i] = mm(
                inverse[i, 0],
                jnp.concatenate([v_ref[rows_of[0], lanes_of[i]], k_rise[i, 0]], axis=1),
            ).astype(BF16)
        yield
        late_part = {i: mm(cross[i], first[i]) for i in some}
        yield
        for i in some:
            start = jnp.concatenate(
                [v_ref[rows_of[1], lanes_of[i]], k_rise[i, 1] * whole[i, 0]], axis=1
            )
            second[i] = mm(inverse[i, 1], start - late_part[i]).astype(BF16)
        yield
        for i in some:
            stop = jnp.concatenate(
                [k_fall[i, 0] * whole[i, 1], k_fall[i, 1]], axis=0
            ).astype(BF16)
            maps = mm(jnp.concatenate([first[i], second[i]], axis=0), stop, ((0,), (0,)))
            move = jnp.where(diagonal, whole[i, 0] * whole[i, 1], 0.0) - maps[128:]
            z_ref[i, 0:128] = move.astype(BF16)
            z_ref[i, 128:256] = maps[:128].astype(BF16)
            parts[i] = (rise, whole, first, second, k_fall)

    def outputs_of(some):
        for i in some:
            rise, whole, first, second, k_fall = parts[i]
            lanes = lanes_of[i]
            q_rise = {
                (i, c): q_ref[rows_of[c], lanes] * rise[i, c] for c in range(2)
            }
            cross = mm(q_rise[i, 1], k_fall[i, 0], ((1,), (1,)))
            out = [
                mm(attend_ref[unit_of(i, 0)], first[i]),
                mm(cross, first[i]) + mm(attend_ref[unit_of(i, 1)], second[i]),
            ]
            for c in range(2):
                o_ref[rows_of[c], lanes] = out[c][:, :128]
            r_ref[rows_of[0], lanes] = (q_rise[i, 0] - out[0][:, 128:]).astype(BF16)
            r_ref[rows_of[1], lanes] = (
                q_rise[i, 1] * whole[i, 0] - out[1][:, 128:]
            ).astype(BF16)
            yield

    def send_maps(some):
        for i in some:

            @pl.when(p != 2 * i)
            def _():
                to_owner(i).start()

    def together(main, other, share):
        for _ in main:
            for _ in range(share):
                next(other, None)

    def finish(*works):
        for work in works:
            for _ in work:
                pass

    early, late_heads = range(0, heads, 2), range(1, heads, 2)
    finish(mixes(early))
    other = mixes(late_heads)
    together(doublings(early), other, 3)
    finish(other)
    other = doublings(late_heads)
    together(maps_of(early), other, 1)
    send_maps(early)
    finish(other, maps_of(late_heads))
    send_maps(late_heads)
    for some in (early, late_heads):
        finish(attends(some), outputs_of(some))

    def to_group(k, at):
        return pltpu.make_async_remote_copy(
            src_ref=total.at[at],
            dst_ref=zall.at[rank, at],
            send_sem=b_send.at[k],
            recv_sem=b_recv.at[rank],
            device_id={"seq": (group * GROUP + k) * PLANE + p},
            device_id_type=MESH,
        )

    def from_group(k, at):
        return pltpu.make_async_remote_copy(
            src_ref=total.at[at],
            dst_ref=zall.at[k, at],
            send_sem=b_send.at[k],
            recv_sem=b_recv.at[k],
            device_id={"seq": s},
            device_id_type=MESH,
        )

    def to_next(k):
        target = jnp.where(rank == 0, 2 * GROUP - 1, 2 * GROUP - 2 - k)
        return pltpu.make_async_remote_copy(
            src_ref=chain,
            dst_ref=held,
            send_sem=f_sem.at[k],
            recv_sem=f_sem.at[3],
            device_id={"seq": target * PLANE + p},
            device_id_type=MESH,
        )

    def feed(act):
        @pl.when(feeds)
        def _():
            act(to_next(0))

        @pl.when(jnp.logical_and(feeds, rank > 0))
        def _():
            for k in range(1, GROUP - 1):
                act(to_next(k))

    def prefix_to(q):
        return pltpu.make_async_remote_copy(
            src_ref=pre.at[q],
            dst_ref=lead.at[y],
            send_sem=g_send.at[q],
            recv_sem=g_recv.at[y],
            device_id={"seq": base + q},
            device_id_type=MESH,
        )

    def entry_to(q):
        return pltpu.make_async_remote_copy(
            src_ref=entry,
            dst_ref=state.at[y],
            send_sem=c_send.at[q],
            recv_sem=c_recv.at[y],
            device_id={"seq": base + q},
            device_id_type=MESH,
        )

    def landed(ref, sem, k):
        pltpu.make_async_remote_copy(
            src_ref=ref.at[k],
            dst_ref=ref.at[k],
            send_sem=sem.at[k],
            recv_sem=sem.at[k],
            device_id={"seq": s},
            device_id_type=MESH,
        ).wait_recv()

    everything, shift_only = pl.ds(0, 256), pl.ds(128, 128)
    half_plane = PLANE // 2

    def join(one, two):
        step = mm(one, two[:128])
        return jnp.concatenate(
            [step[:128].astype(BF16), (step[128:] + two[128:].astype(F32)).astype(BF16)], axis=0
        )

    def moved(state_in, both):
        return (mm(state_in, both[0:128]) + both[128:256].astype(F32)).astype(BF16)

    def group_copies(act):
        for k in (3, 0, 2, 1):
            @pl.when(jnp.logical_and(jnp.logical_and(group == 0, rank == 0), k > 0))
            def _():
                act(to_group(k, shift_only))

            wanted = k > rank
            if k == 0:
                wanted = jnp.logical_and(group == 0, rank > 0)
            else:
                wanted = jnp.logical_and(
                    wanted, jnp.logical_or(group == 1, rank > 0)
                )

            @pl.when(wanted)
            def _():
                act(to_group(k, everything))

    @pl.when(owner)
    def _():
        zin[p] = z_ref[y]
        for k in range(PLANE):

            @pl.when(p != k)
            def _():
                landed(zin, a_recv, k)

        one, two = zin[0], zin[half_plane]
        later = {}
        for k in range(1, half_plane):
            pre[k], later[half_plane + k] = one, two
            one, two = join(one, zin[k]), join(two, zin[half_plane + k])
        pre[half_plane] = one
        whole_map = join(one, two)
        total[...] = whole_map
        group_copies(lambda copy: copy.start())
        zall[rank] = whole_map
        for k in range(half_plane + 1, PLANE):
            pre[k] = join(one, later[k])
        for d in FAR_FIRST:
            q = lax.rem(p + d, PLANE)

            @pl.when(q > 0)
            def _():
                prefix_to(q).start()

        @pl.when(p > 0)
        def _():
            lead[y] = pre[p]

        @pl.when(group == 0)
        def _():
            chain[...] = jnp.zeros_like(chain)
            entry[...] = jnp.zeros_like(entry)
            for k in range(GROUP):
                needed = jnp.logical_or(feeds, k < rank)
                if k == 0:

                    @pl.when(rank > 0)
                    def _():
                        from_group(0, shift_only).wait_recv()

                else:

                    @pl.when(jnp.logical_and(needed, rank != k))
                    def _():
                        from_group(k, everything).wait_recv()

                @pl.when(rank == k)
                def _():
                    entry[...] = chain[...]

                @pl.when(needed)
                def _():
                    if k == 0:
                        chain[...] = zall[0, 128:256]
                    else:
                        chain[...] = moved(chain[...], zall[k])

            feed(lambda copy: copy.start())

        @pl.when(group == 1)
        def _():
            for k in range(GROUP - 1):

                @pl.when(k < rank)
                def _():
                    from_group(k, everything).wait_recv()
                    if k == 0:
                        link[...] = zall[0]
                    else:
                        link[...] = join(link[...], zall[k])

            to_next(0).wait_recv()

            @pl.when(rank == 0)
            def _():
                entry[...] = held[...]

            @pl.when(rank > 0)
            def _():
                entry[...] = moved(held[...], link[...])

        @pl.when(z > 0)
        def _():
            for d in ENTRIES:
                entry_to(lax.rem(p + d, PLANE)).start()

            state[y] = entry[...]

    @pl.when(z == 0)
    def _():
        state[...] = jnp.zeros_like(state)

    @pl.when(p > 0)
    def _():
        for i in range(heads):

            @pl.when(p != 2 * i)
            def _():
                landed(lead, g_recv, i)

        for i in range(heads):
            lanes = lanes_of[i]
            both = mm(r_ref[:, lanes], lead[i], ((1,), (1,)))
            o_ref[:, lanes] = o_ref[:, lanes] + both[:, 128:]
            r_ref[:, lanes] = both[:, :128].astype(BF16)

    after_own = lax.rem(y + 1, heads)
    passes_on = jnp.logical_and(core == 1, z > 0)
    passed = pltpu.make_async_remote_copy(
        src_ref=state.at[after_own],
        dst_ref=state.at[after_own],
        send_sem=c_send.at[0],
        recv_sem=c_recv.at[after_own],
        device_id={"seq": base + lax.rem(p + PLANE - 2, PLANE)},
        device_id_type=MESH,
    )
    for d in (0, 1, 3, 2):
        i = lax.rem(y + d, heads)

        @pl.when(jnp.logical_and(p != 2 * i, z > 0))
        def _():
            landed(state, c_recv, i)

        if d == 1:

            @pl.when(passes_on)
            def _():
                passed.start()

        lanes = pl.ds(pl.multiple_of(i * 128, 128), 128)
        attended = o_ref[:, lanes] + mm(r_ref[:, lanes], state[i], ((1,), (1,)))
        scale = lax.rsqrt(jnp.mean(attended * attended, axis=1, keepdims=True) + 1e-05)
        normed[:, lanes] = (attended * scale * gain_ref[...] * gate_ref[:, lanes]).astype(BF16)
    loads[14].wait()


    def partial(to):
        at = pl.ds(pl.multiple_of(to * rows, 16), rows)
        return jnp.dot(normed[at, :], ow_ref[...], preferred_element_type=F32)

    def pass_on(k, src, dst, target):
        return pltpu.make_async_remote_copy(
            src_ref=src,
            dst_ref=dst,
            send_sem=d_send.at[k],
            recv_sem=d_recv.at[k],
            device_id={"head": target},
            device_id_type=MESH,
        )

    top, low = pl.ds(0, half), pl.ds(half, half)
    part[0] = partial(far).astype(BF16)
    far_right = pass_on(0, part.at[0, top], inbox.at[0, top], right)
    far_left = pass_on(1, part.at[0, low], inbox.at[0, low], left)
    far_right.start()
    far_left.start()
    sums[0] = partial(right)
    part[1, low] = sums[0, low].astype(BF16)
    right_low = pass_on(2, part.at[1, low], inbox.at[1, low], right)
    right_low.start()
    sums[1] = partial(left)
    part[2, top] = sums[1, top].astype(BF16)
    left_top = pass_on(3, part.at[2, top], inbox.at[2, top], left)
    left_top.start()
    far_right.wait_recv()
    part[1, top] = (sums[0, top] + inbox[0, top].astype(F32)).astype(BF16)
    right_top = pass_on(4, part.at[1, top], inbox.at[1, top], right)
    right_top.start()
    far_left.wait_recv()
    part[2, low] = (sums[1, low] + inbox[0, low].astype(F32)).astype(BF16)
    left_low = pass_on(5, part.at[2, low], inbox.at[2, low], left)
    left_low.start()
    own = partial(h)
    right_low.wait_recv()
    left_top.wait_recv()
    right_top.wait_recv()
    left_low.wait_recv()
    out_ref[...] = (own + inbox[1].astype(F32) + inbox[2].astype(F32)).astype(BF16)

    for copy in (far_right, far_left, right_low, left_top, right_top, left_low):
        copy.wait_send()
    for n in (0, 1, 4, 5):
        moves[n].wait_send()

    for head in (0, 2, 3):
        each_edge(head, lambda copy: copy.wait_send())

    for i in range(heads):

        @pl.when(p != 2 * i)
        def _():
            to_owner(i).wait_send()

    @pl.when(owner)
    def _():
        group_copies(lambda copy: copy.wait_send())

        feed(lambda copy: copy.wait_send())

        for d in FAR_FIRST:
            q = lax.rem(p + d, PLANE)

            @pl.when(q > 0)
            def _():
                prefix_to(q).wait_send()

        @pl.when(z > 0)
        def _():
            for d in ENTRIES:
                entry_to(lax.rem(p + d, PLANE)).wait_send()

    @pl.when(passes_on)
    def _():
        passed.wait_send()


def layer(depth, x, w, down, gdown, beta, up, gup, conv, dlog, bias, span, gain, ow):
    vmem = pl.BlockSpec(memory_space=pltpu.VMEM)
    hbm = pl.BlockSpec(memory_space=pl.ANY)
    rows, model = x.shape
    count, width = 4 * rows, w.shape[2]
    heads = width // 128
    dma = pltpu.SemaphoreType.DMA
    return pl.pallas_call(
        functools.partial(kernel, depth),
        name="layer",
        out_shape=pltpu.VMEM((rows, model), BF16),
        in_specs=[hbm] * 13,
        out_specs=vmem,
        scratch_shapes=[
            pltpu.VMEM((count + HALO, model), BF16),
            pltpu.VMEM(w.shape, BF16),
            pltpu.VMEM((model, 256), BF16),
            pltpu.VMEM(beta.shape, BF16),
            pltpu.VMEM(up.shape, BF16),
            pltpu.VMEM(gup.shape, BF16),
            pltpu.VMEM(conv.shape, BF16),
            pltpu.SMEM(dlog.shape, F32),
            pltpu.VMEM(bias.shape, F32),
            pltpu.VMEM(span.shape, BF16),
            pltpu.VMEM(gain.shape, F32),
            pltpu.VMEM(ow.shape, BF16),
            pltpu.VMEM((3, HALO + count, width), F32),
            pltpu.VMEM((count, width), F32),
            pltpu.VMEM((count, heads), F32),
            pltpu.VMEM((count, width), F32),
            pltpu.VMEM((count, width), F32),
            pltpu.VMEM((count, width), F32),
            pltpu.VMEM((2, (len(LEVELS) + 2) * HALF, width), F32),
            pltpu.VMEM((count, width), F32),
            pltpu.VMEM((count, width), BF16),
            pltpu.VMEM((count, width), F32),
            pltpu.VMEM((heads, 256, 128), BF16),
            pltpu.VMEM((2 * heads, len(LEVELS), HALF, HALF), BF16),
            pltpu.VMEM((2 * heads, len(LEVELS), HALF, 128), BF16),
            pltpu.VMEM((2 * heads, HALF, HALF), BF16),
            pltpu.VMEM((PLANE, 256, 128), BF16),
            pltpu.VMEM((PLANE, 256, 128), BF16),
            pltpu.VMEM((256, 128), BF16),
            pltpu.VMEM((GROUP, 256, 128), BF16),
            pltpu.VMEM((128, 128), BF16),
            pltpu.VMEM((256, 128), BF16),
            pltpu.VMEM((128, 128), BF16),
            pltpu.VMEM((128, 128), BF16),
            pltpu.VMEM((heads, 256, 128), BF16),
            pltpu.VMEM((heads, 128, 128), BF16),
            pltpu.VMEM((count, width), BF16),
            pltpu.VMEM((3, rows, model), BF16),
            pltpu.VMEM((2, rows, model), F32),
            pltpu.VMEM((3, rows, model), BF16),
            dma((15,)), dma((6,)), dma((6,)), dma((3,)), dma((4,)), dma((PLANE,)), dma((heads,)),
            dma((heads,)), dma((PLANE,)), dma((GROUP,)), dma((GROUP,)),
            dma((PLANE,)), dma((heads,)), dma((6,)), dma((6,)),
        ],
        compiler_params=pltpu.CompilerParams(
            collective_id=0, has_side_effects=True, vmem_limit_bytes=56 << 20
        ),
    )(x, w, down, gdown, beta, up, gup, conv, dlog, bias, span, gain, ow)


def solution(mesh):
    seq_size = mesh.shape["seq"]
    span = span_matrix()

    def shards(
        hidden_in, qkv_weight, conv_weight, decay_log, dt_bias, decay_down, decay_up,
        beta_weight, gate_down, gate_up, norm_gain, out_weight,
    ):
        return layer(
            seq_size // PLANE,
            hidden_in,
            jnp.transpose(qkv_weight, (1, 0, 2)),
            decay_down,
            gate_down,
            beta_weight.T,
            decay_up,
            gate_up,
            conv_weight,
            decay_log,
            dt_bias.reshape(1, -1),
            jnp.asarray(span, BF16),
            norm_gain.reshape(1, -1),
            out_weight,
        )

    rows = P(("seq", "head"), None)
    return jax.shard_map(
        shards,
        mesh=mesh,
        in_specs=(
            rows, P(None, None, "head"), P(None, None, "head"), P("head"), P("head"), P(),
            P(None, "head"), P(None, "head"), P(), P(None, "head"), P(), P("head", None),
        ),
        out_specs=rows,
        check_vma=False,
    )
```

```python
import functools

import jax
import jax.numpy as jnp
import numpy as np
from jax import lax
from jax.experimental import pallas as pl
from jax.experimental.pallas import tpu as pltpu
from jax.sharding import PartitionSpec as P

F32 = jnp.float32
BF16 = jnp.bfloat16
MESH = pl.DeviceIdType.MESH

HALO = 16
EDGE = 8
HALF = 128
LEVELS = (1, 2, 4, 8, 16, 32, 64)
PLANE = 8
GROUP = 4
FAR_FIRST = (4, 5, 2, 3, 6, 7, 1)
ENTRIES = (7, 4, 6, 2, 1, 3)


def span_matrix():
    r, i = np.arange(HALF)[:, None], np.arange(HALF)[None, :]
    rows = []
    for size in LEVELS:
        middle = (r // (2 * size)) * 2 * size + size - 1
        late = (r % (2 * size)) >= size
        rows.append(np.where(late, (i > middle) & (i <= r), (i > r) & (i <= middle)))
    rows.append(i <= r)
    rows.append(i > r)
    spans = np.concatenate(rows, axis=0)
    return np.concatenate([spans, spans], axis=1).astype(np.float32)


def mm(a, b, dims=((1,), (0,))):
    return lax.dot_general(
        a.astype(BF16), b.astype(BF16), (dims, ((), ())), preferred_element_type=F32
    )


def sigmoid(v):
    return 1.0 / (1.0 + jnp.exp(-v))


def kernel(
    depth, x_hbm, w_hbm, down_hbm, gdown_hbm, beta_hbm, up_hbm, gup_hbm, conv_hbm, dlog_hbm,
    bias_hbm, span_hbm, gain_hbm, ow_hbm, out_ref,
    x_ref, w_ref, dg_ref, beta_ref, up_ref, gup_ref, conv_ref, dlog_ref, bias_ref, span_ref,
    gain_ref, ow_ref,
    proj_ref, fade_ref, strength_ref, q_ref, k_ref, v_ref, e_ref, o_ref, r_ref, gate_ref, z_ref,
    mix_ref, faded_ref, attend_ref, zin, pre, total, zall, chain, link, held, entry, lead, state, normed, part, sums, inbox,
    l_sem, x_send, x_recv, e_sem, f_sem, g_send, g_recv,
    a_send, a_recv, b_send, b_recv, c_send, c_recv, d_send, d_recv,
):
    s = lax.axis_index("seq")
    h = lax.axis_index("head")
    z = lax.div(s, PLANE)
    p = lax.rem(s, PLANE)
    y, core = lax.div(p, 2), lax.rem(p, 2)
    base = z * PLANE
    right, left, far = lax.rem(h + 1, 4), lax.rem(h + 3, 4), lax.rem(h + 2, 4)
    owner = core == 0
    group, rank = lax.div(z, GROUP), lax.rem(z, GROUP)
    feeds = jnp.logical_and(group == 0, jnp.logical_or(rank == 0, rank == GROUP - 1))
    has_next = s < depth * PLANE - 1
    edge_from = jnp.where(h == 1, 2, h)
    rows = x_hbm.shape[0]
    half = rows // 2
    count = 4 * rows
    width = w_ref.shape[2]
    heads = width // 128

    barrier = pltpu.get_barrier_semaphore()
    pl.semaphore_signal(barrier, 1, device_id={"head": right}, device_id_type=MESH)
    pl.semaphore_signal(barrier, 1, device_id={"head": left}, device_id_type=MESH)

    @pl.when(s > 0)
    def _():
        pl.semaphore_signal(
            barrier, 1, device_id={"seq": s - 1, "head": edge_from}, device_id_type=MESH
        )

    for d in range(1, PLANE):
        q = lax.rem(p + d, PLANE)

        @pl.when(jnp.logical_or(owner, lax.rem(q, 2) == 0))
        def _():
            pl.semaphore_signal(barrier, 1, device_id={"seq": base + q}, device_id_type=MESH)

    @pl.when(core == 1)
    def _():
        pl.semaphore_signal(
            barrier, 1, device_id={"seq": base + lax.rem(p + 2, PLANE)}, device_id_type=MESH
        )

    @pl.when(owner)
    def _():
        for d in range(1, GROUP):
            other = group * GROUP + lax.rem(rank + d, GROUP)
            pl.semaphore_signal(
                barrier, 1, device_id={"seq": other * PLANE + p}, device_id_type=MESH
            )

        @pl.when(group == 1)
        def _():
            feeder = jnp.where(rank < GROUP - 1, GROUP - 1, 0)
            pl.semaphore_signal(
                barrier, 1, device_id={"seq": feeder * PLANE + p}, device_id_type=MESH
            )

    greeted = (
        2
        + jnp.where(owner, PLANE - 1 + GROUP - 1, PLANE // 2 + 1)
        + jnp.where(jnp.logical_and(owner, feeds), jnp.where(rank == 0, 1, GROUP - 1), 0)
        + jnp.where(has_next, jnp.where(h == 2, 2, jnp.where(h == 1, 0, 1)), 0)
    )

    loads = [
        pltpu.make_async_copy(src, dst, l_sem.at[k])
        for k, (src, dst) in enumerate(
            [
                (x_hbm, x_ref.at[pl.ds(0, rows)]),
                (w_hbm.at[0], w_ref.at[0]),
                (w_hbm.at[1], w_ref.at[1]),
                (w_hbm.at[2], w_ref.at[2]),
                (down_hbm, dg_ref.at[:, pl.ds(0, 128)]),
                (gdown_hbm, dg_ref.at[:, pl.ds(128, 128)]),
                (beta_hbm, beta_ref),
                (up_hbm, up_ref),
                (gup_hbm, gup_ref),
                (conv_hbm, conv_ref),
                (dlog_hbm, dlog_ref),
                (bias_hbm, bias_ref),
                (gain_hbm, gain_ref),
                (span_hbm, span_ref),
                (ow_hbm, ow_ref),
            ]
        )
    ]
    for load in loads:
        load.start()
    x_ref[count + EDGE :, :] = jnp.zeros((HALO - EDGE, x_ref.shape[1]), BF16)

    @pl.when(s == 0)
    def _():
        x_ref[count : count + EDGE, :] = jnp.zeros((EDGE, x_ref.shape[1]), BF16)

    pl.semaphore_wait(barrier, greeted)

    def piece(src, slot, half_at, target, k):
        return pltpu.make_async_remote_copy(
            src_ref=src,
            dst_ref=x_ref.at[pl.ds(slot * rows + half_at * half, half)],
            send_sem=x_send.at[k],
            recv_sem=x_recv.at[k],
            device_id={"head": target},
            device_id_type=MESH,
        )

    def rows_at(slot, half_at):
        return x_ref.at[pl.ds(slot * rows + half_at * half, half)]

    loads[0].wait()
    mine = [rows_at(0, 0), rows_at(0, 1)]
    moves = [
        piece(mine[0], 1, 0, right, 0),
        piece(mine[1], 2, 1, left, 1),
        piece(mine[1], 1, 1, right, 2),
        piece(mine[0], 2, 0, left, 3),
        piece(rows_at(1, 0), 3, 0, right, 4),
        piece(rows_at(2, 1), 3, 1, left, 5),
    ]
    for move in moves[:4]:
        move.start()

    def edge(k, src, target):
        return pltpu.make_async_remote_copy(
            src_ref=src,
            dst_ref=x_ref.at[pl.ds(count, EDGE)],
            send_sem=e_sem.at[k],
            recv_sem=e_sem.at[2],
            device_id={"seq": s + 1, "head": target},
            device_id_type=MESH,
        )

    last = pl.ds(rows - EDGE, EDGE)
    edges = {
        3: [edge(0, x_ref.at[last], 3)],
        0: [edge(0, x_ref.at[pl.ds(2 * rows - EDGE, EDGE)], 0)],
        2: [
            edge(0, x_ref.at[pl.ds(3 * rows - EDGE, EDGE)], 2),
            edge(1, x_ref.at[pl.ds(3 * rows - EDGE, EDGE)], 1),
        ],
    }

    def each_edge(head, act):
        @pl.when(jnp.logical_and(h == head, has_next))
        def _():
            for copy in edges[head]:
                act(copy)

    each_edge(3, lambda copy: copy.start())
    for load in loads[1:14]:
        load.wait()

    rate = jnp.concatenate(
        [jnp.exp(jnp.full((1, 128), dlog_ref[i], F32)) for i in range(heads)], axis=1
    )

    def project(first, slots):
        size = len(slots) * rows
        at = [pl.ds(pl.multiple_of(slot * rows, 16), rows) for slot in slots]
        some = x_ref[first : first + size, :]
        both = jnp.dot(some, dg_ref[...], preferred_element_type=F32).astype(BF16)
        force = sigmoid(
            lax.dot_general(
                some, beta_ref[...], (((1,), (1,)), ((), ())), preferred_element_type=F32
            )
        )
        raw = jnp.dot(both[:, 0:128], up_ref[...], preferred_element_type=F32) + bias_ref[...]
        soft = jnp.maximum(raw, 0.0) + jnp.log1p(jnp.exp(-jnp.abs(raw)))
        log_decay = -rate * soft
        gate = sigmoid(jnp.dot(both[:, 128:256], gup_ref[...], preferred_element_type=F32))
        for n, where in enumerate(at):
            own = slice(n * rows, (n + 1) * rows)
            fade_ref[where, :] = log_decay[own]
            gate_ref[where, :] = gate[own]
            strength_ref[where, :] = force[own]

    def project_qkv(c, first, slots, tail):
        size = len(slots) * rows
        some = x_ref[first : first + size + tail, :]
        got = jnp.dot(some, w_ref[c], preferred_element_type=F32).astype(BF16).astype(F32)
        for n, slot in enumerate(slots):
            at = pl.ds(pl.multiple_of(HALO + slot * rows, 16), rows)
            proj_ref[c, at, :] = got[n * rows : (n + 1) * rows]
        if tail:
            proj_ref[c, HALO - EDGE : HALO, :] = got[size : size + EDGE]

    def decays(c):
        piece_of = fade_ref[pl.ds(pl.multiple_of(c * HALF, HALF), HALF), :]
        top = piece_of.astype(BF16)
        rest = (piece_of - top.astype(F32)).astype(BF16)
        e_ref[c] = jnp.exp(
            jnp.dot(
                span_ref[...], jnp.concatenate([top, rest], axis=0), preferred_element_type=F32
            )
        )

    project(0, (h,))
    for c in range(3):
        project_qkv(c, 0, (h,), 0)

    moves[0].wait_recv()
    moves[2].wait_send()
    moves[4].start()
    moves[1].wait_recv()
    moves[3].wait_send()
    moves[5].start()
    each_edge(2, lambda copy: copy.start())
    moves[2].wait_recv()
    each_edge(0, lambda copy: copy.start())
    moves[3].wait_recv()

    near = (left, right)
    project(rows, near)
    for c in range(3):
        project_qkv(c, rows, near, 0)
    far_square = lax.div(far, 2)
    decays(1 - far_square)
    moves[4].wait_recv()
    moves[5].wait_recv()

    @pl.when(s > 0)
    def _():
        edges[0][0].wait_recv()

    def convolve(c):
        target = (q_ref, k_ref, v_ref)[c]
        taps = conv_ref[c].astype(F32)
        mixed = proj_ref[c, pl.ds(HALO - 3, count), :] * taps[0:1]
        for i in range(1, 4):
            mixed = mixed + proj_ref[c, pl.ds(HALO - 3 + i, count), :] * taps[i : i + 1]
        mixed = (mixed * sigmoid(mixed)).astype(BF16).astype(F32)
        if c == 2:
            target[...] = mixed
            return
        for i in range(heads):
            lanes = slice(i * 128, (i + 1) * 128)
            u = mixed[:, lanes]
            scale = lax.rsqrt(jnp.sum(u * u, axis=1, keepdims=True) + 1e-06)
            if c == 0:
                scale = scale * (128**-0.5)
            target[:, lanes] = u * scale

    project(3 * rows, (far,))
    project_qkv(1, 3 * rows, (far,), HALO)
    decays(far_square)
    convolve(1)
    project_qkv(2, 3 * rows, (far,), HALO)
    convolve(2)
    beta = strength_ref[...]

    t = lax.broadcasted_iota(jnp.int32, (HALF, HALF), 0)
    j = lax.broadcasted_iota(jnp.int32, (HALF, HALF), 1)
    row = lax.broadcasted_iota(jnp.int32, (HALF, 128), 0)
    masks = [
        ((t ^ j) >= size) & ((t ^ j) < 2 * size) & (t > j) for size in LEVELS
    ]
    diagonal = t == j

    lanes_of = [slice(i * 128, (i + 1) * 128) for i in range(heads)]
    rows_of = [slice(c * HALF, (c + 1) * HALF) for c in range(2)]

    def to_owner(i):
        return pltpu.make_async_remote_copy(
            src_ref=z_ref.at[i],
            dst_ref=zin.at[p],
            send_sem=a_send.at[i],
            recv_sem=a_recv.at[p],
            device_id={"seq": base + 2 * i},
            device_id_type=MESH,
        )

    strength, written, inverse = {}, {}, {}

    def unit_of(i, c):
        return 2 * i + c

    def mix(i, c, n):
        kc = k_ref[rows_of[c], lanes_of[i]]
        if n == 0:
            strength[i, c] = jnp.broadcast_to(beta[rows_of[c], i : i + 1], (HALF, 128))
            written[i, c] = kc * strength[i, c]
        fade = e_ref[c, n * HALF : (n + 1) * HALF, lanes_of[i]]
        size = LEVELS[n]
        if size < 8:
            chosen = jnp.where((row & size) != 0, kc, written[i, c])
        else:
            chosen = jnp.concatenate(
                [
                    (kc if at & size else written[i, c])[at : at + size]
                    for at in range(0, HALF, size)
                ],
                axis=0,
            )
        kx = (chosen * fade).astype(BF16)
        faded_ref[unit_of(i, c), n] = kx
        mix_ref[unit_of(i, c), n] = jnp.where(masks[n], mm(kx, kx, ((1,), (1,))), 0.0).astype(BF16)

    def mixes(some):
        for i in some:
            for c in range(2):
                for n in range(len(LEVELS)):
                    mix(i, c, n)
                    yield

    def attends(some):
        for i in some:
            for c in range(2):
                kc, qc = k_ref[rows_of[c], lanes_of[i]], q_ref[rows_of[c], lanes_of[i]]
                own = jnp.sum(qc * kc, axis=1, keepdims=True) * strength[i, c]
                attend = jnp.where(diagonal, own, 0.0)
                for n in range(len(LEVELS)):
                    qx = qc * e_ref[c, n * HALF : (n + 1) * HALF, lanes_of[i]]
                    both = mm(qx, faded_ref[unit_of(i, c), n], ((1,), (1,)))
                    attend = jnp.where(masks[n], both, attend)
                attend_ref[unit_of(i, c)] = attend.astype(BF16)
                yield

    def doublings(some):
        units = [(i, c) for i in some for c in range(2)]
        for unit in units:
            inverse[unit] = jnp.where(diagonal, 1.0, 0.0) - mix_ref[unit_of(*unit), 0].astype(F32)
        for n in range(1, len(LEVELS)):
            own = {unit: inverse[unit].astype(BF16) for unit in units}
            left_part = {}
            for unit in units:
                left_part[unit] = mm(own[unit], mix_ref[unit_of(*unit), n]).astype(BF16)
            yield
            for unit in units:
                inverse[unit] = inverse[unit] - mm(left_part[unit], own[unit])
            yield
        for unit in units:
            inverse[unit] = inverse[unit].astype(BF16)

    parts = {}

    def maps_of(some):
        n = len(LEVELS)
        units = [(i, c) for i in some for c in range(2)]
        rise = {u: e_ref[u[1], n * HALF : (n + 1) * HALF, lanes_of[u[0]]] for u in units}
        fall = {u: e_ref[u[1], (n + 1) * HALF : (n + 2) * HALF, lanes_of[u[0]]] for u in units}
        whole = {u: rise[u][HALF - 1 : HALF] for u in units}
        k_rise = {u: k_ref[rows_of[u[1]], lanes_of[u[0]]] * rise[u] for u in units}
        k_fall = {
            u: written[u] * fall[u] for u in units
        }
        cross, first, second = {}, {}, {}
        for i in some:
            cross[i] = mm(k_rise[i, 1], k_fall[i, 0], ((1,), (1,))).astype(BF16)
        for i in some:
            first[i] = mm(
                inverse[i, 0],
                jnp.concatenate([v_ref[rows_of[0], lanes_of[i]], k_rise[i, 0]], axis=1),
            ).astype(BF16)
        yield
        late_part = {i: mm(cross[i], first[i]) for i in some}
        yield
        for i in some:
            start = jnp.concatenate(
                [v_ref[rows_of[1], lanes_of[i]], k_rise[i, 1] * whole[i, 0]], axis=1
            )
            second[i] = mm(inverse[i, 1], start - late_part[i]).astype(BF16)
        yield
        for i in some:
            stop = jnp.concatenate(
                [k_fall[i, 0] * whole[i, 1], k_fall[i, 1]], axis=0
            ).astype(BF16)
            maps = mm(jnp.concatenate([first[i], second[i]], axis=0), stop, ((0,), (0,)))
            move = jnp.where(diagonal, whole[i, 0] * whole[i, 1], 0.0) - maps[128:]
            z_ref[i, 0:128] = move.astype(BF16)
            z_ref[i, 128:256] = maps[:128].astype(BF16)
            parts[i] = (rise, whole, first, second, k_fall)

    def outputs_of(some):
        for i in some:
            rise, whole, first, second, k_fall = parts[i]
            lanes = lanes_of[i]
            q_rise = {
                (i, c): q_ref[rows_of[c], lanes] * rise[i, c] for c in range(2)
            }
            cross = mm(q_rise[i, 1], k_fall[i, 0], ((1,), (1,)))
            out = [
                mm(attend_ref[unit_of(i, 0)], first[i]),
                mm(cross, first[i]) + mm(attend_ref[unit_of(i, 1)], second[i]),
            ]
            for c in range(2):
                o_ref[rows_of[c], lanes] = out[c][:, :128]
            r_ref[rows_of[0], lanes] = (q_rise[i, 0] - out[0][:, 128:]).astype(BF16)
            r_ref[rows_of[1], lanes] = (
                q_rise[i, 1] * whole[i, 0] - out[1][:, 128:]
            ).astype(BF16)
            yield

    def send_maps(some):
        for i in some:

            @pl.when(p != 2 * i)
            def _():
                to_owner(i).start()

    def together(main, other, share):
        for _ in main:
            for _ in range(share):
                next(other, None)

    def finish(*works):
        for work in works:
            for _ in work:
                pass

    early, late_heads = range(0, heads, 2), range(1, heads, 2)
    finish(mixes(early))
    other = mixes(late_heads)
    together(doublings(early), other, 3)
    finish(other)
    other = doublings(late_heads)
    together(maps_of(early), other, 1)
    send_maps(early)
    finish(other, maps_of(late_heads))
    send_maps(late_heads)
    project_qkv(0, 3 * rows, (far,), HALO)
    convolve(0)
    for some in (early, late_heads):
        finish(attends(some), outputs_of(some))

    def to_group(k, at):
        return pltpu.make_async_remote_copy(
            src_ref=total.at[at],
            dst_ref=zall.at[rank, at],
            send_sem=b_send.at[k],
            recv_sem=b_recv.at[rank],
            device_id={"seq": (group * GROUP + k) * PLANE + p},
            device_id_type=MESH,
        )

    def from_group(k, at):
        return pltpu.make_async_remote_copy(
            src_ref=total.at[at],
            dst_ref=zall.at[k, at],
            send_sem=b_send.at[k],
            recv_sem=b_recv.at[k],
            device_id={"seq": s},
            device_id_type=MESH,
        )

    def to_next(k):
        target = jnp.where(rank == 0, 2 * GROUP - 1, 2 * GROUP - 2 - k)
        return pltpu.make_async_remote_copy(
            src_ref=chain,
            dst_ref=held,
            send_sem=f_sem.at[k],
            recv_sem=f_sem.at[3],
            device_id={"seq": target * PLANE + p},
            device_id_type=MESH,
        )

    def feed(act):
        @pl.when(feeds)
        def _():
            act(to_next(0))

        @pl.when(jnp.logical_and(feeds, rank > 0))
        def _():
            for k in range(1, GROUP - 1):
                act(to_next(k))

    def prefix_to(q):
        return pltpu.make_async_remote_copy(
            src_ref=pre.at[q],
            dst_ref=lead.at[y],
            send_sem=g_send.at[q],
            recv_sem=g_recv.at[y],
            device_id={"seq": base + q},
            device_id_type=MESH,
        )

    def entry_to(q):
        return pltpu.make_async_remote_copy(
            src_ref=entry,
            dst_ref=state.at[y],
            send_sem=c_send.at[q],
            recv_sem=c_recv.at[y],
            device_id={"seq": base + q},
            device_id_type=MESH,
        )

    def landed(ref, sem, k):
        pltpu.make_async_remote_copy(
            src_ref=ref.at[k],
            dst_ref=ref.at[k],
            send_sem=sem.at[k],
            recv_sem=sem.at[k],
            device_id={"seq": s},
            device_id_type=MESH,
        ).wait_recv()

    everything, shift_only = pl.ds(0, 256), pl.ds(128, 128)
    half_plane = PLANE // 2

    def join(one, two):
        step = mm(one, two[:128])
        return jnp.concatenate(
            [step[:128].astype(BF16), (step[128:] + two[128:].astype(F32)).astype(BF16)], axis=0
        )

    def moved(state_in, both):
        return (mm(state_in, both[0:128]) + both[128:256].astype(F32)).astype(BF16)

    def group_copies(act):
        for k in (3, 0, 2, 1):
            @pl.when(jnp.logical_and(jnp.logical_and(group == 0, rank == 0), k > 0))
            def _():
                act(to_group(k, shift_only))

            wanted = k > rank
            if k == 0:
                wanted = jnp.logical_and(group == 0, rank > 0)
            else:
                wanted = jnp.logical_and(
                    wanted, jnp.logical_or(group == 1, rank > 0)
                )

            @pl.when(wanted)
            def _():
                act(to_group(k, everything))

    @pl.when(owner)
    def _():
        zin[p] = z_ref[y]
        for k in range(PLANE):

            @pl.when(p != k)
            def _():
                landed(zin, a_recv, k)

        one, two = zin[0], zin[half_plane]
        later = {}
        for k in range(1, half_plane):
            pre[k], later[half_plane + k] = one, two
            one, two = join(one, zin[k]), join(two, zin[half_plane + k])
        pre[half_plane] = one
        whole_map = join(one, two)
        total[...] = whole_map
        group_copies(lambda copy: copy.start())
        zall[rank] = whole_map
        for k in range(half_plane + 1, PLANE):
            pre[k] = join(one, later[k])
        for d in FAR_FIRST:
            q = lax.rem(p + d, PLANE)

            @pl.when(q > 0)
            def _():
                prefix_to(q).start()

        @pl.when(p > 0)
        def _():
            lead[y] = pre[p]

        @pl.when(group == 0)
        def _():
            chain[...] = jnp.zeros_like(chain)
            entry[...] = jnp.zeros_like(entry)
            for k in range(GROUP):
                needed = jnp.logical_or(feeds, k < rank)
                if k == 0:

                    @pl.when(rank > 0)
                    def _():
                        from_group(0, shift_only).wait_recv()

                else:

                    @pl.when(jnp.logical_and(needed, rank != k))
                    def _():
                        from_group(k, everything).wait_recv()

                @pl.when(rank == k)
                def _():
                    entry[...] = chain[...]

                @pl.when(needed)
                def _():
                    if k == 0:
                        chain[...] = zall[0, 128:256]
                    else:
                        chain[...] = moved(chain[...], zall[k])

            feed(lambda copy: copy.start())

        @pl.when(group == 1)
        def _():
            for k in range(GROUP - 1):

                @pl.when(k < rank)
                def _():
                    from_group(k, everything).wait_recv()
                    if k == 0:
                        link[...] = zall[0]
                    else:
                        link[...] = join(link[...], zall[k])

            to_next(0).wait_recv()

            @pl.when(rank == 0)
            def _():
                entry[...] = held[...]

            @pl.when(rank > 0)
            def _():
                entry[...] = moved(held[...], link[...])

        @pl.when(z > 0)
        def _():
            for d in ENTRIES:
                entry_to(lax.rem(p + d, PLANE)).start()

            state[y] = entry[...]

    @pl.when(z == 0)
    def _():
        state[...] = jnp.zeros_like(state)

    @pl.when(p > 0)
    def _():
        for i in range(heads):

            @pl.when(p != 2 * i)
            def _():
                landed(lead, g_recv, i)

        for i in range(heads):
            lanes = lanes_of[i]
            both = mm(r_ref[:, lanes], lead[i], ((1,), (1,)))
            o_ref[:, lanes] = o_ref[:, lanes] + both[:, 128:]
            r_ref[:, lanes] = both[:, :128].astype(BF16)

    after_own = lax.rem(y + 1, heads)
    passes_on = jnp.logical_and(core == 1, z > 0)
    passed = pltpu.make_async_remote_copy(
        src_ref=state.at[after_own],
        dst_ref=state.at[after_own],
        send_sem=c_send.at[0],
        recv_sem=c_recv.at[after_own],
        device_id={"seq": base + lax.rem(p + PLANE - 2, PLANE)},
        device_id_type=MESH,
    )
    for d in (0, 1, 3, 2):
        i = lax.rem(y + d, heads)

        @pl.when(jnp.logical_and(p != 2 * i, z > 0))
        def _():
            landed(state, c_recv, i)

        if d == 1:

            @pl.when(passes_on)
            def _():
                passed.start()

        lanes = pl.ds(pl.multiple_of(i * 128, 128), 128)
        attended = o_ref[:, lanes] + mm(r_ref[:, lanes], state[i], ((1,), (1,)))
        scale = lax.rsqrt(jnp.mean(attended * attended, axis=1, keepdims=True) + 1e-05)
        normed[:, lanes] = (attended * scale * gain_ref[...] * gate_ref[:, lanes]).astype(BF16)
    loads[14].wait()


    def partial(to, lanes=slice(None)):
        at = pl.ds(pl.multiple_of(to * rows, 16), rows)
        return jnp.dot(normed[at, :], ow_ref[:, lanes], preferred_element_type=F32)

    def pass_on(k, src, dst, target):
        return pltpu.make_async_remote_copy(
            src_ref=src,
            dst_ref=dst,
            send_sem=d_send.at[k],
            recv_sem=d_recv.at[k],
            device_id={"head": target},
            device_id_type=MESH,
        )

    top, low = pl.ds(0, half), pl.ds(half, half)
    columns = out_ref.shape[1]
    split = columns // 2 // 128 * 128
    far_right, far_left = [], []
    for n, (first_lane, end_lane) in enumerate([(0, split), (split, columns)]):
        part[0, :, first_lane:end_lane] = partial(far, slice(first_lane, end_lane)).astype(BF16)
        some = pl.ds(first_lane, end_lane - first_lane)
        far_right.append(
            pass_on(2 * n, part.at[0, top, some], inbox.at[0, top, some], right)
        )
        far_left.append(
            pass_on(2 * n + 1, part.at[0, low, some], inbox.at[0, low, some], left)
        )
        far_right[n].start()
        far_left[n].start()
    sums[0] = partial(right)
    part[1, low] = sums[0, low].astype(BF16)
    right_low = pass_on(4, part.at[1, low], inbox.at[1, low], right)
    right_low.start()
    sums[1] = partial(left)
    part[2, top] = sums[1, top].astype(BF16)
    left_top = pass_on(5, part.at[2, top], inbox.at[2, top], left)
    left_top.start()
    for copy in far_right:
        copy.wait_recv()
    part[1, top] = (sums[0, top] + inbox[0, top].astype(F32)).astype(BF16)
    right_top = pass_on(6, part.at[1, top], inbox.at[1, top], right)
    right_top.start()
    for copy in far_left:
        copy.wait_recv()
    part[2, low] = (sums[1, low] + inbox[0, low].astype(F32)).astype(BF16)
    left_low = pass_on(7, part.at[2, low], inbox.at[2, low], left)
    left_low.start()
    own = partial(h)
    right_low.wait_recv()
    left_top.wait_recv()
    right_top.wait_recv()
    left_low.wait_recv()
    out_ref[...] = (own + inbox[1].astype(F32) + inbox[2].astype(F32)).astype(BF16)

    for copy in (*far_right, *far_left, right_low, left_top, right_top, left_low):
        copy.wait_send()
    for n in (0, 1, 4, 5):
        moves[n].wait_send()

    for head in (0, 2, 3):
        each_edge(head, lambda copy: copy.wait_send())

    for i in range(heads):

        @pl.when(p != 2 * i)
        def _():
            to_owner(i).wait_send()

    @pl.when(owner)
    def _():
        group_copies(lambda copy: copy.wait_send())

        feed(lambda copy: copy.wait_send())

        for d in FAR_FIRST:
            q = lax.rem(p + d, PLANE)

            @pl.when(q > 0)
            def _():
                prefix_to(q).wait_send()

        @pl.when(z > 0)
        def _():
            for d in ENTRIES:
                entry_to(lax.rem(p + d, PLANE)).wait_send()

    @pl.when(passes_on)
    def _():
        passed.wait_send()


def layer(depth, x, w, down, gdown, beta, up, gup, conv, dlog, bias, span, gain, ow):
    vmem = pl.BlockSpec(memory_space=pltpu.VMEM)
    hbm = pl.BlockSpec(memory_space=pl.ANY)
    rows, model = x.shape
    count, width = 4 * rows, w.shape[2]
    heads = width // 128
    dma = pltpu.SemaphoreType.DMA
    return pl.pallas_call(
        functools.partial(kernel, depth),
        name="layer",
        out_shape=pltpu.VMEM((rows, model), BF16),
        in_specs=[hbm] * 13,
        out_specs=vmem,
        scratch_shapes=[
            pltpu.VMEM((count + HALO, model), BF16),
            pltpu.VMEM(w.shape, BF16),
            pltpu.VMEM((model, 256), BF16),
            pltpu.VMEM(beta.shape, BF16),
            pltpu.VMEM(up.shape, BF16),
            pltpu.VMEM(gup.shape, BF16),
            pltpu.VMEM(conv.shape, BF16),
            pltpu.SMEM(dlog.shape, F32),
            pltpu.VMEM(bias.shape, F32),
            pltpu.VMEM(span.shape, BF16),
            pltpu.VMEM(gain.shape, F32),
            pltpu.VMEM(ow.shape, BF16),
            pltpu.VMEM((3, HALO + count, width), F32),
            pltpu.VMEM((count, width), F32),
            pltpu.VMEM((count, heads), F32),
            pltpu.VMEM((count, width), F32),
            pltpu.VMEM((count, width), F32),
            pltpu.VMEM((count, width), F32),
            pltpu.VMEM((2, (len(LEVELS) + 2) * HALF, width), F32),
            pltpu.VMEM((count, width), F32),
            pltpu.VMEM((count, width), BF16),
            pltpu.VMEM((count, width), F32),
            pltpu.VMEM((heads, 256, 128), BF16),
            pltpu.VMEM((2 * heads, len(LEVELS), HALF, HALF), BF16),
            pltpu.VMEM((2 * heads, len(LEVELS), HALF, 128), BF16),
            pltpu.VMEM((2 * heads, HALF, HALF), BF16),
            pltpu.VMEM((PLANE, 256, 128), BF16),
            pltpu.VMEM((PLANE, 256, 128), BF16),
            pltpu.VMEM((256, 128), BF16),
            pltpu.VMEM((GROUP, 256, 128), BF16),
            pltpu.VMEM((128, 128), BF16),
            pltpu.VMEM((256, 128), BF16),
            pltpu.VMEM((128, 128), BF16),
            pltpu.VMEM((128, 128), BF16),
            pltpu.VMEM((heads, 256, 128), BF16),
            pltpu.VMEM((heads, 128, 128), BF16),
            pltpu.VMEM((count, width), BF16),
            pltpu.VMEM((3, rows, model), BF16),
            pltpu.VMEM((2, rows, model), F32),
            pltpu.VMEM((3, rows, model), BF16),
            dma((15,)), dma((6,)), dma((6,)), dma((3,)), dma((4,)), dma((PLANE,)), dma((heads,)),
            dma((heads,)), dma((PLANE,)), dma((GROUP,)), dma((GROUP,)),
            dma((PLANE,)), dma((heads,)), dma((8,)), dma((8,)),
        ],
        compiler_params=pltpu.CompilerParams(
            collective_id=0, has_side_effects=True, vmem_limit_bytes=56 << 20
        ),
    )(x, w, down, gdown, beta, up, gup, conv, dlog, bias, span, gain, ow)


def solution(mesh):
    seq_size = mesh.shape["seq"]
    span = span_matrix()

    def shards(
        hidden_in, qkv_weight, conv_weight, decay_log, dt_bias, decay_down, decay_up,
        beta_weight, gate_down, gate_up, norm_gain, out_weight,
    ):
        return layer(
            seq_size // PLANE,
            hidden_in,
            jnp.transpose(qkv_weight, (1, 0, 2)),
            decay_down,
            gate_down,
            beta_weight.T,
            decay_up,
            gate_up,
            conv_weight,
            decay_log,
            dt_bias.reshape(1, -1),
            jnp.asarray(span, BF16),
            norm_gain.reshape(1, -1),
            out_weight,
        )

    rows = P(("seq", "head"), None)
    return jax.shard_map(
        shards,
        mesh=mesh,
        in_specs=(
            rows, P(None, None, "head"), P(None, None, "head"), P("head"), P("head"), P(),
            P(None, "head"), P(None, "head"), P(), P(None, "head"), P(), P("head", None),
        ),
        out_specs=rows,
        check_vma=False,
    )
```

```python
import functools

import jax
import jax.numpy as jnp
import numpy as np
from jax import lax
from jax.experimental import pallas as pl
from jax.experimental.pallas import tpu as pltpu
from jax.sharding import PartitionSpec as P

F32 = jnp.float32
BF16 = jnp.bfloat16
MESH = pl.DeviceIdType.MESH

HALO = 16
EDGE = 8
HALF = 128
LEVELS = (1, 2, 4, 8, 16, 32, 64)
PLANE = 8
GROUP = 4
FAR_FIRST = (4, 5, 2, 3, 6, 7, 1)
ENTRIES = (7, 4, 6, 2, 1, 3)


def span_matrix():
    r, i = np.arange(HALF)[:, None], np.arange(HALF)[None, :]
    rows = []
    for size in LEVELS:
        middle = (r // (2 * size)) * 2 * size + size - 1
        late = (r % (2 * size)) >= size
        rows.append(np.where(late, (i > middle) & (i <= r), (i > r) & (i <= middle)))
    rows.append(i <= r)
    rows.append(i > r)
    spans = np.concatenate(rows, axis=0)
    return np.concatenate([spans, spans], axis=1).astype(np.float32)


def mm(a, b, dims=((1,), (0,))):
    return lax.dot_general(
        a.astype(BF16), b.astype(BF16), (dims, ((), ())), preferred_element_type=F32
    )


def sigmoid(v):
    return 1.0 / (1.0 + jnp.exp(-v))


def kernel(
    depth, x_hbm, w_hbm, down_hbm, gdown_hbm, beta_hbm, up_hbm, gup_hbm, conv_hbm, dlog_hbm,
    bias_hbm, span_hbm, gain_hbm, ow_hbm, out_ref,
    x_ref, w_ref, dg_ref, beta_ref, up_ref, gup_ref, conv_ref, dlog_ref, bias_ref, span_ref,
    gain_ref, ow_ref,
    proj_ref, fade_ref, strength_ref, q_ref, k_ref, v_ref, e_ref, o_ref, r_ref, gate_ref, z_ref,
    mix_ref, faded_ref, attend_ref, zin, pre, total, zall, chain, link, held, entry, lead, state, normed, part, sums, inbox,
    l_sem, x_send, x_recv, e_sem, f_sem, g_send, g_recv,
    a_send, a_recv, b_send, b_recv, c_send, c_recv, d_send, d_recv,
):
    s = lax.axis_index("seq")
    h = lax.axis_index("head")
    z = lax.div(s, PLANE)
    p = lax.rem(s, PLANE)
    y, core = lax.div(p, 2), lax.rem(p, 2)
    base = z * PLANE
    right, left, far = lax.rem(h + 1, 4), lax.rem(h + 3, 4), lax.rem(h + 2, 4)
    owner = core == 0
    group, rank = lax.div(z, GROUP), lax.rem(z, GROUP)
    feeds = jnp.logical_and(group == 0, jnp.logical_or(rank == 0, rank == GROUP - 1))
    has_next = s < depth * PLANE - 1
    edge_from = jnp.where(h == 1, 2, h)
    rows = x_hbm.shape[0]
    half = rows // 2
    count = 4 * rows
    width = w_ref.shape[2]
    heads = width // 128

    barrier = pltpu.get_barrier_semaphore()
    pl.semaphore_signal(barrier, 1, device_id={"head": right}, device_id_type=MESH)
    pl.semaphore_signal(barrier, 1, device_id={"head": left}, device_id_type=MESH)

    @pl.when(s > 0)
    def _():
        pl.semaphore_signal(
            barrier, 1, device_id={"seq": s - 1, "head": edge_from}, device_id_type=MESH
        )

    for d in range(1, PLANE):
        q = lax.rem(p + d, PLANE)

        @pl.when(jnp.logical_or(owner, lax.rem(q, 2) == 0))
        def _():
            pl.semaphore_signal(barrier, 1, device_id={"seq": base + q}, device_id_type=MESH)

    @pl.when(core == 1)
    def _():
        pl.semaphore_signal(
            barrier, 1, device_id={"seq": base + lax.rem(p + 2, PLANE)}, device_id_type=MESH
        )

    @pl.when(owner)
    def _():
        for d in range(1, GROUP):
            other = group * GROUP + lax.rem(rank + d, GROUP)
            pl.semaphore_signal(
                barrier, 1, device_id={"seq": other * PLANE + p}, device_id_type=MESH
            )

        @pl.when(group == 1)
        def _():
            feeder = jnp.where(rank < GROUP - 1, GROUP - 1, 0)
            pl.semaphore_signal(
                barrier, 1, device_id={"seq": feeder * PLANE + p}, device_id_type=MESH
            )

    greeted = (
        2
        + jnp.where(owner, PLANE - 1 + GROUP - 1, PLANE // 2 + 1)
        + jnp.where(jnp.logical_and(owner, feeds), jnp.where(rank == 0, 1, GROUP - 1), 0)
        + jnp.where(has_next, jnp.where(h == 2, 2, jnp.where(h == 1, 0, 1)), 0)
    )

    loads = [
        pltpu.make_async_copy(src, dst, l_sem.at[k])
        for k, (src, dst) in enumerate(
            [
                (x_hbm, x_ref.at[pl.ds(0, rows)]),
                (w_hbm.at[0], w_ref.at[0]),
                (w_hbm.at[1], w_ref.at[1]),
                (w_hbm.at[2], w_ref.at[2]),
                (down_hbm, dg_ref.at[:, pl.ds(0, 128)]),
                (gdown_hbm, dg_ref.at[:, pl.ds(128, 128)]),
                (beta_hbm, beta_ref),
                (up_hbm, up_ref),
                (gup_hbm, gup_ref),
                (conv_hbm, conv_ref),
                (dlog_hbm, dlog_ref),
                (bias_hbm, bias_ref),
                (gain_hbm, gain_ref),
                (span_hbm, span_ref),
                (ow_hbm, ow_ref),
            ]
        )
    ]
    for load in loads:
        load.start()
    x_ref[count + EDGE :, :] = jnp.zeros((HALO - EDGE, x_ref.shape[1]), BF16)

    @pl.when(s == 0)
    def _():
        x_ref[count : count + EDGE, :] = jnp.zeros((EDGE, x_ref.shape[1]), BF16)

    pl.semaphore_wait(barrier, greeted)

    def piece(src, slot, half_at, target, k):
        return pltpu.make_async_remote_copy(
            src_ref=src,
            dst_ref=x_ref.at[pl.ds(slot * rows + half_at * half, half)],
            send_sem=x_send.at[k],
            recv_sem=x_recv.at[k],
            device_id={"head": target},
            device_id_type=MESH,
        )

    def rows_at(slot, half_at):
        return x_ref.at[pl.ds(slot * rows + half_at * half, half)]

    loads[0].wait()
    mine = [rows_at(0, 0), rows_at(0, 1)]
    moves = [
        piece(mine[0], 1, 0, right, 0),
        piece(mine[1], 2, 1, left, 1),
        piece(mine[1], 1, 1, right, 2),
        piece(mine[0], 2, 0, left, 3),
        piece(rows_at(1, 0), 3, 0, right, 4),
        piece(rows_at(2, 1), 3, 1, left, 5),
    ]
    for move in moves[:4]:
        move.start()

    def edge(k, src, target):
        return pltpu.make_async_remote_copy(
            src_ref=src,
            dst_ref=x_ref.at[pl.ds(count, EDGE)],
            send_sem=e_sem.at[k],
            recv_sem=e_sem.at[2],
            device_id={"seq": s + 1, "head": target},
            device_id_type=MESH,
        )

    last = pl.ds(rows - EDGE, EDGE)
    edges = {
        3: [edge(0, x_ref.at[last], 3)],
        0: [edge(0, x_ref.at[pl.ds(2 * rows - EDGE, EDGE)], 0)],
        2: [
            edge(0, x_ref.at[pl.ds(3 * rows - EDGE, EDGE)], 2),
            edge(1, x_ref.at[pl.ds(3 * rows - EDGE, EDGE)], 1),
        ],
    }

    def each_edge(head, act):
        @pl.when(jnp.logical_and(h == head, has_next))
        def _():
            for copy in edges[head]:
                act(copy)

    each_edge(3, lambda copy: copy.start())
    for load in loads[1:14]:
        load.wait()

    rate = jnp.concatenate(
        [jnp.exp(jnp.full((1, 128), dlog_ref[i], F32)) for i in range(heads)], axis=1
    )

    def project(first, slots):
        size = len(slots) * rows
        at = [pl.ds(pl.multiple_of(slot * rows, 16), rows) for slot in slots]
        some = x_ref[first : first + size, :]
        both = jnp.dot(some, dg_ref[...], preferred_element_type=F32).astype(BF16)
        force = sigmoid(
            lax.dot_general(
                some, beta_ref[...], (((1,), (1,)), ((), ())), preferred_element_type=F32
            )
        )
        raw = jnp.dot(both[:, 0:128], up_ref[...], preferred_element_type=F32) + bias_ref[...]
        soft = jnp.maximum(raw, 0.0) + jnp.log1p(jnp.exp(-jnp.abs(raw)))
        log_decay = -rate * soft
        gate = sigmoid(jnp.dot(both[:, 128:256], gup_ref[...], preferred_element_type=F32))
        for n, where in enumerate(at):
            own = slice(n * rows, (n + 1) * rows)
            fade_ref[where, :] = log_decay[own]
            gate_ref[where, :] = gate[own]
            strength_ref[where, :] = force[own]

    def project_qkv(c, first, slots, tail):
        size = len(slots) * rows
        some = x_ref[first : first + size + tail, :]
        got = jnp.dot(some, w_ref[c], preferred_element_type=F32).astype(BF16).astype(F32)
        for n, slot in enumerate(slots):
            at = pl.ds(pl.multiple_of(HALO + slot * rows, 16), rows)
            proj_ref[c, at, :] = got[n * rows : (n + 1) * rows]
        if tail:
            proj_ref[c, HALO - EDGE : HALO, :] = got[size : size + EDGE]

    def decays(c):
        piece_of = fade_ref[pl.ds(pl.multiple_of(c * HALF, HALF), HALF), :]
        top = piece_of.astype(BF16)
        rest = (piece_of - top.astype(F32)).astype(BF16)
        e_ref[c] = jnp.exp(
            jnp.dot(
                span_ref[...], jnp.concatenate([top, rest], axis=0), preferred_element_type=F32
            )
        )

    project(0, (h,))
    for c in range(3):
        project_qkv(c, 0, (h,), 0)

    moves[0].wait_recv()
    moves[2].wait_send()
    moves[4].start()
    moves[1].wait_recv()
    moves[3].wait_send()
    moves[5].start()
    each_edge(2, lambda copy: copy.start())
    moves[2].wait_recv()
    each_edge(0, lambda copy: copy.start())
    moves[3].wait_recv()

    near = (left, right)
    project(rows, near)
    for c in range(3):
        project_qkv(c, rows, near, 0)
    far_square = lax.div(far, 2)
    decays(1 - far_square)
    moves[4].wait_recv()
    moves[5].wait_recv()

    @pl.when(s > 0)
    def _():
        edges[0][0].wait_recv()

    def convolve(c):
        target = (q_ref, k_ref, v_ref)[c]
        taps = conv_ref[c].astype(F32)
        mixed = proj_ref[c, pl.ds(HALO - 3, count), :] * taps[0:1]
        for i in range(1, 4):
            mixed = mixed + proj_ref[c, pl.ds(HALO - 3 + i, count), :] * taps[i : i + 1]
        mixed = (mixed * sigmoid(mixed)).astype(BF16).astype(F32)
        if c == 2:
            target[...] = mixed
            return
        for i in range(heads):
            lanes = slice(i * 128, (i + 1) * 128)
            u = mixed[:, lanes]
            scale = lax.rsqrt(jnp.sum(u * u, axis=1, keepdims=True) + 1e-06)
            if c == 0:
                scale = scale * (128**-0.5)
            target[:, lanes] = u * scale

    project(3 * rows, (far,))
    project_qkv(1, 3 * rows, (far,), HALO)
    decays(far_square)
    convolve(1)
    project_qkv(2, 3 * rows, (far,), HALO)
    convolve(2)
    beta = strength_ref[...]

    t = lax.broadcasted_iota(jnp.int32, (HALF, HALF), 0)
    j = lax.broadcasted_iota(jnp.int32, (HALF, HALF), 1)
    row = lax.broadcasted_iota(jnp.int32, (HALF, 128), 0)
    masks = [
        ((t ^ j) >= size) & ((t ^ j) < 2 * size) & (t > j) for size in LEVELS
    ]
    diagonal = t == j

    lanes_of = [slice(i * 128, (i + 1) * 128) for i in range(heads)]
    rows_of = [slice(c * HALF, (c + 1) * HALF) for c in range(2)]

    def to_owner(i):
        return pltpu.make_async_remote_copy(
            src_ref=z_ref.at[i],
            dst_ref=zin.at[p],
            send_sem=a_send.at[i],
            recv_sem=a_recv.at[p],
            device_id={"seq": base + 2 * i},
            device_id_type=MESH,
        )

    strength, written, inverse = {}, {}, {}

    def unit_of(i, c):
        return 2 * i + c

    def mix(i, c, n):
        kc = k_ref[rows_of[c], lanes_of[i]]
        if n == 0:
            strength[i, c] = jnp.broadcast_to(beta[rows_of[c], i : i + 1], (HALF, 128))
            written[i, c] = kc * strength[i, c]
        fade = e_ref[c, n * HALF : (n + 1) * HALF, lanes_of[i]]
        size = LEVELS[n]
        if size < 8:
            chosen = jnp.where((row & size) != 0, kc, written[i, c])
        else:
            chosen = jnp.concatenate(
                [
                    (kc if at & size else written[i, c])[at : at + size]
                    for at in range(0, HALF, size)
                ],
                axis=0,
            )
        kx = (chosen * fade).astype(BF16)
        faded_ref[unit_of(i, c), n] = kx
        mix_ref[unit_of(i, c), n] = jnp.where(masks[n], mm(kx, kx, ((1,), (1,))), 0.0).astype(BF16)

    def mixes(some):
        for i in some:
            for c in range(2):
                for n in range(len(LEVELS)):
                    mix(i, c, n)
                    yield

    def attends(some):
        for i in some:
            for c in range(2):
                kc, qc = k_ref[rows_of[c], lanes_of[i]], q_ref[rows_of[c], lanes_of[i]]
                own = jnp.sum(qc * kc, axis=1, keepdims=True) * strength[i, c]
                attend = jnp.where(diagonal, own, 0.0)
                for n in range(len(LEVELS)):
                    qx = qc * e_ref[c, n * HALF : (n + 1) * HALF, lanes_of[i]]
                    both = mm(qx, faded_ref[unit_of(i, c), n], ((1,), (1,)))
                    attend = jnp.where(masks[n], both, attend)
                attend_ref[unit_of(i, c)] = attend.astype(BF16)
                yield

    def doublings(some):
        units = [(i, c) for i in some for c in range(2)]
        for unit in units:
            inverse[unit] = jnp.where(diagonal, 1.0, 0.0) - mix_ref[unit_of(*unit), 0].astype(F32)
        for n in range(1, len(LEVELS)):
            own = {unit: inverse[unit].astype(BF16) for unit in units}
            left_part = {}
            for unit in units:
                left_part[unit] = mm(own[unit], mix_ref[unit_of(*unit), n]).astype(BF16)
            yield
            for unit in units:
                inverse[unit] = inverse[unit] - mm(left_part[unit], own[unit])
            yield
        for unit in units:
            inverse[unit] = inverse[unit].astype(BF16)

    parts = {}

    def maps_of(some):
        n = len(LEVELS)
        units = [(i, c) for i in some for c in range(2)]
        rise = {u: e_ref[u[1], n * HALF : (n + 1) * HALF, lanes_of[u[0]]] for u in units}
        fall = {u: e_ref[u[1], (n + 1) * HALF : (n + 2) * HALF, lanes_of[u[0]]] for u in units}
        whole = {u: rise[u][HALF - 1 : HALF] for u in units}
        k_rise = {u: k_ref[rows_of[u[1]], lanes_of[u[0]]] * rise[u] for u in units}
        k_fall = {
            u: written[u] * fall[u] for u in units
        }
        cross, first, second = {}, {}, {}
        for i in some:
            cross[i] = mm(k_rise[i, 1], k_fall[i, 0], ((1,), (1,))).astype(BF16)
        for i in some:
            first[i] = mm(
                inverse[i, 0],
                jnp.concatenate([v_ref[rows_of[0], lanes_of[i]], k_rise[i, 0]], axis=1),
            ).astype(BF16)
        yield
        late_part = {i: mm(cross[i], first[i]) for i in some}
        yield
        for i in some:
            start = jnp.concatenate(
                [v_ref[rows_of[1], lanes_of[i]], k_rise[i, 1] * whole[i, 0]], axis=1
            )
            second[i] = mm(inverse[i, 1], start - late_part[i]).astype(BF16)
        yield
        for i in some:
            stop = jnp.concatenate(
                [k_fall[i, 0] * whole[i, 1], k_fall[i, 1]], axis=0
            ).astype(BF16)
            maps = mm(jnp.concatenate([first[i], second[i]], axis=0), stop, ((0,), (0,)))
            move = jnp.where(diagonal, whole[i, 0] * whole[i, 1], 0.0) - maps[128:]
            z_ref[i, 0:128] = move.astype(BF16)
            z_ref[i, 128:256] = maps[:128].astype(BF16)
            parts[i] = (rise, whole, first, second, k_fall)

    def outputs_of(some):
        for i in some:
            rise, whole, first, second, k_fall = parts[i]
            lanes = lanes_of[i]
            q_rise = {
                (i, c): q_ref[rows_of[c], lanes] * rise[i, c] for c in range(2)
            }
            cross = mm(q_rise[i, 1], k_fall[i, 0], ((1,), (1,)))
            out = [
                mm(attend_ref[unit_of(i, 0)], first[i]),
                mm(cross, first[i]) + mm(attend_ref[unit_of(i, 1)], second[i]),
            ]
            for c in range(2):
                o_ref[rows_of[c], lanes] = out[c][:, :128]
            r_ref[rows_of[0], lanes] = (q_rise[i, 0] - out[0][:, 128:]).astype(BF16)
            r_ref[rows_of[1], lanes] = (
                q_rise[i, 1] * whole[i, 0] - out[1][:, 128:]
            ).astype(BF16)
            yield

    def send_maps(some):
        for i in some:

            @pl.when(p != 2 * i)
            def _():
                to_owner(i).start()

    def together(main, other, share):
        for _ in main:
            for _ in range(share):
                next(other, None)

    def finish(*works):
        for work in works:
            for _ in work:
                pass

    early, late_heads = range(0, heads, 2), range(1, heads, 2)
    finish(mixes(early))
    mixing, other = mixes(late_heads), doublings(late_heads)
    for step, _ in enumerate(doublings(early)):
        if step < 6:
            for _ in range(5):
                next(mixing, None)
        else:
            finish(mixing)
            next(other)
    together(maps_of(early), other, 1)
    send_maps(early)
    finish(other, maps_of(late_heads))
    send_maps(late_heads)
    project_qkv(0, 3 * rows, (far,), HALO)
    convolve(0)
    for some in (early, late_heads):
        finish(attends(some), outputs_of(some))

    def to_group(k, at):
        return pltpu.make_async_remote_copy(
            src_ref=total.at[at],
            dst_ref=zall.at[rank, at],
            send_sem=b_send.at[k],
            recv_sem=b_recv.at[rank],
            device_id={"seq": (group * GROUP + k) * PLANE + p},
            device_id_type=MESH,
        )

    def from_group(k, at):
        return pltpu.make_async_remote_copy(
            src_ref=total.at[at],
            dst_ref=zall.at[k, at],
            send_sem=b_send.at[k],
            recv_sem=b_recv.at[k],
            device_id={"seq": s},
            device_id_type=MESH,
        )

    def to_next(k):
        target = jnp.where(rank == 0, 2 * GROUP - 1, 2 * GROUP - 2 - k)
        return pltpu.make_async_remote_copy(
            src_ref=chain,
            dst_ref=held,
            send_sem=f_sem.at[k],
            recv_sem=f_sem.at[3],
            device_id={"seq": target * PLANE + p},
            device_id_type=MESH,
        )

    def feed(act):
        @pl.when(feeds)
        def _():
            act(to_next(0))

        @pl.when(jnp.logical_and(feeds, rank > 0))
        def _():
            for k in range(1, GROUP - 1):
                act(to_next(k))

    def prefix_to(q):
        return pltpu.make_async_remote_copy(
            src_ref=pre.at[q],
            dst_ref=lead.at[y],
            send_sem=g_send.at[q],
            recv_sem=g_recv.at[y],
            device_id={"seq": base + q},
            device_id_type=MESH,
        )

    def entry_to(q):
        return pltpu.make_async_remote_copy(
            src_ref=entry,
            dst_ref=state.at[y],
            send_sem=c_send.at[q],
            recv_sem=c_recv.at[y],
            device_id={"seq": base + q},
            device_id_type=MESH,
        )

    def landed(ref, sem, k):
        pltpu.make_async_remote_copy(
            src_ref=ref.at[k],
            dst_ref=ref.at[k],
            send_sem=sem.at[k],
            recv_sem=sem.at[k],
            device_id={"seq": s},
            device_id_type=MESH,
        ).wait_recv()

    everything, shift_only = pl.ds(0, 256), pl.ds(128, 128)
    half_plane = PLANE // 2

    def join(one, two):
        step = mm(one, two[:128])
        return jnp.concatenate(
            [step[:128].astype(BF16), (step[128:] + two[128:].astype(F32)).astype(BF16)], axis=0
        )

    def moved(state_in, both):
        return (mm(state_in, both[0:128]) + both[128:256].astype(F32)).astype(BF16)

    def group_copies(act):
        for k in (3, 0, 2, 1):
            @pl.when(jnp.logical_and(jnp.logical_and(group == 0, rank == 0), k > 0))
            def _():
                act(to_group(k, shift_only))

            wanted = k > rank
            if k == 0:
                wanted = jnp.logical_and(group == 0, rank > 0)
            else:
                wanted = jnp.logical_and(
                    wanted, jnp.logical_or(group == 1, rank > 0)
                )

            @pl.when(wanted)
            def _():
                act(to_group(k, everything))

    @pl.when(owner)
    def _():
        zin[p] = z_ref[y]
        for k in range(PLANE):

            @pl.when(p != k)
            def _():
                landed(zin, a_recv, k)

        one, two = zin[0], zin[half_plane]
        later = {}
        for k in range(1, half_plane):
            pre[k], later[half_plane + k] = one, two
            one, two = join(one, zin[k]), join(two, zin[half_plane + k])
        pre[half_plane] = one
        whole_map = join(one, two)
        total[...] = whole_map
        group_copies(lambda copy: copy.start())
        zall[rank] = whole_map
        for k in range(half_plane + 1, PLANE):
            pre[k] = join(one, later[k])
        for d in FAR_FIRST:
            q = lax.rem(p + d, PLANE)

            @pl.when(q > 0)
            def _():
                prefix_to(q).start()

        @pl.when(p > 0)
        def _():
            lead[y] = pre[p]

        @pl.when(group == 0)
        def _():
            chain[...] = jnp.zeros_like(chain)
            entry[...] = jnp.zeros_like(entry)
            for k in range(GROUP):
                needed = jnp.logical_or(feeds, k < rank)
                if k == 0:

                    @pl.when(rank > 0)
                    def _():
                        from_group(0, shift_only).wait_recv()

                else:

                    @pl.when(jnp.logical_and(needed, rank != k))
                    def _():
                        from_group(k, everything).wait_recv()

                @pl.when(rank == k)
                def _():
                    entry[...] = chain[...]

                @pl.when(needed)
                def _():
                    if k == 0:
                        chain[...] = zall[0, 128:256]
                    else:
                        chain[...] = moved(chain[...], zall[k])

            feed(lambda copy: copy.start())

        @pl.when(group == 1)
        def _():
            for k in range(GROUP - 1):

                @pl.when(k < rank)
                def _():
                    from_group(k, everything).wait_recv()
                    if k == 0:
                        link[...] = zall[0]
                    else:
                        link[...] = join(link[...], zall[k])

            to_next(0).wait_recv()

            @pl.when(rank == 0)
            def _():
                entry[...] = held[...]

            @pl.when(rank > 0)
            def _():
                entry[...] = moved(held[...], link[...])

        @pl.when(z > 0)
        def _():
            for d in ENTRIES:
                entry_to(lax.rem(p + d, PLANE)).start()

            state[y] = entry[...]

    @pl.when(z == 0)
    def _():
        state[...] = jnp.zeros_like(state)

    @pl.when(p > 0)
    def _():
        for i in range(heads):

            @pl.when(p != 2 * i)
            def _():
                landed(lead, g_recv, i)

        for i in range(heads):
            lanes = lanes_of[i]
            both = mm(r_ref[:, lanes], lead[i], ((1,), (1,)))
            o_ref[:, lanes] = o_ref[:, lanes] + both[:, 128:]
            r_ref[:, lanes] = both[:, :128].astype(BF16)

    after_own = lax.rem(y + 1, heads)
    passes_on = jnp.logical_and(core == 1, z > 0)
    passed = pltpu.make_async_remote_copy(
        src_ref=state.at[after_own],
        dst_ref=state.at[after_own],
        send_sem=c_send.at[0],
        recv_sem=c_recv.at[after_own],
        device_id={"seq": base + lax.rem(p + PLANE - 2, PLANE)},
        device_id_type=MESH,
    )
    for d in (0, 1, 3, 2):
        i = lax.rem(y + d, heads)

        @pl.when(jnp.logical_and(p != 2 * i, z > 0))
        def _():
            landed(state, c_recv, i)

        if d == 1:

            @pl.when(passes_on)
            def _():
                passed.start()

        lanes = pl.ds(pl.multiple_of(i * 128, 128), 128)
        attended = o_ref[:, lanes] + mm(r_ref[:, lanes], state[i], ((1,), (1,)))
        scale = lax.rsqrt(jnp.mean(attended * attended, axis=1, keepdims=True) + 1e-05)
        normed[:, lanes] = (attended * scale * gain_ref[...] * gate_ref[:, lanes]).astype(BF16)
    loads[14].wait()


    def partial(to, lanes=slice(None)):
        at = pl.ds(pl.multiple_of(to * rows, 16), rows)
        return jnp.dot(normed[at, :], ow_ref[:, lanes], preferred_element_type=F32)

    def pass_on(k, src, dst, target):
        return pltpu.make_async_remote_copy(
            src_ref=src,
            dst_ref=dst,
            send_sem=d_send.at[k],
            recv_sem=d_recv.at[k],
            device_id={"head": target},
            device_id_type=MESH,
        )

    top, low = pl.ds(0, half), pl.ds(half, half)
    columns = out_ref.shape[1]
    split = columns // 2 // 128 * 128
    far_right, far_left = [], []
    for n, (first_lane, end_lane) in enumerate([(0, split), (split, columns)]):
        part[0, :, first_lane:end_lane] = partial(far, slice(first_lane, end_lane)).astype(BF16)
        some = pl.ds(first_lane, end_lane - first_lane)
        far_right.append(
            pass_on(2 * n, part.at[0, top, some], inbox.at[0, top, some], right)
        )
        far_left.append(
            pass_on(2 * n + 1, part.at[0, low, some], inbox.at[0, low, some], left)
        )
        far_right[n].start()
        far_left[n].start()
    sums[0] = partial(right)
    part[1, low] = sums[0, low].astype(BF16)
    right_low = pass_on(4, part.at[1, low], inbox.at[1, low], right)
    right_low.start()
    sums[1] = partial(left)
    part[2, top] = sums[1, top].astype(BF16)
    left_top = pass_on(5, part.at[2, top], inbox.at[2, top], left)
    left_top.start()
    for copy in far_right:
        copy.wait_recv()
    part[1, top] = (sums[0, top] + inbox[0, top].astype(F32)).astype(BF16)
    right_top = pass_on(6, part.at[1, top], inbox.at[1, top], right)
    right_top.start()
    for copy in far_left:
        copy.wait_recv()
    part[2, low] = (sums[1, low] + inbox[0, low].astype(F32)).astype(BF16)
    left_low = pass_on(7, part.at[2, low], inbox.at[2, low], left)
    left_low.start()
    own = partial(h)
    right_low.wait_recv()
    left_top.wait_recv()
    right_top.wait_recv()
    left_low.wait_recv()
    out_ref[...] = (own + inbox[1].astype(F32) + inbox[2].astype(F32)).astype(BF16)

    for copy in (*far_right, *far_left, right_low, left_top, right_top, left_low):
        copy.wait_send()
    for n in (0, 1, 4, 5):
        moves[n].wait_send()

    for head in (0, 2, 3):
        each_edge(head, lambda copy: copy.wait_send())

    for i in range(heads):

        @pl.when(p != 2 * i)
        def _():
            to_owner(i).wait_send()

    @pl.when(owner)
    def _():
        group_copies(lambda copy: copy.wait_send())

        feed(lambda copy: copy.wait_send())

        for d in FAR_FIRST:
            q = lax.rem(p + d, PLANE)

            @pl.when(q > 0)
            def _():
                prefix_to(q).wait_send()

        @pl.when(z > 0)
        def _():
            for d in ENTRIES:
                entry_to(lax.rem(p + d, PLANE)).wait_send()

    @pl.when(passes_on)
    def _():
        passed.wait_send()


def layer(depth, x, w, down, gdown, beta, up, gup, conv, dlog, bias, span, gain, ow):
    vmem = pl.BlockSpec(memory_space=pltpu.VMEM)
    hbm = pl.BlockSpec(memory_space=pl.ANY)
    rows, model = x.shape
    count, width = 4 * rows, w.shape[2]
    heads = width // 128
    dma = pltpu.SemaphoreType.DMA
    return pl.pallas_call(
        functools.partial(kernel, depth),
        name="layer",
        out_shape=pltpu.VMEM((rows, model), BF16),
        in_specs=[hbm] * 13,
        out_specs=vmem,
        scratch_shapes=[
            pltpu.VMEM((count + HALO, model), BF16),
            pltpu.VMEM(w.shape, BF16),
            pltpu.VMEM((model, 256), BF16),
            pltpu.VMEM(beta.shape, BF16),
            pltpu.VMEM(up.shape, BF16),
            pltpu.VMEM(gup.shape, BF16),
            pltpu.VMEM(conv.shape, BF16),
            pltpu.SMEM(dlog.shape, F32),
            pltpu.VMEM(bias.shape, F32),
            pltpu.VMEM(span.shape, BF16),
            pltpu.VMEM(gain.shape, F32),
            pltpu.VMEM(ow.shape, BF16),
            pltpu.VMEM((3, HALO + count, width), F32),
            pltpu.VMEM((count, width), F32),
            pltpu.VMEM((count, heads), F32),
            pltpu.VMEM((count, width), F32),
            pltpu.VMEM((count, width), F32),
            pltpu.VMEM((count, width), F32),
            pltpu.VMEM((2, (len(LEVELS) + 2) * HALF, width), F32),
            pltpu.VMEM((count, width), F32),
            pltpu.VMEM((count, width), BF16),
            pltpu.VMEM((count, width), F32),
            pltpu.VMEM((heads, 256, 128), BF16),
            pltpu.VMEM((2 * heads, len(LEVELS), HALF, HALF), BF16),
            pltpu.VMEM((2 * heads, len(LEVELS), HALF, 128), BF16),
            pltpu.VMEM((2 * heads, HALF, HALF), BF16),
            pltpu.VMEM((PLANE, 256, 128), BF16),
            pltpu.VMEM((PLANE, 256, 128), BF16),
            pltpu.VMEM((256, 128), BF16),
            pltpu.VMEM((GROUP, 256, 128), BF16),
            pltpu.VMEM((128, 128), BF16),
            pltpu.VMEM((256, 128), BF16),
            pltpu.VMEM((128, 128), BF16),
            pltpu.VMEM((128, 128), BF16),
            pltpu.VMEM((heads, 256, 128), BF16),
            pltpu.VMEM((heads, 128, 128), BF16),
            pltpu.VMEM((count, width), BF16),
            pltpu.VMEM((3, rows, model), BF16),
            pltpu.VMEM((2, rows, model), F32),
            pltpu.VMEM((3, rows, model), BF16),
            dma((15,)), dma((6,)), dma((6,)), dma((3,)), dma((4,)), dma((PLANE,)), dma((heads,)),
            dma((heads,)), dma((PLANE,)), dma((GROUP,)), dma((GROUP,)),
            dma((PLANE,)), dma((heads,)), dma((8,)), dma((8,)),
        ],
        compiler_params=pltpu.CompilerParams(
            collective_id=0, has_side_effects=True, vmem_limit_bytes=56 << 20
        ),
    )(x, w, down, gdown, beta, up, gup, conv, dlog, bias, span, gain, ow)


def solution(mesh):
    seq_size = mesh.shape["seq"]
    span = span_matrix()

    def shards(
        hidden_in, qkv_weight, conv_weight, decay_log, dt_bias, decay_down, decay_up,
        beta_weight, gate_down, gate_up, norm_gain, out_weight,
    ):
        return layer(
            seq_size // PLANE,
            hidden_in,
            jnp.transpose(qkv_weight, (1, 0, 2)),
            decay_down,
            gate_down,
            beta_weight.T,
            decay_up,
            gate_up,
            conv_weight,
            decay_log,
            dt_bias.reshape(1, -1),
            jnp.asarray(span, BF16),
            norm_gain.reshape(1, -1),
            out_weight,
        )

    rows = P(("seq", "head"), None)
    return jax.shard_map(
        shards,
        mesh=mesh,
        in_specs=(
            rows, P(None, None, "head"), P(None, None, "head"), P("head"), P("head"), P(),
            P(None, "head"), P(None, "head"), P(), P(None, "head"), P(), P("head", None),
        ),
        out_specs=rows,
        check_vma=False,
    )
```
